32 devices in a mesh: dom: 8 (over z, core), grp: 4 (over y, x).
Axes of the slice: x: 2, y: 2, z: 4, core: 2. Of those that a mesh axis runs over, the one named last changes fastest.
Arguments:
- feats: bfloat16 [8192, 256], P(('dom', 'grp')), may hold values from -6 to 6
- w_self: bfloat16 [256, 256], replicated, may hold values from -0.375 to 0.375
- w_neigh: bfloat16 [256, 256], replicated, may hold values from -0.375 to 0.375
- local_tiles: bfloat16 [64, 3, 128, 128], P(('dom', 'grp')), may hold values from -0.15625 to 0.15625
- local_cols: int32 [64, 3], P(('dom', 'grp')), may hold values from 0 to 7, as said below
- cut_tiles: bfloat16 [64, 10, 128, 128], P(('dom', 'grp')), may hold values from -0.15625 to 0.15625
- cut_src: int32 [64, 10], P(('dom', 'grp')), may hold values from 0 to 7, as said below
- send_block: int32 [32, 8], P(('dom', 'grp')), may hold values from 0 to 1
- send_live: int32 [32, 8], P(('dom', 'grp')), may hold values from 0 to 1, as said below
- cotangent: bfloat16 [8192, 256], P(('dom', 'grp')), may hold values from -0.0625 to 0.0625
Outputs:
- layer_out: bfloat16 [8192, 256], P(('dom', 'grp'))
- grad_self: float32 [256, 256], replicated
- grad_neigh: float32 [256, 256], replicated
The draws below stay inside these ranges and needn't reach their ends.
Inputs may be any that keep to these rules, and one draw needn't show every extreme that they name: `local_cols`: the 3 column blocks of one row block are distinct. `cut_src`: 0 marks an empty slot; the share of filled slots differs from partition to partition. send_live[e, p] is 1 exactly when some row block of device p * 4 + g (g the position of e) has a cut slot with offset naming e's partition; it is 0 where p is e's own partition.
All inputs are finite; a program needn't handle non-finite values.
Results may differ from the reference program's by a relative error of at most 0.0056.
Values may be sent and summed in bfloat16 or wider, within the bound.
A program may use at most 64 MiB of HBM per device.

```python
import jax
import jax.numpy as jnp
from jax import lax

D = 256
BLOCK = 128
RB = 2
KC = 10
PBLOCKS = 8
K = 3
NODES = 8192
N_DOM = 8
N_GRP = 4


def draw_local_cols(key, part):
    keys = jax.random.split(key, NODES // BLOCK)

    def pick_row(one_key):
        return jax.random.permutation(one_key, PBLOCKS)[:K]
    return jax.vmap(pick_row)(keys).astype(jnp.int32)


def cut_plan(key):
    base = jax.random.fold_in(key, 7101)
    level_key = jax.random.fold_in(base, 1)
    top_key = jax.random.fold_in(base, 2)
    slot_key = jax.random.fold_in(base, 3)
    first_key = jax.random.fold_in(base, 4)
    second_key = jax.random.fold_in(base, 5)
    levels = jax.random.randint(level_key, (N_DOM,), 1, 5)
    top_part = jax.random.randint(top_key, (), 0, N_DOM)
    levels = jnp.where(jnp.arange(N_DOM, dtype=jnp.int32) == top_part, 4, levels).astype(jnp.int32)
    row_count = NODES // BLOCK
    row_part = (jnp.arange(row_count, dtype=jnp.int32) // (N_GRP * RB)).astype(jnp.int32)
    slot_roll = jax.random.randint(slot_key, (row_count, KC), 0, 4)
    filled = slot_roll < levels[row_part][:, None]
    first = jax.random.randint(first_key, (row_count, KC), 0, N_DOM - 1)
    second = jax.random.randint(second_key, (row_count, KC), 0, N_DOM - 1)
    offsets = jnp.minimum(first, second) + 1
    cut_offsets = jnp.where(filled, offsets, 0).astype(jnp.int32)
    grouped = cut_offsets.reshape(N_DOM, N_GRP, RB * KC)
    src_part = jnp.arange(N_DOM, dtype=jnp.int32)[:, None, None, None]
    dst_part = jnp.arange(N_DOM, dtype=jnp.int32)[None, None, :, None]
    wanted = (src_part - dst_part) % N_DOM
    reads = grouped.transpose(1, 0, 2)[None, :, :, :]
    hits = jnp.logical_and(reads == wanted, reads != 0)
    live = jnp.any(hits, axis=3).astype(jnp.int32)
    return (cut_offsets, live.reshape(N_DOM * N_GRP, N_DOM))


def draw_cut_src(key, part):
    return cut_plan(key)[0]


def draw_send_live(key, part):
    return cut_plan(key)[1]


def plant(entries, stream_key, smallest, high):
    longest = entries.shape.index(max(entries.shape))
    spots = []
    for shift in (0, 1):
        where = [jax.random.randint(jax.random.fold_in(stream_key, axis), (), 0, length) for axis, length in enumerate(entries.shape)]
        where[longest] = (where[longest] + shift) % entries.shape[longest]
        spots.append(tuple(where))
    return entries.at[spots[0]].set(smallest).at[spots[1]].set(high)


def steps_of(key, dims, pieces, least, top_value):
    gain, own = 1.0, jax.random.fold_in(key, 6)
    for dim, parts in pieces:
        draws = jnp.exp(jax.random.uniform(jax.random.fold_in(own, dim), (parts,), jnp.float32, least / len(pieces), top_value / len(pieces)))
        gain = gain * jnp.repeat(draws, dims[dim] // parts).reshape([-1 if axis == dim else 1 for axis in range(len(dims))])
    return gain


def gaussian(own_key, extent, spread, reach, cuts=(), held_as=jnp.bfloat16):
    array = spread * jax.random.normal(own_key, extent, jnp.float32)
    if cuts:
        array = array * steps_of(own_key, extent, cuts, -0.22, 0.18)
    return jnp.clip(array, -reach, reach).astype(held_as)


def setup_inputs(seed: int = 0) -> dict:
    splits = jax.random.split(jax.random.key(seed), 11)
    feats = gaussian(splits[0], (NODES, D), 1.0, 6.0, ((0, 32),))
    w_self = gaussian(splits[1], (D, D), D ** -0.5, 0.375)
    w_neigh = gaussian(splits[2], (D, D), D ** -0.5, 0.375)
    local_tiles = gaussian(splits[3], (NODES // BLOCK, K, BLOCK, BLOCK), (1.0 / (BLOCK * (K + KC)) ** 0.5), 0.15625, ((0, 32),))
    local_cols = draw_local_cols(jax.random.fold_in(splits[10], 71), 0)
    cut_tiles = gaussian(splits[5], (NODES // BLOCK, KC, BLOCK, BLOCK), (1.0 / (BLOCK * (K + KC)) ** 0.5), 0.15625, ((0, 32),))
    cut_src = draw_cut_src(jax.random.fold_in(splits[10], 71), 0)
    send_block = plant(jax.random.randint(splits[7], (N_DOM * N_GRP, N_DOM), 0, RB), jax.random.fold_in(splits[7], 1), 0, RB - 1).astype(jnp.int32)
    send_live = draw_send_live(jax.random.fold_in(splits[10], 71), 0)
    cotangent = gaussian(splits[9], (NODES, D), (1.0 / NODES ** 0.5), 0.0625, ((0, 32),))
    return {"feats": feats, "w_self": w_self, "w_neigh": w_neigh, "local_tiles": local_tiles, "local_cols": local_cols, "cut_tiles": cut_tiles, "cut_src": cut_src, "send_block": send_block, "send_live": send_live, "cotangent": cotangent}


def reference(feats, w_self, w_neigh, local_tiles, local_cols, cut_tiles, cut_src, send_block, send_live, cotangent):
    feature_blocks = feats.reshape(N_DOM * N_GRP * RB, BLOCK, D)

    def aggregate_device(device):
        part_id = device // N_GRP
        group_id = device % N_GRP
        tiles_here = lax.dynamic_slice_in_dim(local_tiles, device * RB, RB, 0)
        cols_here = lax.dynamic_slice_in_dim(local_cols, device * RB, RB, 0)
        global_ids = (part_id * PBLOCKS + cols_here).astype(jnp.int32)
        chosen = feature_blocks[global_ids].astype(jnp.float32)
        total = jnp.einsum("rkij,rkjf->rif", tiles_here.astype(jnp.float32), chosen)
        cut_here = lax.dynamic_slice_in_dim(cut_tiles, device * RB, RB, 0)
        offsets = lax.dynamic_slice_in_dim(cut_src, device * RB, RB, 0)
        source = (part_id + offsets) % N_DOM
        source_dev = (source * N_GRP + group_id).astype(jnp.int32)
        sent_block = send_block[source_dev, part_id]
        alive = send_live[source_dev, part_id].astype(jnp.float32)
        remote = feature_blocks[(source_dev * RB + sent_block).astype(jnp.int32)].astype(jnp.float32)
        remote = remote * alive[:, :, None, None]
        total = total + jnp.einsum("rkij,rkjf->rif", cut_here.astype(jnp.float32), remote)
        return total.reshape(RB * BLOCK, D)

    devices = jnp.arange(N_DOM * N_GRP, dtype=jnp.int32)
    agg = lax.map(aggregate_device, devices).reshape(NODES, D).astype(jnp.bfloat16)
    preact = jnp.dot(feats, w_self, preferred_element_type=jnp.float32) + jnp.dot(agg, w_neigh, preferred_element_type=jnp.float32)
    sigmoid = jax.nn.sigmoid(preact)
    layer_out = (preact * sigmoid).astype(jnp.bfloat16)
    grad_pre = (cotangent.astype(jnp.float32) * sigmoid * (1.0 + preact * (1.0 - sigmoid))).astype(jnp.bfloat16)
    grad_self = jnp.dot(feats.T, grad_pre, preferred_element_type=jnp.float32)
    grad_neigh = jnp.dot(agg.T, grad_pre, preferred_element_type=jnp.float32)
    return layer_out, grad_self, grad_neigh
```

```python
import functools

import jax
import jax.numpy as jnp
from jax import lax
from jax.experimental import pallas as pl
from jax.experimental.pallas import tpu as pltpu
from jax.sharding import PartitionSpec as P

MESH = pl.DeviceIdType.MESH
PACK = 16
FEW = 4
CORES = 2
ORDERS = (("grp", "dom"), ("dom", "grp"))


def piece_rows(rows, n):
    return rows // n if n > FEW and rows % (PACK * n) == 0 else rows


def f32_dot(a, b):
    return jnp.dot(a, b, preferred_element_type=jnp.float32)


def kernel_wide(
    n_dom,
    n_grp,
    cols_hbm,
    src_hbm,
    block_hbm,
    live_hbm,
    feats_hbm,
    w_self_hbm,
    w_neigh_hbm,
    local_hbm,
    cut_hbm,
    cot_hbm,
    out_ref,
    grad_ref,
    cols_ref,
    src_ref,
    block_ref,
    live_ref,
    w_self_ref,
    w_neigh_ref,
    local_ref,
    cut_ref,
    cot_ref,
    feats_ref,
    near,
    outgoing,
    far,
    acc,
    pre,
    part,
    part_low,
    sums1_a,
    sums1_b,
    mid_a,
    mid_b,
    low_a,
    low_b,
    sums2_a,
    sums2_b,
    load_sem,
    near_send,
    near_recv,
    far_send,
    far_recv,
    s1_send,
    s1_recv,
    s2_send,
    s2_recv,
    s3_send,
    s3_recv,
    s4_send,
    s4_recv,
):
    sums1, mid, mid_low = (sums1_a, sums1_b), (mid_a, mid_b), (low_a, low_b)
    sums2 = (sums2_a, sums2_b)
    row_blocks, local_slots, block, _ = local_ref.shape
    cut_slots = cut_ref.shape[1]
    features = w_self_ref.shape[0]
    width = part.shape[2]
    me_d, me_g = lax.axis_index("dom"), lax.axis_index("grp")
    dom_peer = [lax.rem(me_d + o, n_dom) for o in range(n_dom)]
    grp_peer = [lax.rem(me_g + o, n_grp) for o in range(n_grp)]

    def remote(src, dst, send, recv, o, axis):
        peer = dom_peer[o] if axis == "dom" else grp_peer[o]
        return pltpu.make_async_remote_copy(
            src_ref=src,
            dst_ref=dst,
            send_sem=send,
            recv_sem=recv,
            device_id={axis: peer},
            device_id_type=MESH,
        )

    def begin(copies):
        for copy in copies:
            copy.start()
        return copies

    barrier = pltpu.get_barrier_semaphore()
    for o in range(1, n_dom):
        pl.semaphore_signal(barrier, inc=1, device_id={"dom": dom_peer[o]}, device_id_type=MESH)
    for o in range(1, n_grp):
        pl.semaphore_signal(barrier, inc=1, device_id={"grp": grp_peer[o]}, device_id_type=MESH)
    loads = begin(
        [
            pltpu.make_async_copy(src, dst, load_sem.at[i])
            for i, (src, dst) in enumerate(
                (
                    (block_hbm, block_ref),
                    (live_hbm, live_ref),
                    (feats_hbm, feats_ref),
                    (feats_hbm, near.at[pl.ds(0, row_blocks)]),
                    (cols_hbm, cols_ref),
                    (src_hbm, src_ref),
                    (w_self_hbm, w_self_ref),
                    (local_hbm, local_ref),
                    (cut_hbm, cut_ref),
                    (w_neigh_hbm, w_neigh_ref),
                    (cot_hbm, cot_ref),
                )
            )
        ]
    )
    for load in loads[:3]:
        load.wait()

    for o in range(n_dom):
        alive = live_ref[0, dom_peer[o]].astype(jnp.float32)
        chosen = feats_ref[block_ref[0, dom_peer[o]]].astype(jnp.float32)
        target = far if o == 0 else outgoing
        target[o] = (chosen * alive).astype(jnp.bfloat16)
    pl.semaphore_wait(barrier, n_dom + n_grp - 2)

    far_copies = begin(
        [
            remote(outgoing.at[o], far.at[o], far_send.at[o], far_recv.at[o], o, "dom")
            for o in sorted(range(1, n_dom), key=lambda o: abs(2 * o - n_dom))
        ]
    )
    near_copies = begin(
        [
            remote(
                feats_ref,
                near.at[pl.ds(o * row_blocks, row_blocks)],
                near_send.at[o],
                near_recv.at[o],
                o,
                "grp",
            )
            for o in range(1, n_grp)
        ]
    )

    for load in loads[3:]:
        load.wait()
    for b in range(row_blocks):
        pre[b] = f32_dot(feats_ref[b], w_self_ref[...])
    for copy in near_copies:
        copy.wait_recv()
    for b in range(row_blocks):
        total = jnp.zeros((block, features), jnp.float32)
        for k in range(local_slots):
            col = cols_ref[b, k]
            owner = lax.div(col, row_blocks)
            slot = lax.rem(me_g - owner + n_grp, n_grp)
            where = slot * row_blocks + lax.rem(col, row_blocks)
            total = total + f32_dot(local_ref[b, k], near[where])
        acc[b] = total

    for copy in far_copies:
        copy.wait_recv()
    grads_own = jnp.zeros((features, features), jnp.float32)
    grads_agg = jnp.zeros((features, features), jnp.float32)
    for b in range(row_blocks):
        total = acc[b]
        for k in range(cut_slots):
            slot = lax.rem(n_dom - src_ref[b, k], n_dom)
            total = total + f32_dot(cut_ref[b, k], far[slot])
        agg = total.astype(jnp.bfloat16)
        own = feats_ref[b]
        preact = pre[b] + f32_dot(agg, w_neigh_ref[...])
        sig = jax.nn.sigmoid(preact)
        out_ref[b] = (preact * sig).astype(jnp.bfloat16)
        grad_pre = (
            cot_ref[b].astype(jnp.float32) * sig * (1.0 + preact * (1.0 - sig))
        ).astype(jnp.bfloat16)
        dims = (((0,), (0,)), ((), ()))
        grads_own = grads_own + lax.dot_general(
            own, grad_pre, dims, preferred_element_type=jnp.float32
        )
        grads_agg = grads_agg + lax.dot_general(
            agg, grad_pre, dims, preferred_element_type=jnp.float32
        )

    peers = {"grp": grp_peer, "dom": dom_peer}
    here = {"grp": me_g, "dom": me_d}
    count = {"grp": n_grp, "dom": n_dom}

    def rows_at(start, size):
        return pl.ds(pl.multiple_of(start, size), size)

    def to_peers(axis, src, dst, send, recv):
        return begin(
            [
                remote(src(o), dst(o), send.at[o], recv.at[o], o, axis)
                for o in range(1, count[axis])
            ]
        )

    flows = []
    for h, (one, two) in enumerate(ORDERS):
        rows = 2 * features // count[one]
        piece = piece_rows(rows, count[two])
        split = piece < rows
        flows.append(
            dict(
                one=one,
                two=two,
                rows=rows,
                piece=piece,
                split=split,
                columns=pl.ds(h * width, width),
                mine=rows_at(here[one] * rows, rows),
                inner=rows_at(here[two] * piece, piece) if split else pl.ds(0, rows),
                spot=rows_at(here[one] * rows + (here[two] * piece if split else 0), piece),
                sums1=sums1[h],
                mid=mid[h],
                mid_low=mid_low[h],
                sums2=sums2[h],
            )
        )

    first = []
    for h, f in enumerate(flows):
        cut = slice(h * width, (h + 1) * width)
        part[h, 0:features] = grads_own[:, cut]
        part[h, features : 2 * features] = grads_agg[:, cut]
        part_low[h, 0:features] = grads_own[:, cut].astype(jnp.bfloat16)
        part_low[h, features : 2 * features] = grads_agg[:, cut].astype(jnp.bfloat16)
        first.append(
            to_peers(
                f["one"],
                lambda o: part_low.at[h, rows_at(peers[f["one"]][o] * f["rows"], f["rows"])],
                lambda o: f["sums1"].at[o],
                s1_send.at[h],
                s1_recv.at[h],
            )
        )
    second = []
    for h, f in enumerate(flows):
        total = part[h, f["mine"]]
        for o, copy in enumerate(first[h], 1):
            copy.wait_recv()
            total = total + f["sums1"][o].astype(jnp.float32)
        f["mid"][...] = total
        f["mid_low"][...] = total.astype(jnp.bfloat16)
        second.append(
            to_peers(
                f["two"],
                lambda o: f["mid_low"].at[rows_at(peers[f["two"]][o] * f["piece"], f["piece"])]
                if f["split"]
                else f["mid_low"],
                lambda o: f["sums2"].at[o if f["split"] else here[f["two"]]],
                s2_send.at[h],
                s2_recv.at[h],
            )
        )
    third, fourth = [], []

    def gather(h, f):
        rows_of = grad_ref.at[f["mine"], f["columns"]]
        return to_peers(
            f["one"], lambda o: rows_of, lambda o: rows_of, s4_send.at[h], s4_recv.at[h]
        )

    for h, f in enumerate(flows):
        if f["split"]:
            total = f["mid"][f["inner"]]
            for o, copy in enumerate(second[h], 1):
                copy.wait_recv()
                total = total + f["sums2"][o].astype(jnp.float32)
        else:
            f["sums2"][here[f["two"]]] = f["mid_low"][...]
            for copy in second[h]:
                copy.wait_recv()
            total = f["sums2"][0].astype(jnp.float32)
            for o in range(1, count[f["two"]]):
                total = total + f["sums2"][o].astype(jnp.float32)
        grad_ref[f["spot"], f["columns"]] = total.astype(jnp.bfloat16)
        if f["split"]:
            block_of = grad_ref.at[f["spot"], f["columns"]]
            third.append(
                to_peers(
                    f["two"],
                    lambda o: block_of,
                    lambda o: block_of,
                    s3_send.at[h],
                    s3_recv.at[h],
                )
            )
        else:
            third.append([])
            fourth += gather(h, f)
    for h, f in enumerate(flows):
        if f["split"]:
            for copy in third[h]:
                copy.wait_recv()
            fourth += gather(h, f)
    for copy in fourth:
        copy.wait_recv()

    sent = [far_copies, near_copies, *first, *second, *third, fourth]
    for copy in [copy for group in sent for copy in group]:
        copy.wait_send()


def kernel_near(
    n_dom,
    n_grp,
    cols_hbm,
    src_hbm,
    block_hbm,
    live_hbm,
    feats_hbm,
    w_self_hbm,
    w_neigh_hbm,
    local_hbm,
    cut_hbm,
    cot_hbm,
    out_ref,
    cols_ref,
    src_ref,
    block_ref,
    live_ref,
    w_self_ref,
    w_neigh_ref,
    local_ref,
    cut_ref,
    cot_ref,
    lhs,
    pre,
    grad_pre_ref,
    near,
    outgoing,
    far,
    core_out,
    core_in,
    mine,
    mine_low,
    pieces,
    load_sem,
    near_send,
    near_recv,
    far_send,
    far_recv,
    core_send,
    core_recv,
    rs_send,
    rs_recv,
    ag_send,
    ag_recv,
    fw_send,
    fw_recv,
):
    row_blocks, local_slots, block, _ = local_ref.shape
    cut_slots = cut_ref.shape[1]
    features = w_self_ref.shape[0]
    rows = row_blocks * block
    n_z = n_dom // CORES
    piece = pieces.shape[1]
    me_d, me_g = lax.axis_index("dom"), lax.axis_index("grp")
    me_z, me_c = lax.div(me_d, CORES), lax.rem(me_d, CORES)
    core_peer = (me_d + 1 - 2 * me_c, me_g)
    dom_peer = [lax.rem(me_d + o, n_dom) for o in range(n_dom)]
    grp_peer = [lax.rem(me_g + o, n_grp) for o in range(n_grp)]
    steps = [(dz, dg) for dz in range(n_z) for dg in range(n_grp) if dz or dg]

    def flat(x):
        return x.reshape(rows, features)

    def chip_at(dz, dg):
        return lax.rem(me_z + dz, n_z), lax.rem(me_g + dg, n_grp)

    def remote(src, dst, send, recv, device):
        return pltpu.make_async_remote_copy(
            src_ref=src,
            dst_ref=dst,
            send_sem=send,
            recv_sem=recv,
            device_id=device,
            device_id_type=MESH,
        )

    def begin(copies):
        for copy in copies:
            copy.start()
        return copies

    def greet(device):
        pl.semaphore_signal(barrier, inc=1, device_id=device, device_id_type=MESH)

    barrier = pltpu.get_barrier_semaphore()
    greeted = [(dom_peer[o], me_g) for o in range(1, n_dom)]
    greeted += [(me_d, grp_peer[o]) for o in range(1, n_grp)]
    for dz, dg in steps:
        if dz and dg:
            z, g = chip_at(dz, dg)
            greeted.append((z * CORES + me_c, g))
    for device in greeted:
        greet(device)
    feats_ref = lhs.at[0]
    loads = begin(
        [
            pltpu.make_async_copy(src, dst, load_sem.at[i])
            for i, (src, dst) in enumerate(
                (
                    (block_hbm, block_ref),
                    (live_hbm, live_ref),
                    (feats_hbm, lhs.at[0]),
                    (feats_hbm, near.at[pl.ds(0, row_blocks)]),
                    (cols_hbm, cols_ref),
                    (src_hbm, src_ref),
                    (w_self_hbm, w_self_ref),
                    (local_hbm, local_ref),
                    (cut_hbm, cut_ref),
                    (w_neigh_hbm, w_neigh_ref),
                    (cot_hbm, cot_ref),
                )
            )
        ]
    )
    for load in loads[:4]:
        load.wait()

    for o in range(n_dom):
        alive = live_ref[0, dom_peer[o]].astype(jnp.float32)
        chosen = lhs[0, block_ref[0, dom_peer[o]]].astype(jnp.float32)
        target = far if o == 0 else outgoing
        target[o] = (chosen * alive).astype(jnp.bfloat16)
    pl.semaphore_wait(barrier, len(greeted))

    far_copies = begin(
        [
            remote(
                outgoing.at[o],
                far.at[o],
                far_send.at[o],
                far_recv.at[o],
                (dom_peer[o], me_g),
            )
            for o in sorted(range(1, n_dom), key=lambda o: abs(2 * o - n_dom))
        ]
    )
    near_copies = begin(
        [
            remote(
                feats_ref,
                near.at[pl.ds(o * row_blocks, row_blocks)],
                near_send.at[o],
                near_recv.at[o],
                (me_d, grp_peer[o]),
            )
            for o in range(1, n_grp)
        ]
    )

    for load in loads[4:]:
        load.wait()
    pre[...] = f32_dot(flat(feats_ref[...]), w_self_ref[...])
    for copy in near_copies:
        copy.wait_recv()
    acc = []
    for b in range(row_blocks):
        total = jnp.zeros((block, features), jnp.float32)
        for k in range(local_slots):
            col = cols_ref[b, k]
            owner = lax.div(col, row_blocks)
            slot = lax.rem(me_g - owner + n_grp, n_grp)
            where = slot * row_blocks + lax.rem(col, row_blocks)
            total = total + f32_dot(local_ref[b, k], near[where])
        acc.append(total)

    for copy in far_copies:
        copy.wait_recv()
    for b in range(row_blocks):
        here = pl.ds(b * block, block)
        total = acc[b]
        for k in range(cut_slots):
            slot = lax.rem(n_dom - src_ref[b, k], n_dom)
            total = total + f32_dot(cut_ref[b, k], far[slot])
        agg = total.astype(jnp.bfloat16)
        lhs[1, b] = agg
        preact = pre[here] + f32_dot(agg, w_neigh_ref[...])
        sig = jax.nn.sigmoid(preact)
        out_ref[here] = (preact * sig).astype(jnp.bfloat16)
        grad_pre_ref[here] = (
            cot_ref[here].astype(jnp.float32) * sig * (1.0 + preact * (1.0 - sig))
        ).astype(jnp.bfloat16)

    def product(side):
        return lax.dot_general(
            flat(lhs[side]),
            grad_pre_ref[...],
            (((0,), (0,)), ((), ())),
            preferred_element_type=jnp.float32,
        )

    core_out[...] = product(1 - me_c).astype(jnp.bfloat16)
    core_copy = remote(core_out, core_in, core_send, core_recv, core_peer)
    core_copy.start()
    mine[...] = product(me_c)
    core_copy.wait_recv()
    total = mine[...] + core_in[...].astype(jnp.float32)
    mine[...] = total
    mine_low[...] = total.astype(jnp.bfloat16)

    def rows_of(z, g):
        return pl.ds(pl.multiple_of((z * n_grp + g) * piece, piece), piece)

    first = []
    for i, (dz, dg) in enumerate(steps):
        z, g = chip_at(dz, dg)
        first.append(
            remote(
                mine_low.at[rows_of(z, g)],
                pieces.at[i],
                rs_send.at[i],
                rs_recv.at[i],
                (z * CORES + me_c, g),
            )
        )
    begin(sorted_far(first, steps, n_z))
    total = mine[rows_of(me_z, me_g)]
    for i, copy in enumerate(first):
        copy.wait_recv()
        total = total + pieces[i].astype(jnp.float32)

    def spot(z, g):
        start = rows + me_c * features + (z * n_grp + g) * piece
        return out_ref.at[pl.ds(pl.multiple_of(start, piece), piece)]

    own = spot(me_z, me_g)
    own[...] = total.astype(jnp.bfloat16)
    second = []
    for i, (dz, dg) in enumerate(steps):
        z, g = chip_at(dz, dg)
        second.append(remote(own, own, ag_send.at[i], ag_recv.at[i], (z * CORES + me_c, g)))
    begin(sorted_far(second, steps, n_z))
    forward = begin([remote(own, own, fw_send.at[0], fw_recv.at[0], core_peer)])
    for i, (dz, dg) in enumerate(steps):
        second[i].wait_recv()
        part = spot(lax.rem(me_z - dz + n_z, n_z), lax.rem(me_g - dg + n_grp, n_grp))
        forward += begin([remote(part, part, fw_send.at[i + 1], fw_recv.at[i + 1], core_peer)])
    for copy in forward:
        copy.wait_recv()

    for copy in [*far_copies, *near_copies, core_copy, *first, *second, *forward]:
        copy.wait_send()


def sorted_far(copies, steps, n_z):
    order = sorted(range(len(steps)), key=lambda i: -min(steps[i][0], n_z - steps[i][0]))
    return [copies[i] for i in order]


def body_wide(
    feats,
    w_self,
    w_neigh,
    local_tiles,
    local_cols,
    cut_tiles,
    cut_src,
    send_block,
    send_live,
    cotangent,
):
    row_blocks, _, block, _ = local_tiles.shape
    features = feats.shape[1]
    n_dom, n_grp = lax.axis_size("dom"), lax.axis_size("grp")
    blocks = (row_blocks, block, features)
    halves = len(ORDERS)
    count = {"grp": n_grp, "dom": n_dom}
    most = max(n_grp, n_dom)
    sizes = []
    for one, two in ORDERS:
        rows = 2 * features // count[one]
        sizes.append((count[one], rows, count[two], piece_rows(rows, count[two])))
    width = features // halves
    dma = pltpu.SemaphoreType.DMA
    hbm = pl.BlockSpec(memory_space=pltpu.HBM)
    vmem = pl.BlockSpec(memory_space=pltpu.VMEM)
    out, grads = pl.pallas_call(
        functools.partial(kernel_wide, n_dom, n_grp),
        out_shape=(
            jax.ShapeDtypeStruct(blocks, jnp.bfloat16),
            jax.ShapeDtypeStruct((2 * features, features), jnp.bfloat16),
        ),
        in_specs=[hbm] * 10,
        out_specs=(vmem, vmem),
        scratch_shapes=[
            pltpu.SMEM(local_cols.shape, jnp.int32),
            pltpu.SMEM(cut_src.shape, jnp.int32),
            pltpu.SMEM(send_block.shape, jnp.int32),
            pltpu.SMEM(send_live.shape, jnp.int32),
            pltpu.VMEM(w_self.shape, jnp.bfloat16),
            pltpu.VMEM(w_neigh.shape, jnp.bfloat16),
            pltpu.VMEM(local_tiles.shape, jnp.bfloat16),
            pltpu.VMEM(cut_tiles.shape, jnp.bfloat16),
            pltpu.VMEM(blocks, jnp.bfloat16),
            pltpu.VMEM(blocks, jnp.bfloat16),
            pltpu.VMEM((n_grp * row_blocks, block, features), jnp.bfloat16),
            pltpu.VMEM((n_dom, block, features), jnp.bfloat16),
            pltpu.VMEM((n_dom, block, features), jnp.bfloat16),
            pltpu.VMEM(blocks, jnp.float32),
            pltpu.VMEM(blocks, jnp.float32),
            pltpu.VMEM((halves, 2 * features, width), jnp.float32),
            pltpu.VMEM((halves, 2 * features, width), jnp.bfloat16),
        ]
        + [pltpu.VMEM((n, r, width), jnp.bfloat16) for n, r, _, _ in sizes]
        + [pltpu.VMEM((r, width), jnp.float32) for _, r, _, _ in sizes]
        + [pltpu.VMEM((r, width), jnp.bfloat16) for _, r, _, _ in sizes]
        + [pltpu.VMEM((n, p, width), jnp.bfloat16) for _, _, n, p in sizes]
        + [
            dma((11,)),
        ]
        + [dma((n_grp,))] * 2
        + [dma((n_dom,))] * 2
        + [dma((halves, most))] * 8,
        compiler_params=pltpu.CompilerParams(
            collective_id=0, has_side_effects=True, vmem_limit_bytes=32 * 2**20
        ),
    )(
        *(
            pltpu.with_memory_space_constraint(x, pltpu.HBM)
            for x in (
                local_cols,
                cut_src,
                send_block,
                send_live,
                feats.reshape(blocks),
                w_self,
                w_neigh,
                local_tiles,
                cut_tiles,
                cotangent.reshape(blocks),
            )
        )
    )
    summed = grads.astype(jnp.float32)
    return (out.reshape(feats.shape), summed[:features], summed[features:])


def body_near(
    feats,
    w_self,
    w_neigh,
    local_tiles,
    local_cols,
    cut_tiles,
    cut_src,
    send_block,
    send_live,
    cotangent,
):
    row_blocks, _, block, _ = local_tiles.shape
    rows, features = feats.shape
    blocks = (row_blocks, block, features)
    n_dom, n_grp = lax.axis_size("dom"), lax.axis_size("grp")
    chips = n_dom // CORES * n_grp
    piece = features // chips
    dma = pltpu.SemaphoreType.DMA
    hbm = pl.BlockSpec(memory_space=pltpu.HBM)
    vmem = pl.BlockSpec(memory_space=pltpu.VMEM)
    low = functools.partial(pltpu.VMEM, dtype=jnp.bfloat16)
    wide = functools.partial(pltpu.VMEM, dtype=jnp.float32)
    res = pl.pallas_call(
        functools.partial(kernel_near, n_dom, n_grp),
        out_shape=jax.ShapeDtypeStruct((rows + 2 * features, features), jnp.bfloat16),
        in_specs=[hbm] * 10,
        out_specs=vmem,
        scratch_shapes=[
            pltpu.SMEM(local_cols.shape, jnp.int32),
            pltpu.SMEM(cut_src.shape, jnp.int32),
            pltpu.SMEM(send_block.shape, jnp.int32),
            pltpu.SMEM(send_live.shape, jnp.int32),
            low(w_self.shape),
            low(w_neigh.shape),
            low(local_tiles.shape),
            low(cut_tiles.shape),
            low(feats.shape),
            low((2, *blocks)),
            wide((rows, features)),
            low((rows, features)),
            low((n_grp * row_blocks, block, features)),
            low((n_dom, block, features)),
            low((n_dom, block, features)),
            low((features, features)),
            low((features, features)),
            wide((features, features)),
            low((features, features)),
            low((chips - 1, piece, features)),
            dma((11,)),
            dma((n_grp,)),
            dma((n_grp,)),
            dma((n_dom,)),
            dma((n_dom,)),
            dma,
            dma,
        ]
        + [dma((chips,))] * 6,
        compiler_params=pltpu.CompilerParams(
            collective_id=0, has_side_effects=True, vmem_limit_bytes=32 * 2**20
        ),
    )(
        *(
            pltpu.with_memory_space_constraint(x, pltpu.HBM)
            for x in (
                local_cols,
                cut_src,
                send_block,
                send_live,
                feats.reshape(blocks),
                w_self,
                w_neigh,
                local_tiles,
                cut_tiles,
                cotangent,
            )
        )
    )
    return (
        res[:rows],
        res[rows : rows + features].astype(jnp.float32),
        res[rows + features :].astype(jnp.float32),
    )


def solution(mesh):
    n_dom, n_grp = mesh.shape["dom"], mesh.shape["grp"]
    chips = n_dom // CORES * n_grp
    return jax.shard_map(
        lambda *args: (
            body_near if args[1].shape[0] % (PACK * chips) == 0 else body_wide
        )(*args),
        mesh=mesh,
        in_specs=(
            P(("dom", "grp"), None),
            P(),
            P(),
            P(("dom", "grp"), None, None, None),
            P(("dom", "grp"), None),
            P(("dom", "grp"), None, None, None),
            P(("dom", "grp"), None),
            P(("dom", "grp"), None),
            P(("dom", "grp"), None),
            P(("dom", "grp"), None),
        ),
        out_specs=(P(("dom", "grp"), None), P(), P()),
        check_vma=False,
    )
```

```python
import functools

import jax
import jax.numpy as jnp
from jax import lax
from jax.experimental import pallas as pl
from jax.experimental.pallas import tpu as pltpu
from jax.sharding import PartitionSpec as P

MESH = pl.DeviceIdType.MESH
PACK = 16
FEW = 4
CORES = 2
LINE = 4
ORDERS = (("grp", "dom"), ("dom", "grp"))


def piece_rows(rows, n):
    return rows // n if n > FEW and rows % (PACK * n) == 0 else rows


def f32_dot(a, b):
    return jnp.dot(a, b, preferred_element_type=jnp.float32)


def kernel_wide(
    n_dom,
    n_grp,
    cols_hbm,
    src_hbm,
    block_hbm,
    live_hbm,
    feats_hbm,
    w_self_hbm,
    w_neigh_hbm,
    local_hbm,
    cut_hbm,
    cot_hbm,
    out_ref,
    grad_ref,
    cols_ref,
    src_ref,
    block_ref,
    live_ref,
    w_self_ref,
    w_neigh_ref,
    local_ref,
    cut_ref,
    cot_ref,
    feats_ref,
    near,
    outgoing,
    far,
    acc,
    pre,
    part,
    part_low,
    sums1_a,
    sums1_b,
    mid_a,
    mid_b,
    low_a,
    low_b,
    sums2_a,
    sums2_b,
    load_sem,
    near_send,
    near_recv,
    far_send,
    far_recv,
    s1_send,
    s1_recv,
    s2_send,
    s2_recv,
    s3_send,
    s3_recv,
    s4_send,
    s4_recv,
):
    sums1, mid, mid_low = (sums1_a, sums1_b), (mid_a, mid_b), (low_a, low_b)
    sums2 = (sums2_a, sums2_b)
    row_blocks, local_slots, block, _ = local_ref.shape
    cut_slots = cut_ref.shape[1]
    features = w_self_ref.shape[0]
    width = part.shape[2]
    me_d, me_g = lax.axis_index("dom"), lax.axis_index("grp")
    dom_peer = [lax.rem(me_d + o, n_dom) for o in range(n_dom)]
    grp_peer = [lax.rem(me_g + o, n_grp) for o in range(n_grp)]

    def remote(src, dst, send, recv, o, axis):
        peer = dom_peer[o] if axis == "dom" else grp_peer[o]
        return pltpu.make_async_remote_copy(
            src_ref=src,
            dst_ref=dst,
            send_sem=send,
            recv_sem=recv,
            device_id={axis: peer},
            device_id_type=MESH,
        )

    def begin(copies):
        for copy in copies:
            copy.start()
        return copies

    barrier = pltpu.get_barrier_semaphore()
    for o in range(1, n_dom):
        pl.semaphore_signal(barrier, inc=1, device_id={"dom": dom_peer[o]}, device_id_type=MESH)
    for o in range(1, n_grp):
        pl.semaphore_signal(barrier, inc=1, device_id={"grp": grp_peer[o]}, device_id_type=MESH)
    loads = begin(
        [
            pltpu.make_async_copy(src, dst, load_sem.at[i])
            for i, (src, dst) in enumerate(
                (
                    (block_hbm, block_ref),
                    (live_hbm, live_ref),
                    (feats_hbm, feats_ref),
                    (feats_hbm, near.at[pl.ds(0, row_blocks)]),
                    (cols_hbm, cols_ref),
                    (src_hbm, src_ref),
                    (w_self_hbm, w_self_ref),
                    (local_hbm, local_ref),
                    (cut_hbm, cut_ref),
                    (w_neigh_hbm, w_neigh_ref),
                    (cot_hbm, cot_ref),
                )
            )
        ]
    )
    for load in loads[:3]:
        load.wait()

    for o in range(n_dom):
        alive = live_ref[0, dom_peer[o]].astype(jnp.float32)
        chosen = feats_ref[block_ref[0, dom_peer[o]]].astype(jnp.float32)
        target = far if o == 0 else outgoing
        target[o] = (chosen * alive).astype(jnp.bfloat16)
    pl.semaphore_wait(barrier, n_dom + n_grp - 2)

    far_copies = begin(
        [
            remote(outgoing.at[o], far.at[o], far_send.at[o], far_recv.at[o], o, "dom")
            for o in sorted(range(1, n_dom), key=lambda o: abs(2 * o - n_dom))
        ]
    )
    near_copies = begin(
        [
            remote(
                feats_ref,
                near.at[pl.ds(o * row_blocks, row_blocks)],
                near_send.at[o],
                near_recv.at[o],
                o,
                "grp",
            )
            for o in range(1, n_grp)
        ]
    )

    for load in loads[3:]:
        load.wait()
    for b in range(row_blocks):
        pre[b] = f32_dot(feats_ref[b], w_self_ref[...])
    for copy in near_copies:
        copy.wait_recv()
    for b in range(row_blocks):
        total = jnp.zeros((block, features), jnp.float32)
        for k in range(local_slots):
            col = cols_ref[b, k]
            owner = lax.div(col, row_blocks)
            slot = lax.rem(me_g - owner + n_grp, n_grp)
            where = slot * row_blocks + lax.rem(col, row_blocks)
            total = total + f32_dot(local_ref[b, k], near[where])
        acc[b] = total

    for copy in far_copies:
        copy.wait_recv()
    grads_own = jnp.zeros((features, features), jnp.float32)
    grads_agg = jnp.zeros((features, features), jnp.float32)
    for b in range(row_blocks):
        total = acc[b]
        for k in range(cut_slots):
            slot = lax.rem(n_dom - src_ref[b, k], n_dom)
            total = total + f32_dot(cut_ref[b, k], far[slot])
        agg = total.astype(jnp.bfloat16)
        own = feats_ref[b]
        preact = pre[b] + f32_dot(agg, w_neigh_ref[...])
        sig = jax.nn.sigmoid(preact)
        out_ref[b] = (preact * sig).astype(jnp.bfloat16)
        grad_pre = (
            cot_ref[b].astype(jnp.float32) * sig * (1.0 + preact * (1.0 - sig))
        ).astype(jnp.bfloat16)
        dims = (((0,), (0,)), ((), ()))
        grads_own = grads_own + lax.dot_general(
            own, grad_pre, dims, preferred_element_type=jnp.float32
        )
        grads_agg = grads_agg + lax.dot_general(
            agg, grad_pre, dims, preferred_element_type=jnp.float32
        )

    peers = {"grp": grp_peer, "dom": dom_peer}
    here = {"grp": me_g, "dom": me_d}
    count = {"grp": n_grp, "dom": n_dom}

    def rows_at(start, size):
        return pl.ds(pl.multiple_of(start, size), size)

    def to_peers(axis, src, dst, send, recv):
        return begin(
            [
                remote(src(o), dst(o), send.at[o], recv.at[o], o, axis)
                for o in range(1, count[axis])
            ]
        )

    flows = []
    for h, (one, two) in enumerate(ORDERS):
        rows = 2 * features // count[one]
        piece = piece_rows(rows, count[two])
        split = piece < rows
        flows.append(
            dict(
                one=one,
                two=two,
                rows=rows,
                piece=piece,
                split=split,
                columns=pl.ds(h * width, width),
                mine=rows_at(here[one] * rows, rows),
                inner=rows_at(here[two] * piece, piece) if split else pl.ds(0, rows),
                spot=rows_at(here[one] * rows + (here[two] * piece if split else 0), piece),
                sums1=sums1[h],
                mid=mid[h],
                mid_low=mid_low[h],
                sums2=sums2[h],
            )
        )

    first = []
    for h, f in enumerate(flows):
        cut = slice(h * width, (h + 1) * width)
        part[h, 0:features] = grads_own[:, cut]
        part[h, features : 2 * features] = grads_agg[:, cut]
        part_low[h, 0:features] = grads_own[:, cut].astype(jnp.bfloat16)
        part_low[h, features : 2 * features] = grads_agg[:, cut].astype(jnp.bfloat16)
        first.append(
            to_peers(
                f["one"],
                lambda o: part_low.at[h, rows_at(peers[f["one"]][o] * f["rows"], f["rows"])],
                lambda o: f["sums1"].at[o],
                s1_send.at[h],
                s1_recv.at[h],
            )
        )
    second = []
    for h, f in enumerate(flows):
        total = part[h, f["mine"]]
        for o, copy in enumerate(first[h], 1):
            copy.wait_recv()
            total = total + f["sums1"][o].astype(jnp.float32)
        f["mid"][...] = total
        f["mid_low"][...] = total.astype(jnp.bfloat16)
        second.append(
            to_peers(
                f["two"],
                lambda o: f["mid_low"].at[rows_at(peers[f["two"]][o] * f["piece"], f["piece"])]
                if f["split"]
                else f["mid_low"],
                lambda o: f["sums2"].at[o if f["split"] else here[f["two"]]],
                s2_send.at[h],
                s2_recv.at[h],
            )
        )
    third, fourth = [], []

    def gather(h, f):
        rows_of = grad_ref.at[f["mine"], f["columns"]]
        return to_peers(
            f["one"], lambda o: rows_of, lambda o: rows_of, s4_send.at[h], s4_recv.at[h]
        )

    for h, f in enumerate(flows):
        if f["split"]:
            total = f["mid"][f["inner"]]
            for o, copy in enumerate(second[h], 1):
                copy.wait_recv()
                total = total + f["sums2"][o].astype(jnp.float32)
        else:
            f["sums2"][here[f["two"]]] = f["mid_low"][...]
            for copy in second[h]:
                copy.wait_recv()
            total = f["sums2"][0].astype(jnp.float32)
            for o in range(1, count[f["two"]]):
                total = total + f["sums2"][o].astype(jnp.float32)
        grad_ref[f["spot"], f["columns"]] = total.astype(jnp.bfloat16)
        if f["split"]:
            block_of = grad_ref.at[f["spot"], f["columns"]]
            third.append(
                to_peers(
                    f["two"],
                    lambda o: block_of,
                    lambda o: block_of,
                    s3_send.at[h],
                    s3_recv.at[h],
                )
            )
        else:
            third.append([])
            fourth += gather(h, f)
    for h, f in enumerate(flows):
        if f["split"]:
            for copy in third[h]:
                copy.wait_recv()
            fourth += gather(h, f)
    for copy in fourth:
        copy.wait_recv()

    sent = [far_copies, near_copies, *first, *second, *third, fourth]
    for copy in [copy for group in sent for copy in group]:
        copy.wait_send()


def kernel_near(
    n_dom,
    n_grp,
    cols_hbm,
    src_hbm,
    block_hbm,
    live_hbm,
    feats_hbm,
    w_self_hbm,
    w_neigh_hbm,
    local_hbm,
    cut_hbm,
    cot_hbm,
    out_ref,
    cols_ref,
    src_ref,
    block_ref,
    live_ref,
    w_self_ref,
    w_neigh_ref,
    local_ref,
    cut_ref,
    cot_ref,
    lhs,
    pre,
    grad_pre_ref,
    near,
    outgoing,
    far,
    raw_side,
    raw_mid,
    plan_side,
    plan_mid,
    core_out,
    core_in,
    mine,
    mine_low,
    pieces,
    load_sem,
    near_send,
    near_recv,
    out_send,
    far_recv,
    raw_send,
    side_recv,
    mid_recv,
    core_send,
    core_recv,
    rs_send,
    rs_recv,
    ag_send,
    ag_recv,
    fw_send,
    fw_recv,
    mid_ready,
    line_ready,
    grp_ready,
):
    row_blocks, local_slots, block, _ = local_ref.shape
    cut_slots = cut_ref.shape[1]
    features = w_self_ref.shape[0]
    rows = row_blocks * block
    n_z = n_dom // CORES
    piece = pieces.shape[1]
    me_d, me_g = lax.axis_index("dom"), lax.axis_index("grp")
    me_z, me_c = lax.div(me_d, CORES), lax.rem(me_d, CORES)
    grp_peer = [lax.rem(me_g + o, n_grp) for o in range(n_grp)]
    steps = [(dz, dg) for dz in range(n_z) for dg in range(n_grp) if dz or dg]
    place = jnp.where(me_z < n_z // 2, me_z, n_z - 1 - me_z)
    at_end, in_middle = place == 0, place == 1

    def z_of(t):
        return jnp.where(me_z < n_z // 2, t, n_z - 1 - t)

    def dev(t, core):
        return z_of(t) * CORES + core

    side = z_of(1 - place)
    core_peer = me_d + 1 - 2 * me_c

    def flat(x):
        return x.reshape(rows, features)

    def chip_at(dz, dg):
        return lax.rem(me_z + dz, n_z), lax.rem(me_g + dg, n_grp)

    def remote(src, dst, send, recv, device):
        return pltpu.make_async_remote_copy(
            src_ref=src,
            dst_ref=dst,
            send_sem=send,
            recv_sem=recv,
            device_id=device,
            device_id_type=MESH,
        )

    def begin(copies):
        for copy in copies:
            copy.start()
        return copies

    def signal(sem, dom, grp):
        pl.semaphore_signal(sem, inc=1, device_id=(dom, grp), device_id_type=MESH)

    barrier = pltpu.get_barrier_semaphore()
    signal(barrier, core_peer, me_g)
    for core in range(CORES):
        signal(barrier, side * CORES + core, me_g)

    @pl.when(in_middle)
    def _():
        signal(barrier, dev(2, me_c), me_g)

    for o in range(1, n_grp):
        signal(barrier, me_d, grp_peer[o])
    loads = begin(
        [
            pltpu.make_async_copy(src, dst, load_sem.at[i])
            for i, (src, dst) in enumerate(
                (
                    (block_hbm, block_ref),
                    (live_hbm, live_ref),
                    (feats_hbm, lhs.at[0]),
                    (feats_hbm, near.at[pl.ds(me_g * row_blocks, row_blocks)]),
                    (cols_hbm, cols_ref),
                    (src_hbm, src_ref),
                    (w_self_hbm, w_self_ref),
                    (local_hbm, local_ref),
                    (cut_hbm, cut_ref),
                    (w_neigh_hbm, w_neigh_ref),
                    (cot_hbm, cot_ref),
                )
            )
        ]
    )

    def plan_copies(target, raw, plan, send, recv):
        device = (target, me_g)
        return [
            remote(block_hbm, plan.at[0], send.at[0], recv.at[0], device),
            remote(live_hbm, plan.at[1], send.at[1], recv.at[1], device),
            remote(feats_hbm, raw, send.at[2], recv.at[2], device),
        ]

    side_copies = plan_copies(
        side * CORES + me_c, raw_side, plan_side, raw_send.at[0], side_recv
    )
    mid_copies = plan_copies(dev(2, me_c), raw_mid, plan_mid, raw_send.at[1], mid_recv)
    pl.semaphore_wait(barrier, 3 + place + n_grp - 1)

    @pl.when(in_middle)
    def _():
        begin(mid_copies)

    begin(side_copies)
    near_copies = begin(
        [
            remote(
                feats_hbm,
                near.at[pl.ds(me_g * row_blocks, row_blocks)],
                near_send.at[o],
                near_recv.at[o],
                (me_d, grp_peer[o]),
            )
            for o in range(1, n_grp)
        ]
    )

    @pl.when(in_middle)
    def _():
        signal(mid_ready, dev(2, me_c), me_g)
        pl.semaphore_wait(mid_ready, 1)
        for core in range(CORES):
            signal(line_ready, dev(0, core), me_g)

    def chosen(blocks_of, block_at, alive):
        picked = blocks_of(block_at).astype(jnp.float32)
        return (picked * alive.astype(jnp.float32)).astype(jnp.bfloat16)

    def of_own(target):
        return chosen(lambda i: lhs[0, i], block_ref[0, target], live_ref[0, target])

    def of_side(target):
        return chosen(lambda i: raw_side[i], plan_side[0, 0, target], plan_side[1, 0, target])

    def of_mid(target):
        return chosen(lambda i: raw_mid[i], plan_mid[0, 0, target], plan_mid[1, 0, target])

    def send_block(i, source, target):
        return remote(
            outgoing.at[i], far.at[source], out_send.at[i], far_recv.at[source], (target, me_g)
        )

    for load in loads[:4]:
        load.wait()
    end_jobs = [(dev(t, core)) for t in (2, 3) for core in range(CORES)]

    @pl.when(at_end)
    def _():
        for i, target in enumerate(end_jobs):
            outgoing[2 + i] = of_own(target)
        pl.semaphore_wait(line_ready, CORES)
        for i, target in enumerate(end_jobs):
            send_block(2 + i, me_d, target).start()

    for o in range(1, n_grp):
        signal(grp_ready, me_d, grp_peer[o])
    outgoing[0] = of_own(core_peer)
    send_block(0, me_d, core_peer).start()
    far[me_d] = of_own(me_d)

    for load in loads[4:]:
        load.wait()
    pre[...] = f32_dot(flat(lhs[0]), w_self_ref[...])

    side_d, mid_d = side * CORES + me_c, dev(2, me_c)
    mid_jobs = [dev(0, 0), dev(0, 1), core_peer]

    @pl.when(in_middle)
    def _():
        for copy in mid_copies:
            copy.wait_recv()
        for i, target in enumerate(mid_jobs):
            outgoing[2 + i] = of_mid(target)
            send_block(2 + i, mid_d, target).start()
        far[mid_d] = of_mid(me_d)

    for copy in side_copies:
        copy.wait_recv()
    outgoing[1] = of_side(core_peer)
    send_block(1, side_d, core_peer).start()
    far[side_d] = of_side(me_d)

    for copy in near_copies:
        copy.wait_recv()
    acc = []
    for b in range(row_blocks):
        total = jnp.zeros((block, features), jnp.float32)
        for k in range(local_slots):
            total = total + f32_dot(local_ref[b, k], near[cols_ref[b, k]])
        acc.append(total)

    def arrived(source):
        send_block(0, source, core_peer).wait_recv()

    arrived(core_peer)
    arrived(side * CORES + 1 - me_c)

    @pl.when(in_middle)
    def _():
        arrived(dev(2, 1 - me_c))
        for core in range(CORES):
            arrived(dev(3, core))

    @pl.when(at_end)
    def _():
        for t in (2, 3):
            for core in range(CORES):
                arrived(dev(t, core))

    for b in range(row_blocks):
        here = pl.ds(b * block, block)
        total = acc[b]
        for k in range(cut_slots):
            total = total + f32_dot(cut_ref[b, k], far[lax.rem(me_d + src_ref[b, k], n_dom)])
        agg = total.astype(jnp.bfloat16)
        lhs[1, b] = agg
        preact = pre[here] + f32_dot(agg, w_neigh_ref[...])
        sig = jax.nn.sigmoid(preact)
        out_ref[here] = (preact * sig).astype(jnp.bfloat16)
        grad_pre_ref[here] = (
            cot_ref[here].astype(jnp.float32) * sig * (1.0 + preact * (1.0 - sig))
        ).astype(jnp.bfloat16)

    def product(which):
        return lax.dot_general(
            flat(lhs[which]),
            grad_pre_ref[...],
            (((0,), (0,)), ((), ())),
            preferred_element_type=jnp.float32,
        )

    core_out[...] = product(1 - me_c).astype(jnp.bfloat16)
    core_copy = remote(core_out, core_in, core_send, core_recv, (core_peer, me_g))
    core_copy.start()
    mine[...] = product(me_c)
    pl.semaphore_wait(grp_ready, n_grp - 1)
    core_copy.wait_recv()
    total = mine[...] + core_in[...].astype(jnp.float32)
    mine[...] = total
    mine_low[...] = total.astype(jnp.bfloat16)

    def rows_of(z, g):
        return pl.ds(pl.multiple_of((z * n_grp + g) * piece, piece), piece)

    first = []
    for i, (dz, dg) in enumerate(steps):
        z, g = chip_at(dz, dg)
        first.append(
            remote(
                mine_low.at[rows_of(z, g)],
                pieces.at[i],
                rs_send.at[i],
                rs_recv.at[i],
                (z * CORES + me_c, g),
            )
        )
    begin(sorted_far(first, steps, n_z))
    total = mine[rows_of(me_z, me_g)]
    for i, copy in enumerate(first):
        copy.wait_recv()
        total = total + pieces[i].astype(jnp.float32)

    def spot(z, g):
        start = rows + me_c * features + (z * n_grp + g) * piece
        return out_ref.at[pl.ds(pl.multiple_of(start, piece), piece)]

    own = spot(me_z, me_g)
    own[...] = total.astype(jnp.bfloat16)
    second = []
    for i, (dz, dg) in enumerate(steps):
        z, g = chip_at(dz, dg)
        second.append(remote(own, own, ag_send.at[i], ag_recv.at[i], (z * CORES + me_c, g)))
    begin(sorted_far(second, steps, n_z))
    forward = begin([remote(own, own, fw_send.at[0], fw_recv.at[0], (core_peer, me_g))])
    for i, (dz, dg) in enumerate(steps):
        second[i].wait_recv()
        part = spot(lax.rem(me_z - dz + n_z, n_z), lax.rem(me_g - dg + n_grp, n_grp))
        forward += begin(
            [remote(part, part, fw_send.at[i + 1], fw_recv.at[i + 1], (core_peer, me_g))]
        )
    for copy in forward:
        copy.wait_recv()

    for copy in [*near_copies, *side_copies, core_copy, *first, *second, *forward]:
        copy.wait_send()
    for i in range(2):
        send_block(i, me_d, core_peer).wait_send()

    @pl.when(in_middle)
    def _():
        for copy in mid_copies:
            copy.wait_send()
        for i, target in enumerate(mid_jobs):
            send_block(2 + i, mid_d, target).wait_send()

    @pl.when(at_end)
    def _():
        for i, target in enumerate(end_jobs):
            send_block(2 + i, me_d, target).wait_send()


def sorted_far(copies, steps, n_z):
    order = sorted(range(len(steps)), key=lambda i: -min(steps[i][0], n_z - steps[i][0]))
    return [copies[i] for i in order]


def body_wide(
    feats,
    w_self,
    w_neigh,
    local_tiles,
    local_cols,
    cut_tiles,
    cut_src,
    send_block,
    send_live,
    cotangent,
):
    row_blocks, _, block, _ = local_tiles.shape
    features = feats.shape[1]
    n_dom, n_grp = lax.axis_size("dom"), lax.axis_size("grp")
    blocks = (row_blocks, block, features)
    halves = len(ORDERS)
    count = {"grp": n_grp, "dom": n_dom}
    most = max(n_grp, n_dom)
    sizes = []
    for one, two in ORDERS:
        rows = 2 * features // count[one]
        sizes.append((count[one], rows, count[two], piece_rows(rows, count[two])))
    width = features // halves
    dma = pltpu.SemaphoreType.DMA
    hbm = pl.BlockSpec(memory_space=pltpu.HBM)
    vmem = pl.BlockSpec(memory_space=pltpu.VMEM)
    out, grads = pl.pallas_call(
        functools.partial(kernel_wide, n_dom, n_grp),
        out_shape=(
            jax.ShapeDtypeStruct(blocks, jnp.bfloat16),
            jax.ShapeDtypeStruct((2 * features, features), jnp.bfloat16),
        ),
        in_specs=[hbm] * 10,
        out_specs=(vmem, vmem),
        scratch_shapes=[
            pltpu.SMEM(local_cols.shape, jnp.int32),
            pltpu.SMEM(cut_src.shape, jnp.int32),
            pltpu.SMEM(send_block.shape, jnp.int32),
            pltpu.SMEM(send_live.shape, jnp.int32),
            pltpu.VMEM(w_self.shape, jnp.bfloat16),
            pltpu.VMEM(w_neigh.shape, jnp.bfloat16),
            pltpu.VMEM(local_tiles.shape, jnp.bfloat16),
            pltpu.VMEM(cut_tiles.shape, jnp.bfloat16),
            pltpu.VMEM(blocks, jnp.bfloat16),
            pltpu.VMEM(blocks, jnp.bfloat16),
            pltpu.VMEM((n_grp * row_blocks, block, features), jnp.bfloat16),
            pltpu.VMEM((n_dom, block, features), jnp.bfloat16),
            pltpu.VMEM((n_dom, block, features), jnp.bfloat16),
            pltpu.VMEM(blocks, jnp.float32),
            pltpu.VMEM(blocks, jnp.float32),
            pltpu.VMEM((halves, 2 * features, width), jnp.float32),
            pltpu.VMEM((halves, 2 * features, width), jnp.bfloat16),
        ]
        + [pltpu.VMEM((n, r, width), jnp.bfloat16) for n, r, _, _ in sizes]
        + [pltpu.VMEM((r, width), jnp.float32) for _, r, _, _ in sizes]
        + [pltpu.VMEM((r, width), jnp.bfloat16) for _, r, _, _ in sizes]
        + [pltpu.VMEM((n, p, width), jnp.bfloat16) for _, _, n, p in sizes]
        + [
            dma((11,)),
        ]
        + [dma((n_grp,))] * 2
        + [dma((n_dom,))] * 2
        + [dma((halves, most))] * 8,
        compiler_params=pltpu.CompilerParams(
            collective_id=0, has_side_effects=True, vmem_limit_bytes=32 * 2**20
        ),
    )(
        *(
            pltpu.with_memory_space_constraint(x, pltpu.HBM)
            for x in (
                local_cols,
                cut_src,
                send_block,
                send_live,
                feats.reshape(blocks),
                w_self,
                w_neigh,
                local_tiles,
                cut_tiles,
                cotangent.reshape(blocks),
            )
        )
    )
    summed = grads.astype(jnp.float32)
    return (out.reshape(feats.shape), summed[:features], summed[features:])


def body_near(
    feats,
    w_self,
    w_neigh,
    local_tiles,
    local_cols,
    cut_tiles,
    cut_src,
    send_block,
    send_live,
    cotangent,
):
    row_blocks, _, block, _ = local_tiles.shape
    rows, features = feats.shape
    blocks = (row_blocks, block, features)
    n_dom, n_grp = lax.axis_size("dom"), lax.axis_size("grp")
    chips = n_dom // CORES * n_grp
    piece = features // chips
    dma = pltpu.SemaphoreType.DMA
    hbm = pl.BlockSpec(memory_space=pltpu.HBM)
    vmem = pl.BlockSpec(memory_space=pltpu.VMEM)
    low = functools.partial(pltpu.VMEM, dtype=jnp.bfloat16)
    wide = functools.partial(pltpu.VMEM, dtype=jnp.float32)
    res = pl.pallas_call(
        functools.partial(kernel_near, n_dom, n_grp),
        out_shape=jax.ShapeDtypeStruct((rows + 2 * features, features), jnp.bfloat16),
        in_specs=[hbm] * 10,
        out_specs=vmem,
        scratch_shapes=[
            pltpu.SMEM(local_cols.shape, jnp.int32),
            pltpu.SMEM(cut_src.shape, jnp.int32),
            pltpu.SMEM(send_block.shape, jnp.int32),
            pltpu.SMEM(send_live.shape, jnp.int32),
            low(w_self.shape),
            low(w_neigh.shape),
            low(local_tiles.shape),
            low(cut_tiles.shape),
            low(feats.shape),
            low((2, *blocks)),
            wide((rows, features)),
            low((rows, features)),
            low((n_grp * row_blocks, block, features)),
            low((6, block, features)),
            low((n_dom, block, features)),
            low(blocks),
            low(blocks),
            pltpu.SMEM((2, *send_block.shape), jnp.int32),
            pltpu.SMEM((2, *send_block.shape), jnp.int32),
            low((features, features)),
            low((features, features)),
            wide((features, features)),
            low((features, features)),
            low((chips - 1, piece, features)),
            dma((11,)),
            dma((n_grp,)),
            dma((n_grp,)),
            dma((6,)),
            dma((n_dom,)),
            dma((2, 3)),
            dma((3,)),
            dma((3,)),
            dma,
            dma,
        ]
        + [dma((chips,))] * 6
        + [pltpu.SemaphoreType.REGULAR] * 3,
        compiler_params=pltpu.CompilerParams(
            collective_id=0, has_side_effects=True, vmem_limit_bytes=32 * 2**20
        ),
    )(
        *(
            pltpu.with_memory_space_constraint(x, pltpu.HBM)
            for x in (
                local_cols,
                cut_src,
                send_block,
                send_live,
                feats.reshape(blocks),
                w_self,
                w_neigh,
                local_tiles,
                cut_tiles,
                cotangent,
            )
        )
    )
    return (
        res[:rows],
        res[rows : rows + features].astype(jnp.float32),
        res[rows + features :].astype(jnp.float32),
    )


def solution(mesh):
    n_dom, n_grp = mesh.shape["dom"], mesh.shape["grp"]
    chips = n_dom // CORES * n_grp
    return jax.shard_map(
        lambda *args: (
            body_near
            if n_dom == LINE * CORES and args[1].shape[0] % (PACK * chips) == 0
            else body_wide
        )(*args),
        mesh=mesh,
        in_specs=(
            P(("dom", "grp"), None),
            P(),
            P(),
            P(("dom", "grp"), None, None, None),
            P(("dom", "grp"), None),
            P(("dom", "grp"), None, None, None),
            P(("dom", "grp"), None),
            P(("dom", "grp"), None),
            P(("dom", "grp"), None),
            P(("dom", "grp"), None),
        ),
        out_specs=(P(("dom", "grp"), None), P(), P()),
        check_vma=False,
    )
```

```python
import functools

import jax
import jax.numpy as jnp
from jax import lax
from jax.experimental import pallas as pl
from jax.experimental.pallas import tpu as pltpu
from jax.sharding import PartitionSpec as P

MESH = pl.DeviceIdType.MESH
PACK = 16
FEW = 4
CORES = 2
LINE = 4
ORDERS = (("grp", "dom"), ("dom", "grp"))


def piece_rows(rows, n):
    return rows // n if n > FEW and rows % (PACK * n) == 0 else rows


def f32_dot(a, b):
    return jnp.dot(a, b, preferred_element_type=jnp.float32)


def kernel_wide(
    n_dom,
    n_grp,
    cols_hbm,
    src_hbm,
    block_hbm,
    live_hbm,
    feats_hbm,
    w_self_hbm,
    w_neigh_hbm,
    local_hbm,
    cut_hbm,
    cot_hbm,
    out_ref,
    grad_ref,
    cols_ref,
    src_ref,
    block_ref,
    live_ref,
    w_self_ref,
    w_neigh_ref,
    local_ref,
    cut_ref,
    cot_ref,
    feats_ref,
    near,
    outgoing,
    far,
    acc,
    pre,
    part,
    part_low,
    sums1_a,
    sums1_b,
    mid_a,
    mid_b,
    low_a,
    low_b,
    sums2_a,
    sums2_b,
    load_sem,
    near_send,
    near_recv,
    far_send,
    far_recv,
    s1_send,
    s1_recv,
    s2_send,
    s2_recv,
    s3_send,
    s3_recv,
    s4_send,
    s4_recv,
):
    sums1, mid, mid_low = (sums1_a, sums1_b), (mid_a, mid_b), (low_a, low_b)
    sums2 = (sums2_a, sums2_b)
    row_blocks, local_slots, block, _ = local_ref.shape
    cut_slots = cut_ref.shape[1]
    features = w_self_ref.shape[0]
    width = part.shape[2]
    me_d, me_g = lax.axis_index("dom"), lax.axis_index("grp")
    dom_peer = [lax.rem(me_d + o, n_dom) for o in range(n_dom)]
    grp_peer = [lax.rem(me_g + o, n_grp) for o in range(n_grp)]

    def remote(src, dst, send, recv, o, axis):
        peer = dom_peer[o] if axis == "dom" else grp_peer[o]
        return pltpu.make_async_remote_copy(
            src_ref=src,
            dst_ref=dst,
            send_sem=send,
            recv_sem=recv,
            device_id={axis: peer},
            device_id_type=MESH,
        )

    def begin(copies):
        for copy in copies:
            copy.start()
        return copies

    barrier = pltpu.get_barrier_semaphore()
    for o in range(1, n_dom):
        pl.semaphore_signal(barrier, inc=1, device_id={"dom": dom_peer[o]}, device_id_type=MESH)
    for o in range(1, n_grp):
        pl.semaphore_signal(barrier, inc=1, device_id={"grp": grp_peer[o]}, device_id_type=MESH)
    loads = begin(
        [
            pltpu.make_async_copy(src, dst, load_sem.at[i])
            for i, (src, dst) in enumerate(
                (
                    (block_hbm, block_ref),
                    (live_hbm, live_ref),
                    (feats_hbm, feats_ref),
                    (feats_hbm, near.at[pl.ds(0, row_blocks)]),
                    (cols_hbm, cols_ref),
                    (src_hbm, src_ref),
                    (w_self_hbm, w_self_ref),
                    (local_hbm, local_ref),
                    (cut_hbm, cut_ref),
                    (w_neigh_hbm, w_neigh_ref),
                    (cot_hbm, cot_ref),
                )
            )
        ]
    )
    for load in loads[:3]:
        load.wait()

    for o in range(n_dom):
        alive = live_ref[0, dom_peer[o]].astype(jnp.float32)
        chosen = feats_ref[block_ref[0, dom_peer[o]]].astype(jnp.float32)
        target = far if o == 0 else outgoing
        target[o] = (chosen * alive).astype(jnp.bfloat16)
    pl.semaphore_wait(barrier, n_dom + n_grp - 2)

    far_copies = begin(
        [
            remote(outgoing.at[o], far.at[o], far_send.at[o], far_recv.at[o], o, "dom")
            for o in sorted(range(1, n_dom), key=lambda o: abs(2 * o - n_dom))
        ]
    )
    near_copies = begin(
        [
            remote(
                feats_ref,
                near.at[pl.ds(o * row_blocks, row_blocks)],
                near_send.at[o],
                near_recv.at[o],
                o,
                "grp",
            )
            for o in range(1, n_grp)
        ]
    )

    for load in loads[3:]:
        load.wait()
    for b in range(row_blocks):
        pre[b] = f32_dot(feats_ref[b], w_self_ref[...])
    for copy in near_copies:
        copy.wait_recv()
    for b in range(row_blocks):
        total = jnp.zeros((block, features), jnp.float32)
        for k in range(local_slots):
            col = cols_ref[b, k]
            owner = lax.div(col, row_blocks)
            slot = lax.rem(me_g - owner + n_grp, n_grp)
            where = slot * row_blocks + lax.rem(col, row_blocks)
            total = total + f32_dot(local_ref[b, k], near[where])
        acc[b] = total

    for copy in far_copies:
        copy.wait_recv()
    grads_own = jnp.zeros((features, features), jnp.float32)
    grads_agg = jnp.zeros((features, features), jnp.float32)
    for b in range(row_blocks):
        total = acc[b]
        for k in range(cut_slots):
            slot = lax.rem(n_dom - src_ref[b, k], n_dom)
            total = total + f32_dot(cut_ref[b, k], far[slot])
        agg = total.astype(jnp.bfloat16)
        own = feats_ref[b]
        preact = pre[b] + f32_dot(agg, w_neigh_ref[...])
        sig = jax.nn.sigmoid(preact)
        out_ref[b] = (preact * sig).astype(jnp.bfloat16)
        grad_pre = (
            cot_ref[b].astype(jnp.float32) * sig * (1.0 + preact * (1.0 - sig))
        ).astype(jnp.bfloat16)
        dims = (((0,), (0,)), ((), ()))
        grads_own = grads_own + lax.dot_general(
            own, grad_pre, dims, preferred_element_type=jnp.float32
        )
        grads_agg = grads_agg + lax.dot_general(
            agg, grad_pre, dims, preferred_element_type=jnp.float32
        )

    peers = {"grp": grp_peer, "dom": dom_peer}
    here = {"grp": me_g, "dom": me_d}
    count = {"grp": n_grp, "dom": n_dom}

    def rows_at(start, size):
        return pl.ds(pl.multiple_of(start, size), size)

    def to_peers(axis, src, dst, send, recv):
        return begin(
            [
                remote(src(o), dst(o), send.at[o], recv.at[o], o, axis)
                for o in range(1, count[axis])
            ]
        )

    flows = []
    for h, (one, two) in enumerate(ORDERS):
        rows = 2 * features // count[one]
        piece = piece_rows(rows, count[two])
        split = piece < rows
        flows.append(
            dict(
                one=one,
                two=two,
                rows=rows,
                piece=piece,
                split=split,
                columns=pl.ds(h * width, width),
                mine=rows_at(here[one] * rows, rows),
                inner=rows_at(here[two] * piece, piece) if split else pl.ds(0, rows),
                spot=rows_at(here[one] * rows + (here[two] * piece if split else 0), piece),
                sums1=sums1[h],
                mid=mid[h],
                mid_low=mid_low[h],
                sums2=sums2[h],
            )
        )

    first = []
    for h, f in enumerate(flows):
        cut = slice(h * width, (h + 1) * width)
        part[h, 0:features] = grads_own[:, cut]
        part[h, features : 2 * features] = grads_agg[:, cut]
        part_low[h, 0:features] = grads_own[:, cut].astype(jnp.bfloat16)
        part_low[h, features : 2 * features] = grads_agg[:, cut].astype(jnp.bfloat16)
        first.append(
            to_peers(
                f["one"],
                lambda o: part_low.at[h, rows_at(peers[f["one"]][o] * f["rows"], f["rows"])],
                lambda o: f["sums1"].at[o],
                s1_send.at[h],
                s1_recv.at[h],
            )
        )
    second = []
    for h, f in enumerate(flows):
        total = part[h, f["mine"]]
        for o, copy in enumerate(first[h], 1):
            copy.wait_recv()
            total = total + f["sums1"][o].astype(jnp.float32)
        f["mid"][...] = total
        f["mid_low"][...] = total.astype(jnp.bfloat16)
        second.append(
            to_peers(
                f["two"],
                lambda o: f["mid_low"].at[rows_at(peers[f["two"]][o] * f["piece"], f["piece"])]
                if f["split"]
                else f["mid_low"],
                lambda o: f["sums2"].at[o if f["split"] else here[f["two"]]],
                s2_send.at[h],
                s2_recv.at[h],
            )
        )
    third, fourth = [], []

    def gather(h, f):
        rows_of = grad_ref.at[f["mine"], f["columns"]]
        return to_peers(
            f["one"], lambda o: rows_of, lambda o: rows_of, s4_send.at[h], s4_recv.at[h]
        )

    for h, f in enumerate(flows):
        if f["split"]:
            total = f["mid"][f["inner"]]
            for o, copy in enumerate(second[h], 1):
                copy.wait_recv()
                total = total + f["sums2"][o].astype(jnp.float32)
        else:
            f["sums2"][here[f["two"]]] = f["mid_low"][...]
            for copy in second[h]:
                copy.wait_recv()
            total = f["sums2"][0].astype(jnp.float32)
            for o in range(1, count[f["two"]]):
                total = total + f["sums2"][o].astype(jnp.float32)
        grad_ref[f["spot"], f["columns"]] = total.astype(jnp.bfloat16)
        if f["split"]:
            block_of = grad_ref.at[f["spot"], f["columns"]]
            third.append(
                to_peers(
                    f["two"],
                    lambda o: block_of,
                    lambda o: block_of,
                    s3_send.at[h],
                    s3_recv.at[h],
                )
            )
        else:
            third.append([])
            fourth += gather(h, f)
    for h, f in enumerate(flows):
        if f["split"]:
            for copy in third[h]:
                copy.wait_recv()
            fourth += gather(h, f)
    for copy in fourth:
        copy.wait_recv()

    sent = [far_copies, near_copies, *first, *second, *third, fourth]
    for copy in [copy for group in sent for copy in group]:
        copy.wait_send()


def kernel_near(
    n_dom,
    n_grp,
    cols_hbm,
    src_hbm,
    block_hbm,
    live_hbm,
    feats_hbm,
    w_self_hbm,
    w_neigh_hbm,
    local_hbm,
    cut_hbm,
    cot_hbm,
    out_ref,
    cols_ref,
    src_ref,
    block_ref,
    live_ref,
    w_self_ref,
    w_neigh_ref,
    local_ref,
    cut_ref,
    cot_ref,
    lhs,
    pre,
    grad_pre_ref,
    near,
    outgoing,
    far,
    raw_side,
    raw_mid_a,
    raw_mid_b,
    plan_side,
    plan_mid,
    core_out,
    core_in,
    mine,
    mine_low,
    pieces,
    load_sem,
    near_send,
    near_recv,
    out_send,
    far_recv,
    raw_send,
    side_recv,
    mid_recv,
    core_send,
    core_recv,
    rs_send,
    rs_recv,
    ag_send,
    ag_recv,
    fw_send,
    fw_recv,
    side_ready,
    mid_ready,
    line_ready,
    grp_ready,
):
    row_blocks, local_slots, block, _ = local_ref.shape
    cut_slots = cut_ref.shape[1]
    features = w_self_ref.shape[0]
    rows = row_blocks * block
    n_z = n_dom // CORES
    piece = pieces.shape[1]
    me_d, me_g = lax.axis_index("dom"), lax.axis_index("grp")
    me_z, me_c = lax.div(me_d, CORES), lax.rem(me_d, CORES)
    grp_peer = [lax.rem(me_g + o, n_grp) for o in range(n_grp)]
    steps = [(dz, dg) for dz in range(n_z) for dg in range(n_grp) if dz or dg]
    place = jnp.where(me_z < n_z // 2, me_z, n_z - 1 - me_z)
    at_end, in_middle = place == 0, place == 1

    def z_of(t):
        return jnp.where(me_z < n_z // 2, t, n_z - 1 - t)

    def dev(t, core):
        return z_of(t) * CORES + core

    side = z_of(1 - place)
    core_peer = me_d + 1 - 2 * me_c
    raw_mids = (raw_mid_a, raw_mid_b)
    halves = [pl.ds(h * (block // 2), block // 2) for h in range(2)]

    def flat(x):
        return x.reshape(rows, features)

    def chip_at(dz, dg):
        return lax.rem(me_z + dz, n_z), lax.rem(me_g + dg, n_grp)

    def remote(src, dst, send, recv, device):
        return pltpu.make_async_remote_copy(
            src_ref=src,
            dst_ref=dst,
            send_sem=send,
            recv_sem=recv,
            device_id=device,
            device_id_type=MESH,
        )

    def begin(copies):
        for copy in copies:
            copy.start()
        return copies

    def signal(sem, dom, grp):
        pl.semaphore_signal(sem, inc=1, device_id=(dom, grp), device_id_type=MESH)

    barrier = pltpu.get_barrier_semaphore()
    signal(barrier, core_peer, me_g)

    @pl.when(in_middle)
    def _():
        signal(barrier, dev(2, me_c), me_g)
        for core in range(CORES):
            signal(barrier, dev(0, core), me_g)

    for o in range(1, n_grp):
        signal(barrier, me_d, grp_peer[o])
    loads = begin(
        [
            pltpu.make_async_copy(src, dst, load_sem.at[i])
            for i, (src, dst) in enumerate(
                (
                    (block_hbm, block_ref),
                    (live_hbm, live_ref),
                    (feats_hbm, lhs.at[0]),
                    (feats_hbm, near.at[pl.ds(me_g * row_blocks, row_blocks)]),
                    (cols_hbm, cols_ref),
                    (src_hbm, src_ref),
                    (w_self_hbm, w_self_ref),
                    (local_hbm, local_ref),
                    (cut_hbm, cut_ref),
                    (w_neigh_hbm, w_neigh_ref),
                    (cot_hbm, cot_ref),
                )
            )
        ]
    )

    def plan_copies(target, plan, send, recv):
        device = (target, me_g)
        return [
            remote(block_hbm, plan.at[0], send.at[0], recv.at[0], device),
            remote(live_hbm, plan.at[1], send.at[1], recv.at[1], device),
        ]

    side_d = side * CORES + me_c
    side_copies = plan_copies(side_d, plan_side, raw_send.at[0], side_recv)
    side_copies.append(
        remote(feats_hbm, raw_side, raw_send.at[0, 2], side_recv.at[2], (side_d, me_g))
    )
    mid_copies = plan_copies(dev(2, me_c), plan_mid, raw_send.at[1], mid_recv)
    mid_copies += [
        remote(
            feats_hbm.at[:, part],
            raw_mids[h],
            raw_send.at[1, 2 + h],
            mid_recv.at[2 + h],
            (dev(2, me_c), me_g),
        )
        for h, part in enumerate(halves)
    ]
    pl.semaphore_wait(barrier, CORES + 1 - place + n_grp - 1)

    @pl.when(in_middle)
    def _():
        begin(mid_copies)

    @pl.when(at_end)
    def _():
        for core in range(CORES):
            signal(side_ready, dev(1, core), me_g)
        begin(side_copies)

    near_copies = begin(
        [
            remote(
                feats_hbm,
                near.at[pl.ds(me_g * row_blocks, row_blocks)],
                near_send.at[o],
                near_recv.at[o],
                (me_d, grp_peer[o]),
            )
            for o in range(1, n_grp)
        ]
    )

    @pl.when(in_middle)
    def _():
        pl.semaphore_wait(side_ready, CORES)
        begin(side_copies)
        signal(mid_ready, dev(2, me_c), me_g)
        pl.semaphore_wait(mid_ready, 1)
        for core in range(CORES):
            signal(line_ready, dev(0, core), me_g)

    def chosen(blocks_of, block_at, alive):
        picked = blocks_of(block_at).astype(jnp.float32)
        return (picked * alive.astype(jnp.float32)).astype(jnp.bfloat16)

    def of_own(target):
        return chosen(lambda i: lhs[0, i], block_ref[0, target], live_ref[0, target])

    def of_side(target):
        return chosen(lambda i: raw_side[i], plan_side[0, 0, target], plan_side[1, 0, target])

    def of_mid(target, part):
        return chosen(
            lambda i: raw_mids[part][i], plan_mid[0, 0, target], plan_mid[1, 0, target]
        )

    def send_block(i, source, target):
        return remote(
            outgoing.at[i],
            far.at[source],
            out_send.at[i, 0],
            far_recv.at[source, 0],
            (target, me_g),
        )

    def send_half(i, source, target, h):
        return remote(
            outgoing.at[i, halves[h]],
            far.at[source, halves[h]],
            out_send.at[i, h],
            far_recv.at[source, h],
            (target, me_g),
        )

    for load in loads[:4]:
        load.wait()
    end_jobs = [(dev(t, core)) for t in (3, 2) for core in range(CORES)]

    @pl.when(at_end)
    def _():
        for i, target in enumerate(end_jobs):
            outgoing[2 + i] = of_own(target)
        pl.semaphore_wait(line_ready, CORES)
        for i, target in enumerate(end_jobs):
            send_block(2 + i, me_d, target).start()

    for o in range(1, n_grp):
        signal(grp_ready, me_d, grp_peer[o])
    outgoing[0] = of_own(core_peer)
    send_block(0, me_d, core_peer).start()
    far[me_d] = of_own(me_d)

    for load in loads[4:]:
        load.wait()
    pre[...] = f32_dot(flat(lhs[0]), w_self_ref[...])

    mid_d = dev(2, me_c)
    mid_jobs = [dev(0, 0), dev(0, 1), core_peer]

    @pl.when(in_middle)
    def _():
        for copy in mid_copies[:2]:
            copy.wait_recv()
        for h, part in enumerate(halves):
            mid_copies[2 + h].wait_recv()
            for i, target in enumerate(mid_jobs):
                outgoing[2 + i, part] = of_mid(target, h)
                send_half(2 + i, mid_d, target, h).start()
            far[mid_d, part] = of_mid(me_d, h)

    for copy in side_copies:
        copy.wait_recv()
    outgoing[1] = of_side(core_peer)
    send_block(1, side_d, core_peer).start()
    far[side_d] = of_side(me_d)

    for copy in near_copies:
        copy.wait_recv()
    acc = []
    for b in range(row_blocks):
        total = jnp.zeros((block, features), jnp.float32)
        for k in range(local_slots):
            total = total + f32_dot(local_ref[b, k], near[cols_ref[b, k]])
        acc.append(total)

    def arrived(source):
        send_block(0, source, core_peer).wait_recv()

    def arrived_halves(source):
        for h in range(2):
            send_half(0, source, core_peer, h).wait_recv()

    arrived(core_peer)
    arrived(side * CORES + 1 - me_c)

    @pl.when(in_middle)
    def _():
        arrived_halves(dev(2, 1 - me_c))
        for core in range(CORES):
            arrived(dev(3, core))

    @pl.when(at_end)
    def _():
        for core in range(CORES):
            arrived_halves(dev(2, core))
            arrived(dev(3, core))

    for b in range(row_blocks):
        here = pl.ds(b * block, block)
        total = acc[b]
        for k in range(cut_slots):
            total = total + f32_dot(cut_ref[b, k], far[lax.rem(me_d + src_ref[b, k], n_dom)])
        agg = total.astype(jnp.bfloat16)
        lhs[1, b] = agg
        preact = pre[here] + f32_dot(agg, w_neigh_ref[...])
        sig = jax.nn.sigmoid(preact)
        out_ref[here] = (preact * sig).astype(jnp.bfloat16)
        grad_pre_ref[here] = (
            cot_ref[here].astype(jnp.float32) * sig * (1.0 + preact * (1.0 - sig))
        ).astype(jnp.bfloat16)

    def product(which):
        return lax.dot_general(
            flat(lhs[which]),
            grad_pre_ref[...],
            (((0,), (0,)), ((), ())),
            preferred_element_type=jnp.float32,
        )

    core_out[...] = product(1 - me_c).astype(jnp.bfloat16)
    core_copy = remote(core_out, core_in, core_send, core_recv, (core_peer, me_g))
    core_copy.start()
    mine[...] = product(me_c)
    pl.semaphore_wait(grp_ready, n_grp - 1)
    core_copy.wait_recv()
    total = mine[...] + core_in[...].astype(jnp.float32)
    mine[...] = total
    mine_low[...] = total.astype(jnp.bfloat16)

    def rows_of(z, g):
        return pl.ds(pl.multiple_of((z * n_grp + g) * piece, piece), piece)

    first = []
    for i, (dz, dg) in enumerate(steps):
        z, g = chip_at(dz, dg)
        first.append(
            remote(
                mine_low.at[rows_of(z, g)],
                pieces.at[i],
                rs_send.at[i],
                rs_recv.at[i],
                (z * CORES + me_c, g),
            )
        )
    begin(sorted_far(first, steps, n_z))
    total = mine[rows_of(me_z, me_g)]
    for i, copy in enumerate(first):
        copy.wait_recv()
        total = total + pieces[i].astype(jnp.float32)

    def spot(z, g):
        start = rows + me_c * features + (z * n_grp + g) * piece
        return out_ref.at[pl.ds(pl.multiple_of(start, piece), piece)]

    own = spot(me_z, me_g)
    own[...] = total.astype(jnp.bfloat16)
    second = []
    for i, (dz, dg) in enumerate(steps):
        z, g = chip_at(dz, dg)
        second.append(remote(own, own, ag_send.at[i], ag_recv.at[i], (z * CORES + me_c, g)))
    begin(sorted_far(second, steps, n_z))
    forward = begin([remote(own, own, fw_send.at[0], fw_recv.at[0], (core_peer, me_g))])
    for i, (dz, dg) in enumerate(steps):
        second[i].wait_recv()
        part = spot(lax.rem(me_z - dz + n_z, n_z), lax.rem(me_g - dg + n_grp, n_grp))
        forward += begin(
            [remote(part, part, fw_send.at[i + 1], fw_recv.at[i + 1], (core_peer, me_g))]
        )
    for copy in forward:
        copy.wait_recv()

    for copy in [*near_copies, *side_copies, core_copy, *first, *second, *forward]:
        copy.wait_send()
    for i in range(2):
        send_block(i, me_d, core_peer).wait_send()

    @pl.when(in_middle)
    def _():
        for copy in mid_copies:
            copy.wait_send()
        for i, target in enumerate(mid_jobs):
            for h in range(2):
                send_half(2 + i, mid_d, target, h).wait_send()

    @pl.when(at_end)
    def _():
        for i, target in enumerate(end_jobs):
            send_block(2 + i, me_d, target).wait_send()


def sorted_far(copies, steps, n_z):
    order = sorted(range(len(steps)), key=lambda i: -min(steps[i][0], n_z - steps[i][0]))
    return [copies[i] for i in order]


def body_wide(
    feats,
    w_self,
    w_neigh,
    local_tiles,
    local_cols,
    cut_tiles,
    cut_src,
    send_block,
    send_live,
    cotangent,
):
    row_blocks, _, block, _ = local_tiles.shape
    features = feats.shape[1]
    n_dom, n_grp = lax.axis_size("dom"), lax.axis_size("grp")
    blocks = (row_blocks, block, features)
    halves = len(ORDERS)
    count = {"grp": n_grp, "dom": n_dom}
    most = max(n_grp, n_dom)
    sizes = []
    for one, two in ORDERS:
        rows = 2 * features // count[one]
        sizes.append((count[one], rows, count[two], piece_rows(rows, count[two])))
    width = features // halves
    dma = pltpu.SemaphoreType.DMA
    hbm = pl.BlockSpec(memory_space=pltpu.HBM)
    vmem = pl.BlockSpec(memory_space=pltpu.VMEM)
    out, grads = pl.pallas_call(
        functools.partial(kernel_wide, n_dom, n_grp),
        out_shape=(
            jax.ShapeDtypeStruct(blocks, jnp.bfloat16),
            jax.ShapeDtypeStruct((2 * features, features), jnp.bfloat16),
        ),
        in_specs=[hbm] * 10,
        out_specs=(vmem, vmem),
        scratch_shapes=[
            pltpu.SMEM(local_cols.shape, jnp.int32),
            pltpu.SMEM(cut_src.shape, jnp.int32),
            pltpu.SMEM(send_block.shape, jnp.int32),
            pltpu.SMEM(send_live.shape, jnp.int32),
            pltpu.VMEM(w_self.shape, jnp.bfloat16),
            pltpu.VMEM(w_neigh.shape, jnp.bfloat16),
            pltpu.VMEM(local_tiles.shape, jnp.bfloat16),
            pltpu.VMEM(cut_tiles.shape, jnp.bfloat16),
            pltpu.VMEM(blocks, jnp.bfloat16),
            pltpu.VMEM(blocks, jnp.bfloat16),
            pltpu.VMEM((n_grp * row_blocks, block, features), jnp.bfloat16),
            pltpu.VMEM((n_dom, block, features), jnp.bfloat16),
            pltpu.VMEM((n_dom, block, features), jnp.bfloat16),
            pltpu.VMEM(blocks, jnp.float32),
            pltpu.VMEM(blocks, jnp.float32),
            pltpu.VMEM((halves, 2 * features, width), jnp.float32),
            pltpu.VMEM((halves, 2 * features, width), jnp.bfloat16),
        ]
        + [pltpu.VMEM((n, r, width), jnp.bfloat16) for n, r, _, _ in sizes]
        + [pltpu.VMEM((r, width), jnp.float32) for _, r, _, _ in sizes]
        + [pltpu.VMEM((r, width), jnp.bfloat16) for _, r, _, _ in sizes]
        + [pltpu.VMEM((n, p, width), jnp.bfloat16) for _, _, n, p in sizes]
        + [
            dma((11,)),
        ]
        + [dma((n_grp,))] * 2
        + [dma((n_dom,))] * 2
        + [dma((halves, most))] * 8,
        compiler_params=pltpu.CompilerParams(
            collective_id=0, has_side_effects=True, vmem_limit_bytes=32 * 2**20
        ),
    )(
        *(
            pltpu.with_memory_space_constraint(x, pltpu.HBM)
            for x in (
                local_cols,
                cut_src,
                send_block,
                send_live,
                feats.reshape(blocks),
                w_self,
                w_neigh,
                local_tiles,
                cut_tiles,
                cotangent.reshape(blocks),
            )
        )
    )
    summed = grads.astype(jnp.float32)
    return (out.reshape(feats.shape), summed[:features], summed[features:])


def body_near(
    feats,
    w_self,
    w_neigh,
    local_tiles,
    local_cols,
    cut_tiles,
    cut_src,
    send_block,
    send_live,
    cotangent,
):
    row_blocks, _, block, _ = local_tiles.shape
    rows, features = feats.shape
    blocks = (row_blocks, block, features)
    n_dom, n_grp = lax.axis_size("dom"), lax.axis_size("grp")
    chips = n_dom // CORES * n_grp
    piece = features // chips
    dma = pltpu.SemaphoreType.DMA
    hbm = pl.BlockSpec(memory_space=pltpu.HBM)
    vmem = pl.BlockSpec(memory_space=pltpu.VMEM)
    low = functools.partial(pltpu.VMEM, dtype=jnp.bfloat16)
    wide = functools.partial(pltpu.VMEM, dtype=jnp.float32)
    res = pl.pallas_call(
        functools.partial(kernel_near, n_dom, n_grp),
        out_shape=jax.ShapeDtypeStruct((rows + 2 * features, features), jnp.bfloat16),
        in_specs=[hbm] * 10,
        out_specs=vmem,
        scratch_shapes=[
            pltpu.SMEM(local_cols.shape, jnp.int32),
            pltpu.SMEM(cut_src.shape, jnp.int32),
            pltpu.SMEM(send_block.shape, jnp.int32),
            pltpu.SMEM(send_live.shape, jnp.int32),
            low(w_self.shape),
            low(w_neigh.shape),
            low(local_tiles.shape),
            low(cut_tiles.shape),
            low(feats.shape),
            low((2, *blocks)),
            wide((rows, features)),
            low((rows, features)),
            low((n_grp * row_blocks, block, features)),
            low((6, block, features)),
            low((n_dom, block, features)),
            low(blocks),
            low((row_blocks, block // 2, features)),
            low((row_blocks, block // 2, features)),
            pltpu.SMEM((2, *send_block.shape), jnp.int32),
            pltpu.SMEM((2, *send_block.shape), jnp.int32),
            low((features, features)),
            low((features, features)),
            wide((features, features)),
            low((features, features)),
            low((chips - 1, piece, features)),
            dma((11,)),
            dma((n_grp,)),
            dma((n_grp,)),
            dma((6, 2)),
            dma((n_dom, 2)),
            dma((2, 4)),
            dma((4,)),
            dma((4,)),
            dma,
            dma,
        ]
        + [dma((chips,))] * 6
        + [pltpu.SemaphoreType.REGULAR] * 4,
        compiler_params=pltpu.CompilerParams(
            collective_id=0, has_side_effects=True, vmem_limit_bytes=32 * 2**20
        ),
    )(
        *(
            pltpu.with_memory_space_constraint(x, pltpu.HBM)
            for x in (
                local_cols,
                cut_src,
                send_block,
                send_live,
                feats.reshape(blocks),
                w_self,
                w_neigh,
                local_tiles,
                cut_tiles,
                cotangent,
            )
        )
    )
    return (
        res[:rows],
        res[rows : rows + features].astype(jnp.float32),
        res[rows + features :].astype(jnp.float32),
    )


def solution(mesh):
    n_dom, n_grp = mesh.shape["dom"], mesh.shape["grp"]
    chips = n_dom // CORES * n_grp
    return jax.shard_map(
        lambda *args: (
            body_near
            if n_dom == LINE * CORES and args[1].shape[0] % (PACK * chips) == 0
            else body_wide
        )(*args),
        mesh=mesh,
        in_specs=(
            P(("dom", "grp"), None),
            P(),
            P(),
            P(("dom", "grp"), None, None, None),
            P(("dom", "grp"), None),
            P(("dom", "grp"), None, None, None),
            P(("dom", "grp"), None),
            P(("dom", "grp"), None),
            P(("dom", "grp"), None),
            P(("dom", "grp"), None),
        ),
        out_specs=(P(("dom", "grp"), None), P(), P()),
        check_vma=False,
    )
```

```python
import functools

import jax
import jax.numpy as jnp
from jax import lax
from jax.experimental import pallas as pl
from jax.experimental.pallas import tpu as pltpu
from jax.sharding import PartitionSpec as P

MESH = pl.DeviceIdType.MESH
PACK = 16
FEW = 4
CORES = 2
LINE = 4
OTHERS_FIRST = (3, 1, 2, 0)
ORDERS = (("grp", "dom"), ("dom", "grp"))


def piece_rows(rows, n):
    return rows // n if n > FEW and rows % (PACK * n) == 0 else rows


def f32_dot(a, b):
    return jnp.dot(a, b, preferred_element_type=jnp.float32)


def kernel_wide(
    n_dom,
    n_grp,
    cols_hbm,
    src_hbm,
    block_hbm,
    live_hbm,
    feats_hbm,
    w_self_hbm,
    w_neigh_hbm,
    local_hbm,
    cut_hbm,
    cot_hbm,
    out_ref,
    grad_ref,
    cols_ref,
    src_ref,
    block_ref,
    live_ref,
    w_self_ref,
    w_neigh_ref,
    local_ref,
    cut_ref,
    cot_ref,
    feats_ref,
    near,
    outgoing,
    far,
    acc,
    pre,
    part,
    part_low,
    sums1_a,
    sums1_b,
    mid_a,
    mid_b,
    low_a,
    low_b,
    sums2_a,
    sums2_b,
    load_sem,
    near_send,
    near_recv,
    far_send,
    far_recv,
    s1_send,
    s1_recv,
    s2_send,
    s2_recv,
    s3_send,
    s3_recv,
    s4_send,
    s4_recv,
):
    sums1, mid, mid_low = (sums1_a, sums1_b), (mid_a, mid_b), (low_a, low_b)
    sums2 = (sums2_a, sums2_b)
    row_blocks, local_slots, block, _ = local_ref.shape
    cut_slots = cut_ref.shape[1]
    features = w_self_ref.shape[0]
    width = part.shape[2]
    me_d, me_g = lax.axis_index("dom"), lax.axis_index("grp")
    dom_peer = [lax.rem(me_d + o, n_dom) for o in range(n_dom)]
    grp_peer = [lax.rem(me_g + o, n_grp) for o in range(n_grp)]

    def remote(src, dst, send, recv, o, axis):
        peer = dom_peer[o] if axis == "dom" else grp_peer[o]
        return pltpu.make_async_remote_copy(
            src_ref=src,
            dst_ref=dst,
            send_sem=send,
            recv_sem=recv,
            device_id={axis: peer},
            device_id_type=MESH,
        )

    def begin(copies):
        for copy in copies:
            copy.start()
        return copies

    barrier = pltpu.get_barrier_semaphore()
    for o in range(1, n_dom):
        pl.semaphore_signal(barrier, inc=1, device_id={"dom": dom_peer[o]}, device_id_type=MESH)
    for o in range(1, n_grp):
        pl.semaphore_signal(barrier, inc=1, device_id={"grp": grp_peer[o]}, device_id_type=MESH)
    loads = begin(
        [
            pltpu.make_async_copy(src, dst, load_sem.at[i])
            for i, (src, dst) in enumerate(
                (
                    (block_hbm, block_ref),
                    (live_hbm, live_ref),
                    (feats_hbm, feats_ref),
                    (feats_hbm, near.at[pl.ds(0, row_blocks)]),
                    (cols_hbm, cols_ref),
                    (src_hbm, src_ref),
                    (w_self_hbm, w_self_ref),
                    (local_hbm, local_ref),
                    (cut_hbm, cut_ref),
                    (w_neigh_hbm, w_neigh_ref),
                    (cot_hbm, cot_ref),
                )
            )
        ]
    )
    for load in loads[:3]:
        load.wait()

    for o in range(n_dom):
        alive = live_ref[0, dom_peer[o]].astype(jnp.float32)
        chosen = feats_ref[block_ref[0, dom_peer[o]]].astype(jnp.float32)
        target = far if o == 0 else outgoing
        target[o] = (chosen * alive).astype(jnp.bfloat16)
    pl.semaphore_wait(barrier, n_dom + n_grp - 2)

    far_copies = begin(
        [
            remote(outgoing.at[o], far.at[o], far_send.at[o], far_recv.at[o], o, "dom")
            for o in sorted(range(1, n_dom), key=lambda o: abs(2 * o - n_dom))
        ]
    )
    near_copies = begin(
        [
            remote(
                feats_ref,
                near.at[pl.ds(o * row_blocks, row_blocks)],
                near_send.at[o],
                near_recv.at[o],
                o,
                "grp",
            )
            for o in range(1, n_grp)
        ]
    )

    for load in loads[3:]:
        load.wait()
    for b in range(row_blocks):
        pre[b] = f32_dot(feats_ref[b], w_self_ref[...])
    for copy in near_copies:
        copy.wait_recv()
    for b in range(row_blocks):
        total = jnp.zeros((block, features), jnp.float32)
        for k in range(local_slots):
            col = cols_ref[b, k]
            owner = lax.div(col, row_blocks)
            slot = lax.rem(me_g - owner + n_grp, n_grp)
            where = slot * row_blocks + lax.rem(col, row_blocks)
            total = total + f32_dot(local_ref[b, k], near[where])
        acc[b] = total

    for copy in far_copies:
        copy.wait_recv()
    grads_own = jnp.zeros((features, features), jnp.float32)
    grads_agg = jnp.zeros((features, features), jnp.float32)
    for b in range(row_blocks):
        total = acc[b]
        for k in range(cut_slots):
            slot = lax.rem(n_dom - src_ref[b, k], n_dom)
            total = total + f32_dot(cut_ref[b, k], far[slot])
        agg = total.astype(jnp.bfloat16)
        own = feats_ref[b]
        preact = pre[b] + f32_dot(agg, w_neigh_ref[...])
        sig = jax.nn.sigmoid(preact)
        out_ref[b] = (preact * sig).astype(jnp.bfloat16)
        grad_pre = (
            cot_ref[b].astype(jnp.float32) * sig * (1.0 + preact * (1.0 - sig))
        ).astype(jnp.bfloat16)
        dims = (((0,), (0,)), ((), ()))
        grads_own = grads_own + lax.dot_general(
            own, grad_pre, dims, preferred_element_type=jnp.float32
        )
        grads_agg = grads_agg + lax.dot_general(
            agg, grad_pre, dims, preferred_element_type=jnp.float32
        )

    peers = {"grp": grp_peer, "dom": dom_peer}
    here = {"grp": me_g, "dom": me_d}
    count = {"grp": n_grp, "dom": n_dom}

    def rows_at(start, size):
        return pl.ds(pl.multiple_of(start, size), size)

    def to_peers(axis, src, dst, send, recv):
        return begin(
            [
                remote(src(o), dst(o), send.at[o], recv.at[o], o, axis)
                for o in range(1, count[axis])
            ]
        )

    flows = []
    for h, (one, two) in enumerate(ORDERS):
        rows = 2 * features // count[one]
        piece = piece_rows(rows, count[two])
        split = piece < rows
        flows.append(
            dict(
                one=one,
                two=two,
                rows=rows,
                piece=piece,
                split=split,
                columns=pl.ds(h * width, width),
                mine=rows_at(here[one] * rows, rows),
                inner=rows_at(here[two] * piece, piece) if split else pl.ds(0, rows),
                spot=rows_at(here[one] * rows + (here[two] * piece if split else 0), piece),
                sums1=sums1[h],
                mid=mid[h],
                mid_low=mid_low[h],
                sums2=sums2[h],
            )
        )

    first = []
    for h, f in enumerate(flows):
        cut = slice(h * width, (h + 1) * width)
        part[h, 0:features] = grads_own[:, cut]
        part[h, features : 2 * features] = grads_agg[:, cut]
        part_low[h, 0:features] = grads_own[:, cut].astype(jnp.bfloat16)
        part_low[h, features : 2 * features] = grads_agg[:, cut].astype(jnp.bfloat16)
        first.append(
            to_peers(
                f["one"],
                lambda o: part_low.at[h, rows_at(peers[f["one"]][o] * f["rows"], f["rows"])],
                lambda o: f["sums1"].at[o],
                s1_send.at[h],
                s1_recv.at[h],
            )
        )
    second = []
    for h, f in enumerate(flows):
        total = part[h, f["mine"]]
        for o, copy in enumerate(first[h], 1):
            copy.wait_recv()
            total = total + f["sums1"][o].astype(jnp.float32)
        f["mid"][...] = total
        f["mid_low"][...] = total.astype(jnp.bfloat16)
        second.append(
            to_peers(
                f["two"],
                lambda o: f["mid_low"].at[rows_at(peers[f["two"]][o] * f["piece"], f["piece"])]
                if f["split"]
                else f["mid_low"],
                lambda o: f["sums2"].at[o if f["split"] else here[f["two"]]],
                s2_send.at[h],
                s2_recv.at[h],
            )
        )
    third, fourth = [], []

    def gather(h, f):
        rows_of = grad_ref.at[f["mine"], f["columns"]]
        return to_peers(
            f["one"], lambda o: rows_of, lambda o: rows_of, s4_send.at[h], s4_recv.at[h]
        )

    for h, f in enumerate(flows):
        if f["split"]:
            total = f["mid"][f["inner"]]
            for o, copy in enumerate(second[h], 1):
                copy.wait_recv()
                total = total + f["sums2"][o].astype(jnp.float32)
        else:
            f["sums2"][here[f["two"]]] = f["mid_low"][...]
            for copy in second[h]:
                copy.wait_recv()
            total = f["sums2"][0].astype(jnp.float32)
            for o in range(1, count[f["two"]]):
                total = total + f["sums2"][o].astype(jnp.float32)
        grad_ref[f["spot"], f["columns"]] = total.astype(jnp.bfloat16)
        if f["split"]:
            block_of = grad_ref.at[f["spot"], f["columns"]]
            third.append(
                to_peers(
                    f["two"],
                    lambda o: block_of,
                    lambda o: block_of,
                    s3_send.at[h],
                    s3_recv.at[h],
                )
            )
        else:
            third.append([])
            fourth += gather(h, f)
    for h, f in enumerate(flows):
        if f["split"]:
            for copy in third[h]:
                copy.wait_recv()
            fourth += gather(h, f)
    for copy in fourth:
        copy.wait_recv()

    sent = [far_copies, near_copies, *first, *second, *third, fourth]
    for copy in [copy for group in sent for copy in group]:
        copy.wait_send()


def kernel_near(
    n_dom,
    n_grp,
    cols_hbm,
    src_hbm,
    block_hbm,
    live_hbm,
    feats_hbm,
    w_self_hbm,
    w_neigh_hbm,
    local_hbm,
    cut_hbm,
    cot_hbm,
    out_ref,
    cols_ref,
    src_ref,
    block_ref,
    live_ref,
    w_self_ref,
    w_neigh_ref,
    local_ref,
    cut_ref,
    cot_ref,
    lhs,
    pre,
    grad_pre_ref,
    near,
    outgoing,
    far,
    raw_side,
    raw_mid_a,
    raw_mid_b,
    plan_side,
    plan_mid,
    core_out,
    core_in,
    mine,
    mine_low,
    pieces,
    load_sem,
    near_send,
    near_recv,
    out_send,
    far_recv,
    raw_send,
    side_recv,
    mid_recv,
    core_send,
    core_recv,
    rs_send,
    rs_recv,
    ag_send,
    ag_recv,
    fw_send,
    fw_recv,
    side_ready,
    mid_ready,
    line_ready,
    grp_ready,
):
    row_blocks, local_slots, block, _ = local_ref.shape
    cut_slots = cut_ref.shape[1]
    features = w_self_ref.shape[0]
    rows = row_blocks * block
    n_z = n_dom // CORES
    piece = pieces.shape[1]
    me_d, me_g = lax.axis_index("dom"), lax.axis_index("grp")
    me_z, me_c = lax.div(me_d, CORES), lax.rem(me_d, CORES)
    grp_peer = [lax.rem(me_g + o, n_grp) for o in range(n_grp)]
    place = jnp.where(me_z < n_z // 2, me_z, n_z - 1 - me_z)
    at_end, in_middle = place == 0, place == 1

    def z_of(t):
        return jnp.where(me_z < n_z // 2, t, n_z - 1 - t)

    def dev(t, core):
        return z_of(t) * CORES + core

    side = z_of(1 - place)
    core_peer = me_d + 1 - 2 * me_c
    raw_mids = (raw_mid_a, raw_mid_b)
    halves = [pl.ds(h * (block // 2), block // 2) for h in range(2)]

    def flat(x):
        return x.reshape(rows, features)

    def remote(src, dst, send, recv, device):
        return pltpu.make_async_remote_copy(
            src_ref=src,
            dst_ref=dst,
            send_sem=send,
            recv_sem=recv,
            device_id=device,
            device_id_type=MESH,
        )

    def begin(copies):
        for copy in copies:
            copy.start()
        return copies

    def signal(sem, dom, grp):
        pl.semaphore_signal(sem, inc=1, device_id=(dom, grp), device_id_type=MESH)

    barrier = pltpu.get_barrier_semaphore()
    signal(barrier, core_peer, me_g)

    @pl.when(in_middle)
    def _():
        signal(barrier, dev(2, me_c), me_g)
        for core in range(CORES):
            signal(barrier, dev(0, core), me_g)

    for o in range(1, n_grp):
        signal(barrier, me_d, grp_peer[o])
    loads = begin(
        [
            pltpu.make_async_copy(src, dst, load_sem.at[i])
            for i, (src, dst) in enumerate(
                (
                    (block_hbm, block_ref),
                    (live_hbm, live_ref),
                    (feats_hbm, lhs.at[0]),
                    (feats_hbm, near.at[pl.ds(me_g * row_blocks, row_blocks)]),
                    (cols_hbm, cols_ref),
                    (src_hbm, src_ref),
                    (w_self_hbm, w_self_ref),
                    (local_hbm, local_ref),
                    (cut_hbm, cut_ref),
                    (w_neigh_hbm, w_neigh_ref),
                    (cot_hbm, cot_ref),
                )
            )
        ]
    )

    def plan_copies(target, plan, send, recv):
        device = (target, me_g)
        return [
            remote(block_hbm, plan.at[0], send.at[0], recv.at[0], device),
            remote(live_hbm, plan.at[1], send.at[1], recv.at[1], device),
        ]

    side_d = side * CORES + me_c
    side_copies = plan_copies(side_d, plan_side, raw_send.at[0], side_recv)
    side_copies.append(
        remote(feats_hbm, raw_side, raw_send.at[0, 2], side_recv.at[2], (side_d, me_g))
    )
    mid_copies = plan_copies(dev(2, me_c), plan_mid, raw_send.at[1], mid_recv)
    mid_copies += [
        remote(
            feats_hbm.at[:, part],
            raw_mids[h],
            raw_send.at[1, 2 + h],
            mid_recv.at[2 + h],
            (dev(2, me_c), me_g),
        )
        for h, part in enumerate(halves)
    ]
    pl.semaphore_wait(barrier, CORES + 1 - place + n_grp - 1)

    @pl.when(in_middle)
    def _():
        begin(mid_copies)

    @pl.when(at_end)
    def _():
        for core in range(CORES):
            signal(side_ready, dev(1, core), me_g)
        begin(side_copies)

    near_copies = begin(
        [
            remote(
                feats_hbm,
                near.at[pl.ds(me_g * row_blocks, row_blocks)],
                near_send.at[o],
                near_recv.at[o],
                (me_d, grp_peer[o]),
            )
            for o in range(1, n_grp)
        ]
    )

    @pl.when(in_middle)
    def _():
        pl.semaphore_wait(side_ready, CORES)
        begin(side_copies)
        signal(mid_ready, dev(2, me_c), me_g)
        pl.semaphore_wait(mid_ready, 1)
        for core in range(CORES):
            signal(line_ready, dev(0, core), me_g)

    def chosen(blocks_of, block_at, alive):
        picked = blocks_of(block_at).astype(jnp.float32)
        return (picked * alive.astype(jnp.float32)).astype(jnp.bfloat16)

    def of_own(target):
        return chosen(lambda i: lhs[0, i], block_ref[0, target], live_ref[0, target])

    def of_side(target):
        return chosen(lambda i: raw_side[i], plan_side[0, 0, target], plan_side[1, 0, target])

    def of_mid(target, part):
        return chosen(
            lambda i: raw_mids[part][i], plan_mid[0, 0, target], plan_mid[1, 0, target]
        )

    def send_block(i, source, target):
        return remote(
            outgoing.at[i],
            far.at[source],
            out_send.at[i, 0],
            far_recv.at[source, 0],
            (target, me_g),
        )

    def send_half(i, source, target, h):
        return remote(
            outgoing.at[i, halves[h]],
            far.at[source, halves[h]],
            out_send.at[i, h],
            far_recv.at[source, h],
            (target, me_g),
        )

    for load in loads[:4]:
        load.wait()
    end_jobs = [(dev(t, core)) for t in (3, 2) for core in range(CORES)]

    @pl.when(at_end)
    def _():
        for i, target in enumerate(end_jobs):
            outgoing[2 + i] = of_own(target)
        pl.semaphore_wait(line_ready, CORES)
        for i, target in enumerate(end_jobs):
            send_block(2 + i, me_d, target).start()

    for o in range(1, n_grp):
        signal(grp_ready, me_d, grp_peer[o])
    outgoing[0] = of_own(core_peer)
    send_block(0, me_d, core_peer).start()
    far[me_d] = of_own(me_d)

    for load in loads[4:]:
        load.wait()
    pre[...] = f32_dot(flat(lhs[0]), w_self_ref[...])

    mid_d = dev(2, me_c)
    mid_jobs = [dev(0, 0), dev(0, 1), core_peer]

    @pl.when(in_middle)
    def _():
        for copy in mid_copies[:2]:
            copy.wait_recv()
        for h, part in enumerate(halves):
            mid_copies[2 + h].wait_recv()
            for i, target in enumerate(mid_jobs):
                outgoing[2 + i, part] = of_mid(target, h)
                send_half(2 + i, mid_d, target, h).start()
            far[mid_d, part] = of_mid(me_d, h)

    for copy in side_copies:
        copy.wait_recv()
    outgoing[1] = of_side(core_peer)
    send_block(1, side_d, core_peer).start()
    far[side_d] = of_side(me_d)

    for copy in near_copies:
        copy.wait_recv()
    acc = []
    for b in range(row_blocks):
        total = jnp.zeros((block, features), jnp.float32)
        for k in range(local_slots):
            total = total + f32_dot(local_ref[b, k], near[cols_ref[b, k]])
        acc.append(total)

    def arrived(source):
        send_block(0, source, core_peer).wait_recv()

    def arrived_halves(source):
        for h in range(2):
            send_half(0, source, core_peer, h).wait_recv()

    arrived(core_peer)
    arrived(side * CORES + 1 - me_c)

    @pl.when(in_middle)
    def _():
        arrived_halves(dev(2, 1 - me_c))
        for core in range(CORES):
            arrived(dev(3, core))

    @pl.when(at_end)
    def _():
        for core in range(CORES):
            arrived_halves(dev(2, core))
            arrived(dev(3, core))

    for b in range(row_blocks):
        here = pl.ds(b * block, block)
        total = acc[b]
        for k in range(cut_slots):
            total = total + f32_dot(cut_ref[b, k], far[lax.rem(me_d + src_ref[b, k], n_dom)])
        agg = total.astype(jnp.bfloat16)
        lhs[1, b] = agg
        preact = pre[here] + f32_dot(agg, w_neigh_ref[...])
        sig = jax.nn.sigmoid(preact)
        out_ref[here] = (preact * sig).astype(jnp.bfloat16)
        grad_pre_ref[here] = (
            cot_ref[here].astype(jnp.float32) * sig * (1.0 + preact * (1.0 - sig))
        ).astype(jnp.bfloat16)

    def product(which):
        return lax.dot_general(
            flat(lhs[which]),
            grad_pre_ref[...],
            (((0,), (0,)), ((), ())),
            preferred_element_type=jnp.float32,
        )

    core_out[...] = product(1 - me_c).astype(jnp.bfloat16)
    core_copy = remote(core_out, core_in, core_send, core_recv, (core_peer, me_g))
    core_copy.start()
    mine[...] = product(me_c)
    pl.semaphore_wait(grp_ready, n_grp - 1)
    core_copy.wait_recv()
    total = mine[...] + core_in[...].astype(jnp.float32)
    mine[...] = total
    mine_low[...] = total.astype(jnp.bfloat16)

    def owner_rows(t, g):
        return pl.multiple_of(((z_of(t) - 1) * n_grp + g) * piece, piece)

    def give(t, o):
        back = (n_grp - o) % n_grp
        slot = n_grp * place + back if t == 2 else 2 * n_grp + (n_grp - 1) * place + back
        g = grp_peer[o]
        return remote(
            mine_low.at[pl.ds(owner_rows(t, g), piece)],
            pieces.at[slot],
            rs_send,
            rs_recv,
            (dev(t, me_c), g),
        )

    def spot(t, g):
        start = rows + me_c * features + owner_rows(t, g)
        return out_ref.at[pl.ds(pl.multiple_of(start, piece), piece)]

    def share(t, o):
        own = spot(1, me_g)
        return remote(
            own, own, ag_send, ag_recv.at[me_z - 1], (dev(t, me_c), grp_peer[o])
        )

    plane = n_grp * piece

    def forward(q, core):
        start = rows + core * features + q * plane
        part = out_ref.at[pl.ds(pl.multiple_of(start, plane), plane)]
        return remote(part, part, fw_send.at[q], fw_recv.at[q], (core_peer, me_g))

    def all_of(ref, send, recv):
        return remote(ref, ref, send, recv, (core_peer, me_g))

    for o in OTHERS_FIRST:
        give(2, o).start()
    for o in OTHERS_FIRST[:-1]:
        give(1, o).start()

    @pl.when(at_end)
    def _():
        give(1, 0).start()

    for copy in [*near_copies, *side_copies, core_copy]:
        copy.wait_send()
    for i in range(2):
        send_block(i, me_d, core_peer).wait_send()

    @pl.when(in_middle)
    def _():
        for copy in mid_copies:
            copy.wait_send()
        for i, target in enumerate(mid_jobs):
            for h in range(2):
                send_half(2 + i, mid_d, target, h).wait_send()

    @pl.when(at_end)
    def _():
        for i, target in enumerate(end_jobs):
            send_block(2 + i, me_d, target).wait_send()

    others = [(t, o) for t in (3, 2, 0) for o in OTHERS_FIRST]
    others += [(1, o) for o in OTHERS_FIRST[:-1]]

    @pl.when(in_middle)
    def _():
        all_of(pieces, rs_send, rs_recv).wait_recv()
        total = mine[pl.ds(owner_rows(1, me_g), piece)]
        for i in range(len(others)):
            total = total + pieces[i].astype(jnp.float32)
        spot(1, me_g)[...] = total.astype(jnp.bfloat16)
        for t, o in others:
            share(t, o).start()
        most = pl.ds(rows + me_c * features, plane - piece)
        all_of(out_ref.at[most], ag_send, ag_recv.at[me_z - 1]).wait_recv()
        forward(me_z - 1, me_c).start()
        forward_q = z_of(2) - 1
        start = rows + me_c * features + forward_q * plane
        part = out_ref.at[pl.ds(pl.multiple_of(start, plane), plane)]
        all_of(part, ag_send, ag_recv.at[forward_q]).wait_recv()
        forward(forward_q, me_c).start()
        all_of(mine_low.at[pl.ds(0, features - piece)], rs_send, rs_recv).wait_send()
        all_of(out_ref.at[pl.ds(0, len(others) * piece)], ag_send, rs_recv).wait_send()

    @pl.when(at_end)
    def _():
        for t in (1, 2):
            q = z_of(t) - 1
            start = rows + me_c * features + q * plane
            part = out_ref.at[pl.ds(pl.multiple_of(start, plane), plane)]
            all_of(part, ag_send, ag_recv.at[q]).wait_recv()
            forward(q, me_c).start()
        all_of(mine_low, rs_send, rs_recv).wait_send()

    for q in range(2):
        forward(q, 1 - me_c).wait_recv()
    for q in range(2):
        forward(q, me_c).wait_send()


def body_wide(
    feats,
    w_self,
    w_neigh,
    local_tiles,
    local_cols,
    cut_tiles,
    cut_src,
    send_block,
    send_live,
    cotangent,
):
    row_blocks, _, block, _ = local_tiles.shape
    features = feats.shape[1]
    n_dom, n_grp = lax.axis_size("dom"), lax.axis_size("grp")
    blocks = (row_blocks, block, features)
    halves = len(ORDERS)
    count = {"grp": n_grp, "dom": n_dom}
    most = max(n_grp, n_dom)
    sizes = []
    for one, two in ORDERS:
        rows = 2 * features // count[one]
        sizes.append((count[one], rows, count[two], piece_rows(rows, count[two])))
    width = features // halves
    dma = pltpu.SemaphoreType.DMA
    hbm = pl.BlockSpec(memory_space=pltpu.HBM)
    vmem = pl.BlockSpec(memory_space=pltpu.VMEM)
    out, grads = pl.pallas_call(
        functools.partial(kernel_wide, n_dom, n_grp),
        out_shape=(
            jax.ShapeDtypeStruct(blocks, jnp.bfloat16),
            jax.ShapeDtypeStruct((2 * features, features), jnp.bfloat16),
        ),
        in_specs=[hbm] * 10,
        out_specs=(vmem, vmem),
        scratch_shapes=[
            pltpu.SMEM(local_cols.shape, jnp.int32),
            pltpu.SMEM(cut_src.shape, jnp.int32),
            pltpu.SMEM(send_block.shape, jnp.int32),
            pltpu.SMEM(send_live.shape, jnp.int32),
            pltpu.VMEM(w_self.shape, jnp.bfloat16),
            pltpu.VMEM(w_neigh.shape, jnp.bfloat16),
            pltpu.VMEM(local_tiles.shape, jnp.bfloat16),
            pltpu.VMEM(cut_tiles.shape, jnp.bfloat16),
            pltpu.VMEM(blocks, jnp.bfloat16),
            pltpu.VMEM(blocks, jnp.bfloat16),
            pltpu.VMEM((n_grp * row_blocks, block, features), jnp.bfloat16),
            pltpu.VMEM((n_dom, block, features), jnp.bfloat16),
            pltpu.VMEM((n_dom, block, features), jnp.bfloat16),
            pltpu.VMEM(blocks, jnp.float32),
            pltpu.VMEM(blocks, jnp.float32),
            pltpu.VMEM((halves, 2 * features, width), jnp.float32),
            pltpu.VMEM((halves, 2 * features, width), jnp.bfloat16),
        ]
        + [pltpu.VMEM((n, r, width), jnp.bfloat16) for n, r, _, _ in sizes]
        + [pltpu.VMEM((r, width), jnp.float32) for _, r, _, _ in sizes]
        + [pltpu.VMEM((r, width), jnp.bfloat16) for _, r, _, _ in sizes]
        + [pltpu.VMEM((n, p, width), jnp.bfloat16) for _, _, n, p in sizes]
        + [
            dma((11,)),
        ]
        + [dma((n_grp,))] * 2
        + [dma((n_dom,))] * 2
        + [dma((halves, most))] * 8,
        compiler_params=pltpu.CompilerParams(
            collective_id=0, has_side_effects=True, vmem_limit_bytes=32 * 2**20
        ),
    )(
        *(
            pltpu.with_memory_space_constraint(x, pltpu.HBM)
            for x in (
                local_cols,
                cut_src,
                send_block,
                send_live,
                feats.reshape(blocks),
                w_self,
                w_neigh,
                local_tiles,
                cut_tiles,
                cotangent.reshape(blocks),
            )
        )
    )
    summed = grads.astype(jnp.float32)
    return (out.reshape(feats.shape), summed[:features], summed[features:])


def body_near(
    feats,
    w_self,
    w_neigh,
    local_tiles,
    local_cols,
    cut_tiles,
    cut_src,
    send_block,
    send_live,
    cotangent,
):
    row_blocks, _, block, _ = local_tiles.shape
    rows, features = feats.shape
    blocks = (row_blocks, block, features)
    n_dom, n_grp = lax.axis_size("dom"), lax.axis_size("grp")
    chips = n_dom // CORES * n_grp
    piece = 2 * features // chips
    dma = pltpu.SemaphoreType.DMA
    hbm = pl.BlockSpec(memory_space=pltpu.HBM)
    vmem = pl.BlockSpec(memory_space=pltpu.VMEM)
    low = functools.partial(pltpu.VMEM, dtype=jnp.bfloat16)
    wide = functools.partial(pltpu.VMEM, dtype=jnp.float32)
    res = pl.pallas_call(
        functools.partial(kernel_near, n_dom, n_grp),
        out_shape=jax.ShapeDtypeStruct((rows + 2 * features, features), jnp.bfloat16),
        in_specs=[hbm] * 10,
        out_specs=vmem,
        scratch_shapes=[
            pltpu.SMEM(local_cols.shape, jnp.int32),
            pltpu.SMEM(cut_src.shape, jnp.int32),
            pltpu.SMEM(send_block.shape, jnp.int32),
            pltpu.SMEM(send_live.shape, jnp.int32),
            low(w_self.shape),
            low(w_neigh.shape),
            low(local_tiles.shape),
            low(cut_tiles.shape),
            low(feats.shape),
            low((2, *blocks)),
            wide((rows, features)),
            low((rows, features)),
            low((n_grp * row_blocks, block, features)),
            low((6, block, features)),
            low((n_dom, block, features)),
            low(blocks),
            low((row_blocks, block // 2, features)),
            low((row_blocks, block // 2, features)),
            pltpu.SMEM((2, *send_block.shape), jnp.int32),
            pltpu.SMEM((2, *send_block.shape), jnp.int32),
            low((features, features)),
            low((features, features)),
            wide((features, features)),
            low((features, features)),
            low((chips - 1, piece, features)),
            dma((11,)),
            dma((n_grp,)),
            dma((n_grp,)),
            dma((6, 2)),
            dma((n_dom, 2)),
            dma((2, 4)),
            dma((4,)),
            dma((4,)),
            dma,
            dma,
        ]
        + [dma] * 3
        + [dma((2,))] * 3
        + [pltpu.SemaphoreType.REGULAR] * 4,
        compiler_params=pltpu.CompilerParams(
            collective_id=0, has_side_effects=True, vmem_limit_bytes=32 * 2**20
        ),
    )(
        *(
            pltpu.with_memory_space_constraint(x, pltpu.HBM)
            for x in (
                local_cols,
                cut_src,
                send_block,
                send_live,
                feats.reshape(blocks),
                w_self,
                w_neigh,
                local_tiles,
                cut_tiles,
                cotangent,
            )
        )
    )
    return (
        res[:rows],
        res[rows : rows + features].astype(jnp.float32),
        res[rows + features :].astype(jnp.float32),
    )


def solution(mesh):
    n_dom, n_grp = mesh.shape["dom"], mesh.shape["grp"]
    chips = n_dom // CORES * n_grp
    return jax.shard_map(
        lambda *args: (
            body_near
            if (n_dom, n_grp) == (LINE * CORES, len(OTHERS_FIRST))
            and 2 * args[1].shape[0] % (PACK * chips) == 0
            else body_wide
        )(*args),
        mesh=mesh,
        in_specs=(
            P(("dom", "grp"), None),
            P(),
            P(),
            P(("dom", "grp"), None, None, None),
            P(("dom", "grp"), None),
            P(("dom", "grp"), None, None, None),
            P(("dom", "grp"), None),
            P(("dom", "grp"), None),
            P(("dom", "grp"), None),
            P(("dom", "grp"), None),
        ),
        out_specs=(P(("dom", "grp"), None), P(), P()),
        check_vma=False,
    )
```

```python
import functools

import jax
import jax.numpy as jnp
from jax import lax
from jax.experimental import pallas as pl
from jax.experimental.pallas import tpu as pltpu
from jax.sharding import PartitionSpec as P

MESH = pl.DeviceIdType.MESH
PACK = 16
FEW = 4
CORES = 2
LINE = 4
OTHERS_FIRST = (3, 1, 2, 0)
ORDERS = (("grp", "dom"), ("dom", "grp"))


def piece_rows(rows, n):
    return rows // n if n > FEW and rows % (PACK * n) == 0 else rows


def f32_dot(a, b):
    return jnp.dot(a, b, preferred_element_type=jnp.float32)


def kernel_wide(
    n_dom,
    n_grp,
    cols_hbm,
    src_hbm,
    block_hbm,
    live_hbm,
    feats_hbm,
    w_self_hbm,
    w_neigh_hbm,
    local_hbm,
    cut_hbm,
    cot_hbm,
    out_ref,
    grad_ref,
    cols_ref,
    src_ref,
    block_ref,
    live_ref,
    w_self_ref,
    w_neigh_ref,
    local_ref,
    cut_ref,
    cot_ref,
    feats_ref,
    near,
    outgoing,
    far,
    acc,
    pre,
    part,
    part_low,
    sums1_a,
    sums1_b,
    mid_a,
    mid_b,
    low_a,
    low_b,
    sums2_a,
    sums2_b,
    load_sem,
    near_send,
    near_recv,
    far_send,
    far_recv,
    s1_send,
    s1_recv,
    s2_send,
    s2_recv,
    s3_send,
    s3_recv,
    s4_send,
    s4_recv,
):
    sums1, mid, mid_low = (sums1_a, sums1_b), (mid_a, mid_b), (low_a, low_b)
    sums2 = (sums2_a, sums2_b)
    row_blocks, local_slots, block, _ = local_ref.shape
    cut_slots = cut_ref.shape[1]
    features = w_self_ref.shape[0]
    width = part.shape[2]
    me_d, me_g = lax.axis_index("dom"), lax.axis_index("grp")
    dom_peer = [lax.rem(me_d + o, n_dom) for o in range(n_dom)]
    grp_peer = [lax.rem(me_g + o, n_grp) for o in range(n_grp)]

    def remote(src, dst, send, recv, o, axis):
        peer = dom_peer[o] if axis == "dom" else grp_peer[o]
        return pltpu.make_async_remote_copy(
            src_ref=src,
            dst_ref=dst,
            send_sem=send,
            recv_sem=recv,
            device_id={axis: peer},
            device_id_type=MESH,
        )

    def begin(copies):
        for copy in copies:
            copy.start()
        return copies

    barrier = pltpu.get_barrier_semaphore()
    for o in range(1, n_dom):
        pl.semaphore_signal(barrier, inc=1, device_id={"dom": dom_peer[o]}, device_id_type=MESH)
    for o in range(1, n_grp):
        pl.semaphore_signal(barrier, inc=1, device_id={"grp": grp_peer[o]}, device_id_type=MESH)
    loads = begin(
        [
            pltpu.make_async_copy(src, dst, load_sem.at[i])
            for i, (src, dst) in enumerate(
                (
                    (block_hbm, block_ref),
                    (live_hbm, live_ref),
                    (feats_hbm, feats_ref),
                    (feats_hbm, near.at[pl.ds(0, row_blocks)]),
                    (cols_hbm, cols_ref),
                    (src_hbm, src_ref),
                    (w_self_hbm, w_self_ref),
                    (local_hbm, local_ref),
                    (cut_hbm, cut_ref),
                    (w_neigh_hbm, w_neigh_ref),
                    (cot_hbm, cot_ref),
                )
            )
        ]
    )
    for load in loads[:3]:
        load.wait()

    for o in range(n_dom):
        alive = live_ref[0, dom_peer[o]].astype(jnp.float32)
        chosen = feats_ref[block_ref[0, dom_peer[o]]].astype(jnp.float32)
        target = far if o == 0 else outgoing
        target[o] = (chosen * alive).astype(jnp.bfloat16)
    pl.semaphore_wait(barrier, n_dom + n_grp - 2)

    far_copies = begin(
        [
            remote(outgoing.at[o], far.at[o], far_send.at[o], far_recv.at[o], o, "dom")
            for o in sorted(range(1, n_dom), key=lambda o: abs(2 * o - n_dom))
        ]
    )
    near_copies = begin(
        [
            remote(
                feats_ref,
                near.at[pl.ds(o * row_blocks, row_blocks)],
                near_send.at[o],
                near_recv.at[o],
                o,
                "grp",
            )
            for o in range(1, n_grp)
        ]
    )

    for load in loads[3:]:
        load.wait()
    for b in range(row_blocks):
        pre[b] = f32_dot(feats_ref[b], w_self_ref[...])
    for copy in near_copies:
        copy.wait_recv()
    for b in range(row_blocks):
        total = jnp.zeros((block, features), jnp.float32)
        for k in range(local_slots):
            col = cols_ref[b, k]
            owner = lax.div(col, row_blocks)
            slot = lax.rem(me_g - owner + n_grp, n_grp)
            where = slot * row_blocks + lax.rem(col, row_blocks)
            total = total + f32_dot(local_ref[b, k], near[where])
        acc[b] = total

    for copy in far_copies:
        copy.wait_recv()
    grads_own = jnp.zeros((features, features), jnp.float32)
    grads_agg = jnp.zeros((features, features), jnp.float32)
    for b in range(row_blocks):
        total = acc[b]
        for k in range(cut_slots):
            slot = lax.rem(n_dom - src_ref[b, k], n_dom)
            total = total + f32_dot(cut_ref[b, k], far[slot])
        agg = total.astype(jnp.bfloat16)
        own = feats_ref[b]
        preact = pre[b] + f32_dot(agg, w_neigh_ref[...])
        sig = jax.nn.sigmoid(preact)
        out_ref[b] = (preact * sig).astype(jnp.bfloat16)
        grad_pre = (
            cot_ref[b].astype(jnp.float32) * sig * (1.0 + preact * (1.0 - sig))
        ).astype(jnp.bfloat16)
        dims = (((0,), (0,)), ((), ()))
        grads_own = grads_own + lax.dot_general(
            own, grad_pre, dims, preferred_element_type=jnp.float32
        )
        grads_agg = grads_agg + lax.dot_general(
            agg, grad_pre, dims, preferred_element_type=jnp.float32
        )

    peers = {"grp": grp_peer, "dom": dom_peer}
    here = {"grp": me_g, "dom": me_d}
    count = {"grp": n_grp, "dom": n_dom}

    def rows_at(start, size):
        return pl.ds(pl.multiple_of(start, size), size)

    def to_peers(axis, src, dst, send, recv):
        return begin(
            [
                remote(src(o), dst(o), send.at[o], recv.at[o], o, axis)
                for o in range(1, count[axis])
            ]
        )

    flows = []
    for h, (one, two) in enumerate(ORDERS):
        rows = 2 * features // count[one]
        piece = piece_rows(rows, count[two])
        split = piece < rows
        flows.append(
            dict(
                one=one,
                two=two,
                rows=rows,
                piece=piece,
                split=split,
                columns=pl.ds(h * width, width),
                mine=rows_at(here[one] * rows, rows),
                inner=rows_at(here[two] * piece, piece) if split else pl.ds(0, rows),
                spot=rows_at(here[one] * rows + (here[two] * piece if split else 0), piece),
                sums1=sums1[h],
                mid=mid[h],
                mid_low=mid_low[h],
                sums2=sums2[h],
            )
        )

    first = []
    for h, f in enumerate(flows):
        cut = slice(h * width, (h + 1) * width)
        part[h, 0:features] = grads_own[:, cut]
        part[h, features : 2 * features] = grads_agg[:, cut]
        part_low[h, 0:features] = grads_own[:, cut].astype(jnp.bfloat16)
        part_low[h, features : 2 * features] = grads_agg[:, cut].astype(jnp.bfloat16)
        first.append(
            to_peers(
                f["one"],
                lambda o: part_low.at[h, rows_at(peers[f["one"]][o] * f["rows"], f["rows"])],
                lambda o: f["sums1"].at[o],
                s1_send.at[h],
                s1_recv.at[h],
            )
        )
    second = []
    for h, f in enumerate(flows):
        total = part[h, f["mine"]]
        for o, copy in enumerate(first[h], 1):
            copy.wait_recv()
            total = total + f["sums1"][o].astype(jnp.float32)
        f["mid"][...] = total
        f["mid_low"][...] = total.astype(jnp.bfloat16)
        second.append(
            to_peers(
                f["two"],
                lambda o: f["mid_low"].at[rows_at(peers[f["two"]][o] * f["piece"], f["piece"])]
                if f["split"]
                else f["mid_low"],
                lambda o: f["sums2"].at[o if f["split"] else here[f["two"]]],
                s2_send.at[h],
                s2_recv.at[h],
            )
        )
    third, fourth = [], []

    def gather(h, f):
        rows_of = grad_ref.at[f["mine"], f["columns"]]
        return to_peers(
            f["one"], lambda o: rows_of, lambda o: rows_of, s4_send.at[h], s4_recv.at[h]
        )

    for h, f in enumerate(flows):
        if f["split"]:
            total = f["mid"][f["inner"]]
            for o, copy in enumerate(second[h], 1):
                copy.wait_recv()
                total = total + f["sums2"][o].astype(jnp.float32)
        else:
            f["sums2"][here[f["two"]]] = f["mid_low"][...]
            for copy in second[h]:
                copy.wait_recv()
            total = f["sums2"][0].astype(jnp.float32)
            for o in range(1, count[f["two"]]):
                total = total + f["sums2"][o].astype(jnp.float32)
        grad_ref[f["spot"], f["columns"]] = total.astype(jnp.bfloat16)
        if f["split"]:
            block_of = grad_ref.at[f["spot"], f["columns"]]
            third.append(
                to_peers(
                    f["two"],
                    lambda o: block_of,
                    lambda o: block_of,
                    s3_send.at[h],
                    s3_recv.at[h],
                )
            )
        else:
            third.append([])
            fourth += gather(h, f)
    for h, f in enumerate(flows):
        if f["split"]:
            for copy in third[h]:
                copy.wait_recv()
            fourth += gather(h, f)
    for copy in fourth:
        copy.wait_recv()

    sent = [far_copies, near_copies, *first, *second, *third, fourth]
    for copy in [copy for group in sent for copy in group]:
        copy.wait_send()


def kernel_near(
    n_dom,
    n_grp,
    cols_hbm,
    src_hbm,
    block_hbm,
    live_hbm,
    feats_hbm,
    w_self_hbm,
    w_neigh_hbm,
    local_hbm,
    cut_hbm,
    cot_hbm,
    out_ref,
    cols_ref,
    src_ref,
    block_ref,
    live_ref,
    w_self_ref,
    w_neigh_ref,
    local_ref,
    cut_ref,
    cot_ref,
    lhs,
    pre,
    grad_pre_ref,
    near,
    outgoing,
    far,
    raw_side,
    raw_mid_a,
    raw_mid_b,
    plan_side,
    plan_mid,
    core_out,
    core_in,
    mine,
    mine_low,
    pieces,
    load_sem,
    near_send,
    near_recv,
    out_send,
    far_recv,
    raw_send,
    side_recv,
    mid_recv,
    core_send,
    core_recv,
    rs_send,
    rs_recv,
    ag_send,
    ag_recv,
    fw_send,
    fw_recv,
    side_ready,
    mid_ready,
    line_ready,
    grp_ready,
):
    row_blocks, local_slots, block, _ = local_ref.shape
    cut_slots = cut_ref.shape[1]
    features = w_self_ref.shape[0]
    rows = row_blocks * block
    n_z = n_dom // CORES
    piece = pieces.shape[1]
    me_d, me_g = lax.axis_index("dom"), lax.axis_index("grp")
    me_z, me_c = lax.div(me_d, CORES), lax.rem(me_d, CORES)
    grp_peer = [lax.rem(me_g + o, n_grp) for o in range(n_grp)]
    place = jnp.where(me_z < n_z // 2, me_z, n_z - 1 - me_z)
    at_end, in_middle = place == 0, place == 1

    def z_of(t):
        return jnp.where(me_z < n_z // 2, t, n_z - 1 - t)

    def dev(t, core):
        return z_of(t) * CORES + core

    side = z_of(1 - place)
    core_peer = me_d + 1 - 2 * me_c
    raw_mids = (raw_mid_a, raw_mid_b)
    halves = [pl.ds(h * (block // 2), block // 2) for h in range(2)]

    def flat(x):
        return x.reshape(rows, features)

    def remote(src, dst, send, recv, device):
        return pltpu.make_async_remote_copy(
            src_ref=src,
            dst_ref=dst,
            send_sem=send,
            recv_sem=recv,
            device_id=device,
            device_id_type=MESH,
        )

    def begin(copies):
        for copy in copies:
            copy.start()
        return copies

    def signal(sem, dom, grp):
        pl.semaphore_signal(sem, inc=1, device_id=(dom, grp), device_id_type=MESH)

    barrier = pltpu.get_barrier_semaphore()
    signal(barrier, core_peer, me_g)

    @pl.when(in_middle)
    def _():
        signal(barrier, dev(2, me_c), me_g)
        for core in range(CORES):
            signal(barrier, dev(0, core), me_g)

    for o in range(1, n_grp):
        signal(barrier, me_d, grp_peer[o])
    loads = begin(
        [
            pltpu.make_async_copy(src, dst, load_sem.at[i])
            for i, (src, dst) in enumerate(
                (
                    (block_hbm, block_ref),
                    (live_hbm, live_ref),
                    (feats_hbm, lhs.at[0]),
                    (feats_hbm, near.at[pl.ds(me_g * row_blocks, row_blocks)]),
                    (cols_hbm, cols_ref),
                    (src_hbm, src_ref),
                    (w_self_hbm, w_self_ref),
                    (local_hbm, local_ref),
                    (cut_hbm, cut_ref),
                    (w_neigh_hbm, w_neigh_ref),
                    (cot_hbm, cot_ref),
                )
            )
        ]
    )

    def plan_copies(target, plan, send, recv):
        device = (target, me_g)
        return [
            remote(block_hbm, plan.at[0], send.at[0], recv.at[0], device),
            remote(live_hbm, plan.at[1], send.at[1], recv.at[1], device),
        ]

    side_d = side * CORES + me_c
    side_copies = plan_copies(side_d, plan_side, raw_send.at[0], side_recv)
    side_copies.append(
        remote(feats_hbm, raw_side, raw_send.at[0, 2], side_recv.at[2], (side_d, me_g))
    )
    mid_copies = plan_copies(dev(2, me_c), plan_mid, raw_send.at[1], mid_recv)
    mid_copies += [
        remote(
            feats_hbm.at[:, part],
            raw_mids[h],
            raw_send.at[1, 2 + h],
            mid_recv.at[2 + h],
            (dev(2, me_c), me_g),
        )
        for h, part in enumerate(halves)
    ]
    pl.semaphore_wait(barrier, CORES + 1 - place + n_grp - 1)

    @pl.when(in_middle)
    def _():
        begin(mid_copies)

    @pl.when(at_end)
    def _():
        for core in range(CORES):
            signal(side_ready, dev(1, core), me_g)
        begin(side_copies)

    near_copies = begin(
        [
            remote(
                feats_hbm,
                near.at[pl.ds(me_g * row_blocks, row_blocks)],
                near_send.at[o],
                near_recv.at[o],
                (me_d, grp_peer[o]),
            )
            for o in range(1, n_grp)
        ]
    )

    @pl.when(in_middle)
    def _():
        pl.semaphore_wait(side_ready, CORES)
        begin(side_copies)
        signal(mid_ready, dev(2, me_c), me_g)
        pl.semaphore_wait(mid_ready, 1)
        for core in range(CORES):
            signal(line_ready, dev(0, core), me_g)

    def chosen(blocks_of, block_at, alive):
        picked = blocks_of(block_at).astype(jnp.float32)
        return (picked * alive.astype(jnp.float32)).astype(jnp.bfloat16)

    def of_own(target):
        return chosen(lambda i: lhs[0, i], block_ref[0, target], live_ref[0, target])

    def of_side(target):
        return chosen(lambda i: raw_side[i], plan_side[0, 0, target], plan_side[1, 0, target])

    def of_mid(target, part):
        return chosen(
            lambda i: raw_mids[part][i], plan_mid[0, 0, target], plan_mid[1, 0, target]
        )

    def send_block(i, source, target):
        return remote(
            outgoing.at[i],
            far.at[source],
            out_send.at[i, 0],
            far_recv.at[source, 0],
            (target, me_g),
        )

    def send_half(i, source, target, h):
        return remote(
            outgoing.at[i, halves[h]],
            far.at[source, halves[h]],
            out_send.at[i, h],
            far_recv.at[source, h],
            (target, me_g),
        )

    for load in loads[:4]:
        load.wait()
    end_jobs = [(dev(t, core)) for t in (3, 2) for core in range(CORES)]

    @pl.when(at_end)
    def _():
        for i, target in enumerate(end_jobs):
            outgoing[2 + i] = of_own(target)
        pl.semaphore_wait(line_ready, CORES)
        for i, target in enumerate(end_jobs):
            send_block(2 + i, me_d, target).start()

    for o in range(1, n_grp):
        signal(grp_ready, me_d, grp_peer[o])
    outgoing[0] = of_own(core_peer)
    send_block(0, me_d, core_peer).start()
    far[me_d] = of_own(me_d)

    for load in loads[4:]:
        load.wait()
    pre[...] = f32_dot(flat(lhs[0]), w_self_ref[...])

    mid_d = dev(2, me_c)
    mid_jobs = [dev(0, 0), dev(0, 1), core_peer]

    @pl.when(in_middle)
    def _():
        for copy in mid_copies[:2]:
            copy.wait_recv()
        for h, part in enumerate(halves):
            mid_copies[2 + h].wait_recv()
            for i, target in enumerate(mid_jobs):
                outgoing[2 + i, part] = of_mid(target, h)
                send_half(2 + i, mid_d, target, h).start()
            far[mid_d, part] = of_mid(me_d, h)

    for copy in side_copies:
        copy.wait_recv()
    outgoing[1] = of_side(core_peer)
    send_block(1, side_d, core_peer).start()
    far[side_d] = of_side(me_d)

    for copy in near_copies:
        copy.wait_recv()
    acc = []
    for b in range(row_blocks):
        total = jnp.zeros((block, features), jnp.float32)
        for k in range(local_slots):
            total = total + f32_dot(local_ref[b, k], near[cols_ref[b, k]])
        acc.append(total)

    def arrived(source):
        send_block(0, source, core_peer).wait_recv()

    def arrived_halves(source):
        for h in range(2):
            send_half(0, source, core_peer, h).wait_recv()

    arrived(core_peer)
    arrived(side * CORES + 1 - me_c)

    @pl.when(in_middle)
    def _():
        arrived_halves(dev(2, 1 - me_c))
        for core in range(CORES):
            arrived(dev(3, core))

    @pl.when(at_end)
    def _():
        for core in range(CORES):
            arrived_halves(dev(2, core))
            arrived(dev(3, core))

    for b in range(row_blocks):
        here = pl.ds(b * block, block)
        total = acc[b]
        tiles = jnp.concatenate([cut_ref[b, k] for k in range(cut_slots)], axis=1)
        blocks = [far[lax.rem(me_d + src_ref[b, k], n_dom)] for k in range(cut_slots)]
        total = total + f32_dot(tiles, jnp.concatenate(blocks, axis=0))
        agg = total.astype(jnp.bfloat16)
        lhs[1, b] = agg
        preact = pre[here] + f32_dot(agg, w_neigh_ref[...])
        sig = jax.nn.sigmoid(preact)
        out_ref[here] = (preact * sig).astype(jnp.bfloat16)
        grad_pre_ref[here] = (
            cot_ref[here].astype(jnp.float32) * sig * (1.0 + preact * (1.0 - sig))
        ).astype(jnp.bfloat16)

    def product(which):
        return lax.dot_general(
            flat(lhs[which]),
            grad_pre_ref[...],
            (((0,), (0,)), ((), ())),
            preferred_element_type=jnp.float32,
        )

    core_out[...] = product(1 - me_c).astype(jnp.bfloat16)
    core_copy = remote(core_out, core_in, core_send, core_recv, (core_peer, me_g))
    core_copy.start()
    mine[...] = product(me_c)
    pl.semaphore_wait(grp_ready, n_grp - 1)
    core_copy.wait_recv()
    total = mine[...] + core_in[...].astype(jnp.float32)
    mine[...] = total
    mine_low[...] = total.astype(jnp.bfloat16)

    def owner_rows(t, g):
        return pl.multiple_of(((z_of(t) - 1) * n_grp + g) * piece, piece)

    def give(t, o):
        back = (n_grp - o) % n_grp
        slot = n_grp * place + back if t == 2 else 2 * n_grp + (n_grp - 1) * place + back
        g = grp_peer[o]
        return remote(
            mine_low.at[pl.ds(owner_rows(t, g), piece)],
            pieces.at[slot],
            rs_send,
            rs_recv,
            (dev(t, me_c), g),
        )

    def spot(t, g):
        start = rows + me_c * features + owner_rows(t, g)
        return out_ref.at[pl.ds(pl.multiple_of(start, piece), piece)]

    def share_at(z, g):
        own = spot(1, me_g)
        return remote(
            own, own, ag_send, ag_recv.at[me_z - 1], (z * CORES + me_c, g)
        )

    def share(t, o):
        return share_at(z_of(t), grp_peer[o])

    plane = n_grp * piece

    def forward(q, core):
        start = rows + core * features + q * plane
        part = out_ref.at[pl.ds(pl.multiple_of(start, plane), plane)]
        return remote(part, part, fw_send.at[q], fw_recv.at[q], (core_peer, me_g))

    def all_of(ref, send, recv):
        return remote(ref, ref, send, recv, (core_peer, me_g))

    for o in OTHERS_FIRST:
        give(2, o).start()
    for o in OTHERS_FIRST[:-1]:
        give(1, o).start()

    @pl.when(at_end)
    def _():
        give(1, 0).start()

    for copy in [*near_copies, *side_copies, core_copy]:
        copy.wait_send()
    for i in range(2):
        send_block(i, me_d, core_peer).wait_send()

    @pl.when(in_middle)
    def _():
        for copy in mid_copies:
            copy.wait_send()
        for i, target in enumerate(mid_jobs):
            for h in range(2):
                send_half(2 + i, mid_d, target, h).wait_send()

    @pl.when(at_end)
    def _():
        for i, target in enumerate(end_jobs):
            send_block(2 + i, me_d, target).wait_send()

    others = [(t, o) for t in (3, 2, 0) for o in OTHERS_FIRST]
    others += [(1, o) for o in OTHERS_FIRST[:-1]]

    @pl.when(in_middle)
    def _():
        all_of(pieces, rs_send, rs_recv).wait_recv()
        total = mine[pl.ds(owner_rows(1, me_g), piece)]
        for i in range(len(others)):
            total = total + pieces[i].astype(jnp.float32)
        spot(1, me_g)[...] = total.astype(jnp.bfloat16)
        for g in range(n_grp):
            share_at(0, g).start()
        for t, o in others[:n_grp]:
            share_at(n_z - 1, grp_peer[o]).start()
        for t, o in [*others[n_grp : 2 * n_grp], *others[3 * n_grp :]]:
            share(t, o).start()
        most = pl.ds(rows + me_c * features, plane - piece)
        all_of(out_ref.at[most], ag_send, ag_recv.at[me_z - 1]).wait_recv()
        forward(me_z - 1, me_c).start()
        forward_q = z_of(2) - 1
        start = rows + me_c * features + forward_q * plane
        part = out_ref.at[pl.ds(pl.multiple_of(start, plane), plane)]
        all_of(part, ag_send, ag_recv.at[forward_q]).wait_recv()
        forward(forward_q, me_c).start()
        all_of(mine_low.at[pl.ds(0, features - piece)], rs_send, rs_recv).wait_send()
        all_of(out_ref.at[pl.ds(0, len(others) * piece)], ag_send, rs_recv).wait_send()

    @pl.when(at_end)
    def _():
        for t in (1, 2):
            q = z_of(t) - 1
            start = rows + me_c * features + q * plane
            part = out_ref.at[pl.ds(pl.multiple_of(start, plane), plane)]
            all_of(part, ag_send, ag_recv.at[q]).wait_recv()
            forward(q, me_c).start()
        all_of(mine_low, rs_send, rs_recv).wait_send()

    for q in range(2):
        forward(q, 1 - me_c).wait_recv()
    for q in range(2):
        forward(q, me_c).wait_send()


def body_wide(
    feats,
    w_self,
    w_neigh,
    local_tiles,
    local_cols,
    cut_tiles,
    cut_src,
    send_block,
    send_live,
    cotangent,
):
    row_blocks, _, block, _ = local_tiles.shape
    features = feats.shape[1]
    n_dom, n_grp = lax.axis_size("dom"), lax.axis_size("grp")
    blocks = (row_blocks, block, features)
    halves = len(ORDERS)
    count = {"grp": n_grp, "dom": n_dom}
    most = max(n_grp, n_dom)
    sizes = []
    for one, two in ORDERS:
        rows = 2 * features // count[one]
        sizes.append((count[one], rows, count[two], piece_rows(rows, count[two])))
    width = features // halves
    dma = pltpu.SemaphoreType.DMA
    hbm = pl.BlockSpec(memory_space=pltpu.HBM)
    vmem = pl.BlockSpec(memory_space=pltpu.VMEM)
    out, grads = pl.pallas_call(
        functools.partial(kernel_wide, n_dom, n_grp),
        out_shape=(
            jax.ShapeDtypeStruct(blocks, jnp.bfloat16),
            jax.ShapeDtypeStruct((2 * features, features), jnp.bfloat16),
        ),
        in_specs=[hbm] * 10,
        out_specs=(vmem, vmem),
        scratch_shapes=[
            pltpu.SMEM(local_cols.shape, jnp.int32),
            pltpu.SMEM(cut_src.shape, jnp.int32),
            pltpu.SMEM(send_block.shape, jnp.int32),
            pltpu.SMEM(send_live.shape, jnp.int32),
            pltpu.VMEM(w_self.shape, jnp.bfloat16),
            pltpu.VMEM(w_neigh.shape, jnp.bfloat16),
            pltpu.VMEM(local_tiles.shape, jnp.bfloat16),
            pltpu.VMEM(cut_tiles.shape, jnp.bfloat16),
            pltpu.VMEM(blocks, jnp.bfloat16),
            pltpu.VMEM(blocks, jnp.bfloat16),
            pltpu.VMEM((n_grp * row_blocks, block, features), jnp.bfloat16),
            pltpu.VMEM((n_dom, block, features), jnp.bfloat16),
            pltpu.VMEM((n_dom, block, features), jnp.bfloat16),
            pltpu.VMEM(blocks, jnp.float32),
            pltpu.VMEM(blocks, jnp.float32),
            pltpu.VMEM((halves, 2 * features, width), jnp.float32),
            pltpu.VMEM((halves, 2 * features, width), jnp.bfloat16),
        ]
        + [pltpu.VMEM((n, r, width), jnp.bfloat16) for n, r, _, _ in sizes]
        + [pltpu.VMEM((r, width), jnp.float32) for _, r, _, _ in sizes]
        + [pltpu.VMEM((r, width), jnp.bfloat16) for _, r, _, _ in sizes]
        + [pltpu.VMEM((n, p, width), jnp.bfloat16) for _, _, n, p in sizes]
        + [
            dma((11,)),
        ]
        + [dma((n_grp,))] * 2
        + [dma((n_dom,))] * 2
        + [dma((halves, most))] * 8,
        compiler_params=pltpu.CompilerParams(
            collective_id=0, has_side_effects=True, vmem_limit_bytes=32 * 2**20
        ),
    )(
        *(
            pltpu.with_memory_space_constraint(x, pltpu.HBM)
            for x in (
                local_cols,
                cut_src,
                send_block,
                send_live,
                feats.reshape(blocks),
                w_self,
                w_neigh,
                local_tiles,
                cut_tiles,
                cotangent.reshape(blocks),
            )
        )
    )
    summed = grads.astype(jnp.float32)
    return (out.reshape(feats.shape), summed[:features], summed[features:])


def body_near(
    feats,
    w_self,
    w_neigh,
    local_tiles,
    local_cols,
    cut_tiles,
    cut_src,
    send_block,
    send_live,
    cotangent,
):
    row_blocks, _, block, _ = local_tiles.shape
    rows, features = feats.shape
    blocks = (row_blocks, block, features)
    n_dom, n_grp = lax.axis_size("dom"), lax.axis_size("grp")
    chips = n_dom // CORES * n_grp
    piece = 2 * features // chips
    dma = pltpu.SemaphoreType.DMA
    hbm = pl.BlockSpec(memory_space=pltpu.HBM)
    vmem = pl.BlockSpec(memory_space=pltpu.VMEM)
    low = functools.partial(pltpu.VMEM, dtype=jnp.bfloat16)
    wide = functools.partial(pltpu.VMEM, dtype=jnp.float32)
    res = pl.pallas_call(
        functools.partial(kernel_near, n_dom, n_grp),
        out_shape=jax.ShapeDtypeStruct((rows + 2 * features, features), jnp.bfloat16),
        in_specs=[hbm] * 10,
        out_specs=vmem,
        scratch_shapes=[
            pltpu.SMEM(local_cols.shape, jnp.int32),
            pltpu.SMEM(cut_src.shape, jnp.int32),
            pltpu.SMEM(send_block.shape, jnp.int32),
            pltpu.SMEM(send_live.shape, jnp.int32),
            low(w_self.shape),
            low(w_neigh.shape),
            low(local_tiles.shape),
            low(cut_tiles.shape),
            low(feats.shape),
            low((2, *blocks)),
            wide((rows, features)),
            low((rows, features)),
            low((n_grp * row_blocks, block, features)),
            low((6, block, features)),
            low((n_dom, block, features)),
            low(blocks),
            low((row_blocks, block // 2, features)),
            low((row_blocks, block // 2, features)),
            pltpu.SMEM((2, *send_block.shape), jnp.int32),
            pltpu.SMEM((2, *send_block.shape), jnp.int32),
            low((features, features)),
            low((features, features)),
            wide((features, features)),
            low((features, features)),
            low((chips - 1, piece, features)),
            dma((11,)),
            dma((n_grp,)),
            dma((n_grp,)),
            dma((6, 2)),
            dma((n_dom, 2)),
            dma((2, 4)),
            dma((4,)),
            dma((4,)),
            dma,
            dma,
        ]
        + [dma] * 3
        + [dma((2,))] * 3
        + [pltpu.SemaphoreType.REGULAR] * 4,
        compiler_params=pltpu.CompilerParams(
            collective_id=0, has_side_effects=True, vmem_limit_bytes=32 * 2**20
        ),
    )(
        *(
            pltpu.with_memory_space_constraint(x, pltpu.HBM)
            for x in (
                local_cols,
                cut_src,
                send_block,
                send_live,
                feats.reshape(blocks),
                w_self,
                w_neigh,
                local_tiles,
                cut_tiles,
                cotangent,
            )
        )
    )
    return (
        res[:rows],
        res[rows : rows + features].astype(jnp.float32),
        res[rows + features :].astype(jnp.float32),
    )


def solution(mesh):
    n_dom, n_grp = mesh.shape["dom"], mesh.shape["grp"]
    chips = n_dom // CORES * n_grp
    return jax.shard_map(
        lambda *args: (
            body_near
            if (n_dom, n_grp) == (LINE * CORES, len(OTHERS_FIRST))
            and 2 * args[1].shape[0] % (PACK * chips) == 0
            else body_wide
        )(*args),
        mesh=mesh,
        in_specs=(
            P(("dom", "grp"), None),
            P(),
            P(),
            P(("dom", "grp"), None, None, None),
            P(("dom", "grp"), None),
            P(("dom", "grp"), None, None, None),
            P(("dom", "grp"), None),
            P(("dom", "grp"), None),
            P(("dom", "grp"), None),
            P(("dom", "grp"), None),
        ),
        out_specs=(P(("dom", "grp"), None), P(), P()),
        check_vma=False,
    )
```

```python
import functools

import jax
import jax.numpy as jnp
from jax import lax
from jax.experimental import pallas as pl
from jax.experimental.pallas import tpu as pltpu
from jax.sharding import PartitionSpec as P

MESH = pl.DeviceIdType.MESH
PACK = 16
FEW = 4
CORES = 2
LINE = 4
OTHERS_FIRST = (3, 1, 2, 0)
ORDERS = (("grp", "dom"), ("dom", "grp"))


def piece_rows(rows, n):
    return rows // n if n > FEW and rows % (PACK * n) == 0 else rows


def f32_dot(a, b):
    return jnp.dot(a, b, preferred_element_type=jnp.float32)


def kernel_wide(
    n_dom,
    n_grp,
    cols_hbm,
    src_hbm,
    block_hbm,
    live_hbm,
    feats_hbm,
    w_self_hbm,
    w_neigh_hbm,
    local_hbm,
    cut_hbm,
    cot_hbm,
    out_ref,
    grad_ref,
    cols_ref,
    src_ref,
    block_ref,
    live_ref,
    w_self_ref,
    w_neigh_ref,
    local_ref,
    cut_ref,
    cot_ref,
    feats_ref,
    near,
    outgoing,
    far,
    acc,
    pre,
    part,
    part_low,
    sums1_a,
    sums1_b,
    mid_a,
    mid_b,
    low_a,
    low_b,
    sums2_a,
    sums2_b,
    load_sem,
    near_send,
    near_recv,
    far_send,
    far_recv,
    s1_send,
    s1_recv,
    s2_send,
    s2_recv,
    s3_send,
    s3_recv,
    s4_send,
    s4_recv,
):
    sums1, mid, mid_low = (sums1_a, sums1_b), (mid_a, mid_b), (low_a, low_b)
    sums2 = (sums2_a, sums2_b)
    row_blocks, local_slots, block, _ = local_ref.shape
    cut_slots = cut_ref.shape[1]
    features = w_self_ref.shape[0]
    width = part.shape[2]
    me_d, me_g = lax.axis_index("dom"), lax.axis_index("grp")
    dom_peer = [lax.rem(me_d + o, n_dom) for o in range(n_dom)]
    grp_peer = [lax.rem(me_g + o, n_grp) for o in range(n_grp)]

    def remote(src, dst, send, recv, o, axis):
        peer = dom_peer[o] if axis == "dom" else grp_peer[o]
        return pltpu.make_async_remote_copy(
            src_ref=src,
            dst_ref=dst,
            send_sem=send,
            recv_sem=recv,
            device_id={axis: peer},
            device_id_type=MESH,
        )

    def begin(copies):
        for copy in copies:
            copy.start()
        return copies

    barrier = pltpu.get_barrier_semaphore()
    for o in range(1, n_dom):
        pl.semaphore_signal(barrier, inc=1, device_id={"dom": dom_peer[o]}, device_id_type=MESH)
    for o in range(1, n_grp):
        pl.semaphore_signal(barrier, inc=1, device_id={"grp": grp_peer[o]}, device_id_type=MESH)
    loads = begin(
        [
            pltpu.make_async_copy(src, dst, load_sem.at[i])
            for i, (src, dst) in enumerate(
                (
                    (block_hbm, block_ref),
                    (live_hbm, live_ref),
                    (feats_hbm, feats_ref),
                    (feats_hbm, near.at[pl.ds(0, row_blocks)]),
                    (cols_hbm, cols_ref),
                    (src_hbm, src_ref),
                    (w_self_hbm, w_self_ref),
                    (local_hbm, local_ref),
                    (cut_hbm, cut_ref),
                    (w_neigh_hbm, w_neigh_ref),
                    (cot_hbm, cot_ref),
                )
            )
        ]
    )
    for load in loads[:3]:
        load.wait()

    for o in range(n_dom):
        alive = live_ref[0, dom_peer[o]].astype(jnp.float32)
        chosen = feats_ref[block_ref[0, dom_peer[o]]].astype(jnp.float32)
        target = far if o == 0 else outgoing
        target[o] = (chosen * alive).astype(jnp.bfloat16)
    pl.semaphore_wait(barrier, n_dom + n_grp - 2)

    far_copies = begin(
        [
            remote(outgoing.at[o], far.at[o], far_send.at[o], far_recv.at[o], o, "dom")
            for o in sorted(range(1, n_dom), key=lambda o: abs(2 * o - n_dom))
        ]
    )
    near_copies = begin(
        [
            remote(
                feats_ref,
                near.at[pl.ds(o * row_blocks, row_blocks)],
                near_send.at[o],
                near_recv.at[o],
                o,
                "grp",
            )
            for o in range(1, n_grp)
        ]
    )

    for load in loads[3:]:
        load.wait()
    for b in range(row_blocks):
        pre[b] = f32_dot(feats_ref[b], w_self_ref[...])
    for copy in near_copies:
        copy.wait_recv()
    for b in range(row_blocks):
        total = jnp.zeros((block, features), jnp.float32)
        for k in range(local_slots):
            col = cols_ref[b, k]
            owner = lax.div(col, row_blocks)
            slot = lax.rem(me_g - owner + n_grp, n_grp)
            where = slot * row_blocks + lax.rem(col, row_blocks)
            total = total + f32_dot(local_ref[b, k], near[where])
        acc[b] = total

    for copy in far_copies:
        copy.wait_recv()
    grads_own = jnp.zeros((features, features), jnp.float32)
    grads_agg = jnp.zeros((features, features), jnp.float32)
    for b in range(row_blocks):
        total = acc[b]
        for k in range(cut_slots):
            slot = lax.rem(n_dom - src_ref[b, k], n_dom)
            total = total + f32_dot(cut_ref[b, k], far[slot])
        agg = total.astype(jnp.bfloat16)
        own = feats_ref[b]
        preact = pre[b] + f32_dot(agg, w_neigh_ref[...])
        sig = jax.nn.sigmoid(preact)
        out_ref[b] = (preact * sig).astype(jnp.bfloat16)
        grad_pre = (
            cot_ref[b].astype(jnp.float32) * sig * (1.0 + preact * (1.0 - sig))
        ).astype(jnp.bfloat16)
        dims = (((0,), (0,)), ((), ()))
        grads_own = grads_own + lax.dot_general(
            own, grad_pre, dims, preferred_element_type=jnp.float32
        )
        grads_agg = grads_agg + lax.dot_general(
            agg, grad_pre, dims, preferred_element_type=jnp.float32
        )

    peers = {"grp": grp_peer, "dom": dom_peer}
    here = {"grp": me_g, "dom": me_d}
    count = {"grp": n_grp, "dom": n_dom}

    def rows_at(start, size):
        return pl.ds(pl.multiple_of(start, size), size)

    def to_peers(axis, src, dst, send, recv):
        return begin(
            [
                remote(src(o), dst(o), send.at[o], recv.at[o], o, axis)
                for o in range(1, count[axis])
            ]
        )

    flows = []
    for h, (one, two) in enumerate(ORDERS):
        rows = 2 * features // count[one]
        piece = piece_rows(rows, count[two])
        split = piece < rows
        flows.append(
            dict(
                one=one,
                two=two,
                rows=rows,
                piece=piece,
                split=split,
                columns=pl.ds(h * width, width),
                mine=rows_at(here[one] * rows, rows),
                inner=rows_at(here[two] * piece, piece) if split else pl.ds(0, rows),
                spot=rows_at(here[one] * rows + (here[two] * piece if split else 0), piece),
                sums1=sums1[h],
                mid=mid[h],
                mid_low=mid_low[h],
                sums2=sums2[h],
            )
        )

    first = []
    for h, f in enumerate(flows):
        cut = slice(h * width, (h + 1) * width)
        part[h, 0:features] = grads_own[:, cut]
        part[h, features : 2 * features] = grads_agg[:, cut]
        part_low[h, 0:features] = grads_own[:, cut].astype(jnp.bfloat16)
        part_low[h, features : 2 * features] = grads_agg[:, cut].astype(jnp.bfloat16)
        first.append(
            to_peers(
                f["one"],
                lambda o: part_low.at[h, rows_at(peers[f["one"]][o] * f["rows"], f["rows"])],
                lambda o: f["sums1"].at[o],
                s1_send.at[h],
                s1_recv.at[h],
            )
        )
    second = []
    for h, f in enumerate(flows):
        total = part[h, f["mine"]]
        for o, copy in enumerate(first[h], 1):
            copy.wait_recv()
            total = total + f["sums1"][o].astype(jnp.float32)
        f["mid"][...] = total
        f["mid_low"][...] = total.astype(jnp.bfloat16)
        second.append(
            to_peers(
                f["two"],
                lambda o: f["mid_low"].at[rows_at(peers[f["two"]][o] * f["piece"], f["piece"])]
                if f["split"]
                else f["mid_low"],
                lambda o: f["sums2"].at[o if f["split"] else here[f["two"]]],
                s2_send.at[h],
                s2_recv.at[h],
            )
        )
    third, fourth = [], []

    def gather(h, f):
        rows_of = grad_ref.at[f["mine"], f["columns"]]
        return to_peers(
            f["one"], lambda o: rows_of, lambda o: rows_of, s4_send.at[h], s4_recv.at[h]
        )

    for h, f in enumerate(flows):
        if f["split"]:
            total = f["mid"][f["inner"]]
            for o, copy in enumerate(second[h], 1):
                copy.wait_recv()
                total = total + f["sums2"][o].astype(jnp.float32)
        else:
            f["sums2"][here[f["two"]]] = f["mid_low"][...]
            for copy in second[h]:
                copy.wait_recv()
            total = f["sums2"][0].astype(jnp.float32)
            for o in range(1, count[f["two"]]):
                total = total + f["sums2"][o].astype(jnp.float32)
        grad_ref[f["spot"], f["columns"]] = total.astype(jnp.bfloat16)
        if f["split"]:
            block_of = grad_ref.at[f["spot"], f["columns"]]
            third.append(
                to_peers(
                    f["two"],
                    lambda o: block_of,
                    lambda o: block_of,
                    s3_send.at[h],
                    s3_recv.at[h],
                )
            )
        else:
            third.append([])
            fourth += gather(h, f)
    for h, f in enumerate(flows):
        if f["split"]:
            for copy in third[h]:
                copy.wait_recv()
            fourth += gather(h, f)
    for copy in fourth:
        copy.wait_recv()

    sent = [far_copies, near_copies, *first, *second, *third, fourth]
    for copy in [copy for group in sent for copy in group]:
        copy.wait_send()


def kernel_near(
    n_dom,
    n_grp,
    cols_hbm,
    src_hbm,
    block_hbm,
    live_hbm,
    feats_hbm,
    w_self_hbm,
    w_neigh_hbm,
    local_hbm,
    cut_hbm,
    cot_hbm,
    out_ref,
    cols_ref,
    src_ref,
    block_ref,
    live_ref,
    w_self_ref,
    w_neigh_ref,
    local_ref,
    cut_ref,
    cot_ref,
    lhs,
    pre,
    grad_pre_ref,
    near,
    outgoing,
    far,
    raw_side,
    raw_mid_a,
    raw_mid_b,
    plan_side,
    plan_mid,
    core_out,
    core_in,
    mine,
    mine_low,
    pieces,
    load_sem,
    near_send,
    near_recv,
    out_send,
    far_recv,
    raw_send,
    side_recv,
    mid_recv,
    core_send,
    core_recv,
    rs_send,
    rs_recv,
    ag_send,
    ag_recv,
    fw_send,
    fw_recv,
    peer_here,
    side_ready,
    mid_ready,
    line_ready,
    grp_ready,
):
    row_blocks, local_slots, block, _ = local_ref.shape
    cut_slots = cut_ref.shape[1]
    features = w_self_ref.shape[0]
    rows = row_blocks * block
    n_z = n_dom // CORES
    piece = pieces.shape[1]
    me_d, me_g = lax.axis_index("dom"), lax.axis_index("grp")
    me_z, me_c = lax.div(me_d, CORES), lax.rem(me_d, CORES)
    grp_peer = [lax.rem(me_g + o, n_grp) for o in range(n_grp)]
    place = jnp.where(me_z < n_z // 2, me_z, n_z - 1 - me_z)
    at_end, in_middle = place == 0, place == 1

    def z_of(t):
        return jnp.where(me_z < n_z // 2, t, n_z - 1 - t)

    def dev(t, core):
        return z_of(t) * CORES + core

    side = z_of(1 - place)
    core_peer = me_d + 1 - 2 * me_c
    raw_mids = (raw_mid_a, raw_mid_b)
    halves = [pl.ds(h * (block // 2), block // 2) for h in range(2)]

    def flat(x):
        return x.reshape(rows, features)

    def remote(src, dst, send, recv, device):
        return pltpu.make_async_remote_copy(
            src_ref=src,
            dst_ref=dst,
            send_sem=send,
            recv_sem=recv,
            device_id=device,
            device_id_type=MESH,
        )

    def begin(copies):
        for copy in copies:
            copy.start()
        return copies

    def signal(sem, dom, grp):
        pl.semaphore_signal(sem, inc=1, device_id=(dom, grp), device_id_type=MESH)

    barrier = pltpu.get_barrier_semaphore()
    signal(barrier, core_peer, me_g)

    @pl.when(in_middle)
    def _():
        signal(barrier, dev(2, me_c), me_g)
        for core in range(CORES):
            signal(barrier, dev(0, core), me_g)

    for g in range(1, n_grp):

        @pl.when(me_g < g)
        def _():
            signal(barrier, me_d, g)

    loads = begin(
        [
            pltpu.make_async_copy(src, dst, load_sem.at[i])
            for i, (src, dst) in enumerate(
                (
                    (block_hbm, block_ref),
                    (live_hbm, live_ref),
                    (feats_hbm, lhs.at[0]),
                    (feats_hbm, near.at[pl.ds(me_g * row_blocks, row_blocks)]),
                    (cols_hbm, cols_ref),
                    (src_hbm, src_ref),
                    (w_self_hbm, w_self_ref),
                    (local_hbm, local_ref),
                    (cut_hbm, cut_ref),
                    (w_neigh_hbm, w_neigh_ref),
                    (cot_hbm, cot_ref),
                )
            )
        ]
    )

    def plan_copies(target, plan, send, recv):
        device = (target, me_g)
        return [
            remote(block_hbm, plan.at[0], send.at[0], recv.at[0], device),
            remote(live_hbm, plan.at[1], send.at[1], recv.at[1], device),
        ]

    side_d = side * CORES + me_c
    side_copies = plan_copies(side_d, plan_side, raw_send.at[0], side_recv)
    side_copies.append(
        remote(feats_hbm, raw_side, raw_send.at[0, 2], side_recv.at[2], (side_d, me_g))
    )
    mid_copies = plan_copies(dev(2, me_c), plan_mid, raw_send.at[1], mid_recv)
    mid_copies += [
        remote(
            feats_hbm.at[:, part],
            raw_mids[h],
            raw_send.at[1, 2 + h],
            mid_recv.at[2 + h],
            (dev(2, me_c), me_g),
        )
        for h, part in enumerate(halves)
    ]
    pl.semaphore_wait(barrier, CORES + 1 - place + me_g)

    @pl.when(in_middle)
    def _():
        begin(mid_copies)

    @pl.when(at_end)
    def _():
        for core in range(CORES):
            signal(side_ready, dev(1, core), me_g)
        begin(side_copies)

    for g in range(n_grp - 1):

        @pl.when(me_g > g)
        def _():
            signal(peer_here, me_d, g)

    @pl.when(in_middle)
    def _():
        pl.semaphore_wait(side_ready, CORES)
        begin(side_copies)
        signal(mid_ready, dev(2, me_c), me_g)
        pl.semaphore_wait(mid_ready, 1)
        for core in range(CORES):
            signal(line_ready, dev(0, core), me_g)

    def chosen(blocks_of, block_at, alive):
        picked = blocks_of(block_at).astype(jnp.float32)
        return (picked * alive.astype(jnp.float32)).astype(jnp.bfloat16)

    def of_own(target):
        return chosen(lambda i: lhs[0, i], block_ref[0, target], live_ref[0, target])

    def of_side(target):
        return chosen(lambda i: raw_side[i], plan_side[0, 0, target], plan_side[1, 0, target])

    def of_mid(target, part):
        return chosen(
            lambda i: raw_mids[part][i], plan_mid[0, 0, target], plan_mid[1, 0, target]
        )

    def send_block(i, source, target):
        return remote(
            outgoing.at[i],
            far.at[source],
            out_send.at[i, 0],
            far_recv.at[source, 0],
            (target, me_g),
        )

    def send_half(i, source, target, h):
        return remote(
            outgoing.at[i, halves[h]],
            far.at[source, halves[h]],
            out_send.at[i, h],
            far_recv.at[source, h],
            (target, me_g),
        )

    for load in loads[:4]:
        load.wait()
    end_jobs = [(dev(t, core)) for t in (3, 2) for core in range(CORES)]

    @pl.when(at_end)
    def _():
        for i, target in enumerate(end_jobs):
            outgoing[2 + i] = of_own(target)

    @pl.when(me_g < n_grp - 1)
    def _():
        pl.semaphore_wait(peer_here, n_grp - 1 - me_g)

    near_copies = begin(
        [
            remote(
                feats_hbm,
                near.at[pl.ds(me_g * row_blocks, row_blocks)],
                near_send.at[o],
                near_recv.at[o],
                (me_d, grp_peer[o]),
            )
            for o in range(1, n_grp)
        ]
    )

    @pl.when(at_end)
    def _():
        pl.semaphore_wait(line_ready, CORES)
        for i, target in enumerate(end_jobs):
            send_block(2 + i, me_d, target).start()

    for o in range(1, n_grp):
        signal(grp_ready, me_d, grp_peer[o])
    outgoing[0] = of_own(core_peer)
    send_block(0, me_d, core_peer).start()
    far[me_d] = of_own(me_d)

    for load in loads[4:]:
        load.wait()
    pre[...] = f32_dot(flat(lhs[0]), w_self_ref[...])

    mid_d = dev(2, me_c)
    mid_jobs = [dev(0, 0), dev(0, 1), core_peer]

    @pl.when(in_middle)
    def _():
        for copy in mid_copies[:2]:
            copy.wait_recv()
        for h, part in enumerate(halves):
            mid_copies[2 + h].wait_recv()
            for i, target in enumerate(mid_jobs):
                outgoing[2 + i, part] = of_mid(target, h)
                send_half(2 + i, mid_d, target, h).start()
            far[mid_d, part] = of_mid(me_d, h)

    for copy in side_copies:
        copy.wait_recv()
    outgoing[1] = of_side(core_peer)
    send_block(1, side_d, core_peer).start()
    far[side_d] = of_side(me_d)

    for copy in near_copies:
        copy.wait_recv()
    acc = []
    for b in range(row_blocks):
        total = jnp.zeros((block, features), jnp.float32)
        for k in range(local_slots):
            total = total + f32_dot(local_ref[b, k], near[cols_ref[b, k]])
        acc.append(total)

    def arrived(source):
        send_block(0, source, core_peer).wait_recv()

    def arrived_halves(source):
        for h in range(2):
            send_half(0, source, core_peer, h).wait_recv()

    arrived(core_peer)
    arrived(side * CORES + 1 - me_c)

    @pl.when(in_middle)
    def _():
        arrived_halves(dev(2, 1 - me_c))
        for core in range(CORES):
            arrived(dev(3, core))

    @pl.when(at_end)
    def _():
        for core in range(CORES):
            arrived_halves(dev(2, core))
            arrived(dev(3, core))

    for b in range(row_blocks):
        tiles = jnp.concatenate([cut_ref[b, k] for k in range(cut_slots)], axis=1)
        blocks = [far[lax.rem(me_d + src_ref[b, k], n_dom)] for k in range(cut_slots)]
        total = acc[b] + f32_dot(tiles, jnp.concatenate(blocks, axis=0))
        lhs[1, b] = total.astype(jnp.bfloat16)
    preact = pre[...] + f32_dot(flat(lhs[1]), w_neigh_ref[...])
    sig = jax.nn.sigmoid(preact)
    grad_pre_ref[...] = (
        cot_ref[...].astype(jnp.float32) * sig * (1.0 + preact * (1.0 - sig))
    ).astype(jnp.bfloat16)
    out_ref[pl.ds(0, rows)] = (preact * sig).astype(jnp.bfloat16)

    plane = n_grp * piece

    def half_of(t):
        return pl.ds(pl.multiple_of((z_of(t) - 1) * plane, plane), plane)

    def product(which, part):
        return lax.dot_general(
            lhs[which, :, :, part].reshape(rows, plane),
            grad_pre_ref[...],
            (((0,), (0,)), ((), ())),
            preferred_element_type=jnp.float32,
        )

    core_copies = {}
    for t in (2, 1):
        part = half_of(t)
        core_out[part] = product(1 - me_c, part).astype(jnp.bfloat16)
        core_copies[t] = remote(
            core_out.at[part],
            core_in.at[part],
            core_send.at[t - 1],
            core_recv.at[z_of(t) - 1],
            (core_peer, me_g),
        )
        core_copies[t].start()
    for t in (2, 1):
        mine[half_of(t)] = product(me_c, half_of(t))
    pl.semaphore_wait(grp_ready, n_grp - 1)

    def owner_rows(t, g):
        return pl.multiple_of(((z_of(t) - 1) * n_grp + g) * piece, piece)

    def give(t, o):
        back = (n_grp - o) % n_grp
        slot = n_grp * place + back if t == 2 else 2 * n_grp + (n_grp - 1) * place + back
        g = grp_peer[o]
        return remote(
            mine_low.at[pl.ds(owner_rows(t, g), piece)],
            pieces.at[slot],
            rs_send,
            rs_recv,
            (dev(t, me_c), g),
        )

    def spot(t, g):
        start = rows + me_c * features + owner_rows(t, g)
        return out_ref.at[pl.ds(pl.multiple_of(start, piece), piece)]

    def share_at(z, g):
        own = spot(1, me_g)
        return remote(
            own, own, ag_send, ag_recv.at[me_z - 1], (z * CORES + me_c, g)
        )

    def share(t, o):
        return share_at(z_of(t), grp_peer[o])

    def forward(q, core):
        start = rows + core * features + q * plane
        part = out_ref.at[pl.ds(pl.multiple_of(start, plane), plane)]
        return remote(part, part, fw_send.at[q], fw_recv.at[q], (core_peer, me_g))

    def all_of(ref, send, recv):
        return remote(ref, ref, send, recv, (core_peer, me_g))

    for t in (2, 1):
        part = half_of(t)
        core_copies[t].wait_recv()
        total = mine[part] + core_in[part].astype(jnp.float32)
        mine[part] = total
        mine_low[part] = total.astype(jnp.bfloat16)
        for o in OTHERS_FIRST if t == 2 else OTHERS_FIRST[:-1]:
            give(t, o).start()

    @pl.when(at_end)
    def _():
        give(1, 0).start()

    for copy in [*near_copies, *side_copies, *core_copies.values()]:
        copy.wait_send()
    for i in range(2):
        send_block(i, me_d, core_peer).wait_send()

    @pl.when(in_middle)
    def _():
        for copy in mid_copies:
            copy.wait_send()
        for i, target in enumerate(mid_jobs):
            for h in range(2):
                send_half(2 + i, mid_d, target, h).wait_send()

    @pl.when(at_end)
    def _():
        for i, target in enumerate(end_jobs):
            send_block(2 + i, me_d, target).wait_send()

    others = [(t, o) for t in (3, 2, 0) for o in OTHERS_FIRST]
    others += [(1, o) for o in OTHERS_FIRST[:-1]]

    @pl.when(in_middle)
    def _():
        all_of(pieces, rs_send, rs_recv).wait_recv()
        total = mine[pl.ds(owner_rows(1, me_g), piece)]
        for i in range(len(others)):
            total = total + pieces[i].astype(jnp.float32)
        spot(1, me_g)[...] = total.astype(jnp.bfloat16)
        for g in range(n_grp):
            share_at(0, g).start()
        for t, o in others[:n_grp]:
            share_at(n_z - 1, grp_peer[o]).start()
        for t, o in [*others[n_grp : 2 * n_grp], *others[3 * n_grp :]]:
            share(t, o).start()
        most = pl.ds(rows + me_c * features, plane - piece)
        all_of(out_ref.at[most], ag_send, ag_recv.at[me_z - 1]).wait_recv()
        forward(me_z - 1, me_c).start()
        forward_q = z_of(2) - 1
        start = rows + me_c * features + forward_q * plane
        part = out_ref.at[pl.ds(pl.multiple_of(start, plane), plane)]
        all_of(part, ag_send, ag_recv.at[forward_q]).wait_recv()
        forward(forward_q, me_c).start()
        all_of(mine_low.at[pl.ds(0, features - piece)], rs_send, rs_recv).wait_send()
        all_of(out_ref.at[pl.ds(0, len(others) * piece)], ag_send, rs_recv).wait_send()

    @pl.when(at_end)
    def _():
        for t in (1, 2):
            q = z_of(t) - 1
            start = rows + me_c * features + q * plane
            part = out_ref.at[pl.ds(pl.multiple_of(start, plane), plane)]
            all_of(part, ag_send, ag_recv.at[q]).wait_recv()
            forward(q, me_c).start()
        all_of(mine_low, rs_send, rs_recv).wait_send()

    for q in range(2):
        forward(q, 1 - me_c).wait_recv()
    for q in range(2):
        forward(q, me_c).wait_send()


def body_wide(
    feats,
    w_self,
    w_neigh,
    local_tiles,
    local_cols,
    cut_tiles,
    cut_src,
    send_block,
    send_live,
    cotangent,
):
    row_blocks, _, block, _ = local_tiles.shape
    features = feats.shape[1]
    n_dom, n_grp = lax.axis_size("dom"), lax.axis_size("grp")
    blocks = (row_blocks, block, features)
    halves = len(ORDERS)
    count = {"grp": n_grp, "dom": n_dom}
    most = max(n_grp, n_dom)
    sizes = []
    for one, two in ORDERS:
        rows = 2 * features // count[one]
        sizes.append((count[one], rows, count[two], piece_rows(rows, count[two])))
    width = features // halves
    dma = pltpu.SemaphoreType.DMA
    hbm = pl.BlockSpec(memory_space=pltpu.HBM)
    vmem = pl.BlockSpec(memory_space=pltpu.VMEM)
    out, grads = pl.pallas_call(
        functools.partial(kernel_wide, n_dom, n_grp),
        out_shape=(
            jax.ShapeDtypeStruct(blocks, jnp.bfloat16),
            jax.ShapeDtypeStruct((2 * features, features), jnp.bfloat16),
        ),
        in_specs=[hbm] * 10,
        out_specs=(vmem, vmem),
        scratch_shapes=[
            pltpu.SMEM(local_cols.shape, jnp.int32),
            pltpu.SMEM(cut_src.shape, jnp.int32),
            pltpu.SMEM(send_block.shape, jnp.int32),
            pltpu.SMEM(send_live.shape, jnp.int32),
            pltpu.VMEM(w_self.shape, jnp.bfloat16),
            pltpu.VMEM(w_neigh.shape, jnp.bfloat16),
            pltpu.VMEM(local_tiles.shape, jnp.bfloat16),
            pltpu.VMEM(cut_tiles.shape, jnp.bfloat16),
            pltpu.VMEM(blocks, jnp.bfloat16),
            pltpu.VMEM(blocks, jnp.bfloat16),
            pltpu.VMEM((n_grp * row_blocks, block, features), jnp.bfloat16),
            pltpu.VMEM((n_dom, block, features), jnp.bfloat16),
            pltpu.VMEM((n_dom, block, features), jnp.bfloat16),
            pltpu.VMEM(blocks, jnp.float32),
            pltpu.VMEM(blocks, jnp.float32),
            pltpu.VMEM((halves, 2 * features, width), jnp.float32),
            pltpu.VMEM((halves, 2 * features, width), jnp.bfloat16),
        ]
        + [pltpu.VMEM((n, r, width), jnp.bfloat16) for n, r, _, _ in sizes]
        + [pltpu.VMEM((r, width), jnp.float32) for _, r, _, _ in sizes]
        + [pltpu.VMEM((r, width), jnp.bfloat16) for _, r, _, _ in sizes]
        + [pltpu.VMEM((n, p, width), jnp.bfloat16) for _, _, n, p in sizes]
        + [
            dma((11,)),
        ]
        + [dma((n_grp,))] * 2
        + [dma((n_dom,))] * 2
        + [dma((halves, most))] * 8,
        compiler_params=pltpu.CompilerParams(
            collective_id=0, has_side_effects=True, vmem_limit_bytes=32 * 2**20
        ),
    )(
        *(
            pltpu.with_memory_space_constraint(x, pltpu.HBM)
            for x in (
                local_cols,
                cut_src,
                send_block,
                send_live,
                feats.reshape(blocks),
                w_self,
                w_neigh,
                local_tiles,
                cut_tiles,
                cotangent.reshape(blocks),
            )
        )
    )
    summed = grads.astype(jnp.float32)
    return (out.reshape(feats.shape), summed[:features], summed[features:])


def body_near(
    feats,
    w_self,
    w_neigh,
    local_tiles,
    local_cols,
    cut_tiles,
    cut_src,
    send_block,
    send_live,
    cotangent,
):
    row_blocks, _, block, _ = local_tiles.shape
    rows, features = feats.shape
    blocks = (row_blocks, block, features)
    n_dom, n_grp = lax.axis_size("dom"), lax.axis_size("grp")
    chips = n_dom // CORES * n_grp
    piece = 2 * features // chips
    dma = pltpu.SemaphoreType.DMA
    hbm = pl.BlockSpec(memory_space=pltpu.HBM)
    vmem = pl.BlockSpec(memory_space=pltpu.VMEM)
    low = functools.partial(pltpu.VMEM, dtype=jnp.bfloat16)
    wide = functools.partial(pltpu.VMEM, dtype=jnp.float32)
    res = pl.pallas_call(
        functools.partial(kernel_near, n_dom, n_grp),
        out_shape=jax.ShapeDtypeStruct((rows + 2 * features, features), jnp.bfloat16),
        in_specs=[hbm] * 10,
        out_specs=vmem,
        scratch_shapes=[
            pltpu.SMEM(local_cols.shape, jnp.int32),
            pltpu.SMEM(cut_src.shape, jnp.int32),
            pltpu.SMEM(send_block.shape, jnp.int32),
            pltpu.SMEM(send_live.shape, jnp.int32),
            low(w_self.shape),
            low(w_neigh.shape),
            low(local_tiles.shape),
            low(cut_tiles.shape),
            low(feats.shape),
            low((2, *blocks)),
            wide((rows, features)),
            low((rows, features)),
            low((n_grp * row_blocks, block, features)),
            low((6, block, features)),
            low((n_dom, block, features)),
            low(blocks),
            low((row_blocks, block // 2, features)),
            low((row_blocks, block // 2, features)),
            pltpu.SMEM((2, *send_block.shape), jnp.int32),
            pltpu.SMEM((2, *send_block.shape), jnp.int32),
            low((features, features)),
            low((features, features)),
            wide((features, features)),
            low((features, features)),
            low((chips - 1, piece, features)),
            dma((11,)),
            dma((n_grp,)),
            dma((n_grp,)),
            dma((6, 2)),
            dma((n_dom, 2)),
            dma((2, 4)),
            dma((4,)),
            dma((4,)),
            dma((2,)),
            dma((2,)),
        ]
        + [dma] * 3
        + [dma((2,))] * 3
        + [pltpu.SemaphoreType.REGULAR] * 5,
        compiler_params=pltpu.CompilerParams(
            collective_id=0, has_side_effects=True, vmem_limit_bytes=32 * 2**20
        ),
    )(
        *(
            pltpu.with_memory_space_constraint(x, pltpu.HBM)
            for x in (
                local_cols,
                cut_src,
                send_block,
                send_live,
                feats.reshape(blocks),
                w_self,
                w_neigh,
                local_tiles,
                cut_tiles,
                cotangent,
            )
        )
    )
    return (
        res[:rows],
        res[rows : rows + features].astype(jnp.float32),
        res[rows + features :].astype(jnp.float32),
    )


def solution(mesh):
    n_dom, n_grp = mesh.shape["dom"], mesh.shape["grp"]
    chips = n_dom // CORES * n_grp
    return jax.shard_map(
        lambda *args: (
            body_near
            if (n_dom, n_grp) == (LINE * CORES, len(OTHERS_FIRST))
            and 2 * args[1].shape[0] % (PACK * chips) == 0
            else body_wide
        )(*args),
        mesh=mesh,
        in_specs=(
            P(("dom", "grp"), None),
            P(),
            P(),
            P(("dom", "grp"), None, None, None),
            P(("dom", "grp"), None),
            P(("dom", "grp"), None, None, None),
            P(("dom", "grp"), None),
            P(("dom", "grp"), None),
            P(("dom", "grp"), None),
            P(("dom", "grp"), None),
        ),
        out_specs=(P(("dom", "grp"), None), P(), P()),
        check_vma=False,
    )
```

```python
import functools

import jax
import jax.numpy as jnp
from jax import lax
from jax.experimental import pallas as pl
from jax.experimental.pallas import tpu as pltpu
from jax.sharding import PartitionSpec as P

MESH = pl.DeviceIdType.MESH
PACK = 16
FEW = 4
CORES = 2
LINE = 4
PARTS = 2
OTHERS_FIRST = (3, 1, 2, 0)
ORDERS = (("grp", "dom"), ("dom", "grp"))


def piece_rows(rows, n):
    return rows // n if n > FEW and rows % (PACK * n) == 0 else rows


def f32_dot(a, b):
    return jnp.dot(a, b, preferred_element_type=jnp.float32)


def kernel_wide(
    n_dom,
    n_grp,
    cols_hbm,
    src_hbm,
    block_hbm,
    live_hbm,
    feats_hbm,
    w_self_hbm,
    w_neigh_hbm,
    local_hbm,
    cut_hbm,
    cot_hbm,
    out_ref,
    grad_ref,
    cols_ref,
    src_ref,
    block_ref,
    live_ref,
    w_self_ref,
    w_neigh_ref,
    local_ref,
    cut_ref,
    cot_ref,
    feats_ref,
    near,
    outgoing,
    far,
    acc,
    pre,
    part,
    part_low,
    sums1_a,
    sums1_b,
    mid_a,
    mid_b,
    low_a,
    low_b,
    sums2_a,
    sums2_b,
    load_sem,
    near_send,
    near_recv,
    far_send,
    far_recv,
    s1_send,
    s1_recv,
    s2_send,
    s2_recv,
    s3_send,
    s3_recv,
    s4_send,
    s4_recv,
):
    sums1, mid, mid_low = (sums1_a, sums1_b), (mid_a, mid_b), (low_a, low_b)
    sums2 = (sums2_a, sums2_b)
    row_blocks, local_slots, block, _ = local_ref.shape
    cut_slots = cut_ref.shape[1]
    features = w_self_ref.shape[0]
    width = part.shape[2]
    me_d, me_g = lax.axis_index("dom"), lax.axis_index("grp")
    dom_peer = [lax.rem(me_d + o, n_dom) for o in range(n_dom)]
    grp_peer = [lax.rem(me_g + o, n_grp) for o in range(n_grp)]

    def remote(src, dst, send, recv, o, axis):
        peer = dom_peer[o] if axis == "dom" else grp_peer[o]
        return pltpu.make_async_remote_copy(
            src_ref=src,
            dst_ref=dst,
            send_sem=send,
            recv_sem=recv,
            device_id={axis: peer},
            device_id_type=MESH,
        )

    def begin(copies):
        for copy in copies:
            copy.start()
        return copies

    barrier = pltpu.get_barrier_semaphore()
    for o in range(1, n_dom):
        pl.semaphore_signal(barrier, inc=1, device_id={"dom": dom_peer[o]}, device_id_type=MESH)
    for o in range(1, n_grp):
        pl.semaphore_signal(barrier, inc=1, device_id={"grp": grp_peer[o]}, device_id_type=MESH)
    loads = begin(
        [
            pltpu.make_async_copy(src, dst, load_sem.at[i])
            for i, (src, dst) in enumerate(
                (
                    (block_hbm, block_ref),
                    (live_hbm, live_ref),
                    (feats_hbm, feats_ref),
                    (feats_hbm, near.at[pl.ds(0, row_blocks)]),
                    (cols_hbm, cols_ref),
                    (src_hbm, src_ref),
                    (w_self_hbm, w_self_ref),
                    (local_hbm, local_ref),
                    (cut_hbm, cut_ref),
                    (w_neigh_hbm, w_neigh_ref),
                    (cot_hbm, cot_ref),
                )
            )
        ]
    )
    for load in loads[:3]:
        load.wait()

    for o in range(n_dom):
        alive = live_ref[0, dom_peer[o]].astype(jnp.float32)
        chosen = feats_ref[block_ref[0, dom_peer[o]]].astype(jnp.float32)
        target = far if o == 0 else outgoing
        target[o] = (chosen * alive).astype(jnp.bfloat16)
    pl.semaphore_wait(barrier, n_dom + n_grp - 2)

    far_copies = begin(
        [
            remote(outgoing.at[o], far.at[o], far_send.at[o], far_recv.at[o], o, "dom")
            for o in sorted(range(1, n_dom), key=lambda o: abs(2 * o - n_dom))
        ]
    )
    near_copies = begin(
        [
            remote(
                feats_ref,
                near.at[pl.ds(o * row_blocks, row_blocks)],
                near_send.at[o],
                near_recv.at[o],
                o,
                "grp",
            )
            for o in range(1, n_grp)
        ]
    )

    for load in loads[3:]:
        load.wait()
    for b in range(row_blocks):
        pre[b] = f32_dot(feats_ref[b], w_self_ref[...])
    for copy in near_copies:
        copy.wait_recv()
    for b in range(row_blocks):
        total = jnp.zeros((block, features), jnp.float32)
        for k in range(local_slots):
            col = cols_ref[b, k]
            owner = lax.div(col, row_blocks)
            slot = lax.rem(me_g - owner + n_grp, n_grp)
            where = slot * row_blocks + lax.rem(col, row_blocks)
            total = total + f32_dot(local_ref[b, k], near[where])
        acc[b] = total

    for copy in far_copies:
        copy.wait_recv()
    grads_own = jnp.zeros((features, features), jnp.float32)
    grads_agg = jnp.zeros((features, features), jnp.float32)
    for b in range(row_blocks):
        total = acc[b]
        for k in range(cut_slots):
            slot = lax.rem(n_dom - src_ref[b, k], n_dom)
            total = total + f32_dot(cut_ref[b, k], far[slot])
        agg = total.astype(jnp.bfloat16)
        own = feats_ref[b]
        preact = pre[b] + f32_dot(agg, w_neigh_ref[...])
        sig = jax.nn.sigmoid(preact)
        out_ref[b] = (preact * sig).astype(jnp.bfloat16)
        grad_pre = (
            cot_ref[b].astype(jnp.float32) * sig * (1.0 + preact * (1.0 - sig))
        ).astype(jnp.bfloat16)
        dims = (((0,), (0,)), ((), ()))
        grads_own = grads_own + lax.dot_general(
            own, grad_pre, dims, preferred_element_type=jnp.float32
        )
        grads_agg = grads_agg + lax.dot_general(
            agg, grad_pre, dims, preferred_element_type=jnp.float32
        )

    peers = {"grp": grp_peer, "dom": dom_peer}
    here = {"grp": me_g, "dom": me_d}
    count = {"grp": n_grp, "dom": n_dom}

    def rows_at(start, size):
        return pl.ds(pl.multiple_of(start, size), size)

    def to_peers(axis, src, dst, send, recv):
        return begin(
            [
                remote(src(o), dst(o), send.at[o], recv.at[o], o, axis)
                for o in range(1, count[axis])
            ]
        )

    flows = []
    for h, (one, two) in enumerate(ORDERS):
        rows = 2 * features // count[one]
        piece = piece_rows(rows, count[two])
        split = piece < rows
        flows.append(
            dict(
                one=one,
                two=two,
                rows=rows,
                piece=piece,
                split=split,
                columns=pl.ds(h * width, width),
                mine=rows_at(here[one] * rows, rows),
                inner=rows_at(here[two] * piece, piece) if split else pl.ds(0, rows),
                spot=rows_at(here[one] * rows + (here[two] * piece if split else 0), piece),
                sums1=sums1[h],
                mid=mid[h],
                mid_low=mid_low[h],
                sums2=sums2[h],
            )
        )

    first = []
    for h, f in enumerate(flows):
        cut = slice(h * width, (h + 1) * width)
        part[h, 0:features] = grads_own[:, cut]
        part[h, features : 2 * features] = grads_agg[:, cut]
        part_low[h, 0:features] = grads_own[:, cut].astype(jnp.bfloat16)
        part_low[h, features : 2 * features] = grads_agg[:, cut].astype(jnp.bfloat16)
        first.append(
            to_peers(
                f["one"],
                lambda o: part_low.at[h, rows_at(peers[f["one"]][o] * f["rows"], f["rows"])],
                lambda o: f["sums1"].at[o],
                s1_send.at[h],
                s1_recv.at[h],
            )
        )
    second = []
    for h, f in enumerate(flows):
        total = part[h, f["mine"]]
        for o, copy in enumerate(first[h], 1):
            copy.wait_recv()
            total = total + f["sums1"][o].astype(jnp.float32)
        f["mid"][...] = total
        f["mid_low"][...] = total.astype(jnp.bfloat16)
        second.append(
            to_peers(
                f["two"],
                lambda o: f["mid_low"].at[rows_at(peers[f["two"]][o] * f["piece"], f["piece"])]
                if f["split"]
                else f["mid_low"],
                lambda o: f["sums2"].at[o if f["split"] else here[f["two"]]],
                s2_send.at[h],
                s2_recv.at[h],
            )
        )
    third, fourth = [], []

    def gather(h, f):
        rows_of = grad_ref.at[f["mine"], f["columns"]]
        return to_peers(
            f["one"], lambda o: rows_of, lambda o: rows_of, s4_send.at[h], s4_recv.at[h]
        )

    for h, f in enumerate(flows):
        if f["split"]:
            total = f["mid"][f["inner"]]
            for o, copy in enumerate(second[h], 1):
                copy.wait_recv()
                total = total + f["sums2"][o].astype(jnp.float32)
        else:
            f["sums2"][here[f["two"]]] = f["mid_low"][...]
            for copy in second[h]:
                copy.wait_recv()
            total = f["sums2"][0].astype(jnp.float32)
            for o in range(1, count[f["two"]]):
                total = total + f["sums2"][o].astype(jnp.float32)
        grad_ref[f["spot"], f["columns"]] = total.astype(jnp.bfloat16)
        if f["split"]:
            block_of = grad_ref.at[f["spot"], f["columns"]]
            third.append(
                to_peers(
                    f["two"],
                    lambda o: block_of,
                    lambda o: block_of,
                    s3_send.at[h],
                    s3_recv.at[h],
                )
            )
        else:
            third.append([])
            fourth += gather(h, f)
    for h, f in enumerate(flows):
        if f["split"]:
            for copy in third[h]:
                copy.wait_recv()
            fourth += gather(h, f)
    for copy in fourth:
        copy.wait_recv()

    sent = [far_copies, near_copies, *first, *second, *third, fourth]
    for copy in [copy for group in sent for copy in group]:
        copy.wait_send()


def kernel_near(
    n_dom,
    n_grp,
    cols_hbm,
    src_hbm,
    block_hbm,
    live_hbm,
    feats_hbm,
    w_self_hbm,
    w_neigh_hbm,
    local_hbm,
    cut_hbm,
    cot_hbm,
    out_ref,
    cols_ref,
    src_ref,
    block_ref,
    live_ref,
    w_self_ref,
    w_neigh_ref,
    local_ref,
    cut_ref,
    cot_ref,
    lhs,
    pre,
    grad_pre_ref,
    near,
    outgoing,
    far,
    raw_side,
    raw_mid_a,
    raw_mid_b,
    plan_side,
    plan_mid,
    core_out,
    core_in,
    mine,
    mine_low,
    pieces,
    load_sem,
    near_send,
    near_recv,
    out_send,
    far_recv,
    raw_send,
    side_recv,
    mid_recv,
    core_send,
    core_recv,
    rs_send,
    rs_recv,
    ag_send,
    ag_recv,
    fw_send,
    fw_recv,
    peer_here,
    side_ready,
    mid_ready,
    line_ready,
    grp_ready,
):
    row_blocks, local_slots, block, _ = local_ref.shape
    cut_slots = cut_ref.shape[1]
    features = w_self_ref.shape[0]
    rows = row_blocks * block
    n_z = n_dom // CORES
    parts, _, piece, _ = pieces.shape
    me_d, me_g = lax.axis_index("dom"), lax.axis_index("grp")
    me_z, me_c = lax.div(me_d, CORES), lax.rem(me_d, CORES)
    grp_peer = [lax.rem(me_g + o, n_grp) for o in range(n_grp)]
    place = jnp.where(me_z < n_z // 2, me_z, n_z - 1 - me_z)
    at_end, in_middle = place == 0, place == 1

    def z_of(t):
        return jnp.where(me_z < n_z // 2, t, n_z - 1 - t)

    def dev(t, core):
        return z_of(t) * CORES + core

    side = z_of(1 - place)
    core_peer = me_d + 1 - 2 * me_c
    raw_mids = (raw_mid_a, raw_mid_b)
    halves = [pl.ds(h * (block // 2), block // 2) for h in range(2)]

    def flat(x):
        return x.reshape(rows, features)

    def remote(src, dst, send, recv, device):
        return pltpu.make_async_remote_copy(
            src_ref=src,
            dst_ref=dst,
            send_sem=send,
            recv_sem=recv,
            device_id=device,
            device_id_type=MESH,
        )

    def begin(copies):
        for copy in copies:
            copy.start()
        return copies

    def signal(sem, dom, grp):
        pl.semaphore_signal(sem, inc=1, device_id=(dom, grp), device_id_type=MESH)

    barrier = pltpu.get_barrier_semaphore()
    signal(barrier, core_peer, me_g)

    @pl.when(in_middle)
    def _():
        signal(barrier, dev(2, me_c), me_g)
        for core in range(CORES):
            signal(barrier, dev(0, core), me_g)

    for g in range(1, n_grp):

        @pl.when(me_g < g)
        def _():
            signal(barrier, me_d, g)

    loads = begin(
        [
            pltpu.make_async_copy(src, dst, load_sem.at[i])
            for i, (src, dst) in enumerate(
                (
                    (block_hbm, block_ref),
                    (live_hbm, live_ref),
                    (feats_hbm, lhs.at[0]),
                    (feats_hbm, near.at[pl.ds(me_g * row_blocks, row_blocks)]),
                    (cols_hbm, cols_ref),
                    (src_hbm, src_ref),
                    (w_self_hbm, w_self_ref),
                    (local_hbm, local_ref),
                    (cut_hbm, cut_ref),
                    (w_neigh_hbm, w_neigh_ref),
                    (cot_hbm, cot_ref),
                )
            )
        ]
    )

    def plan_copies(target, plan, send, recv):
        device = (target, me_g)
        return [
            remote(block_hbm, plan.at[0], send.at[0], recv.at[0], device),
            remote(live_hbm, plan.at[1], send.at[1], recv.at[1], device),
        ]

    side_d = side * CORES + me_c
    side_copies = plan_copies(side_d, plan_side, raw_send.at[0], side_recv)
    side_copies.append(
        remote(feats_hbm, raw_side, raw_send.at[0, 2], side_recv.at[2], (side_d, me_g))
    )
    mid_copies = plan_copies(dev(2, me_c), plan_mid, raw_send.at[1], mid_recv)
    mid_copies += [
        remote(
            feats_hbm.at[:, part],
            raw_mids[h],
            raw_send.at[1, 2 + h],
            mid_recv.at[2 + h],
            (dev(2, me_c), me_g),
        )
        for h, part in enumerate(halves)
    ]
    pl.semaphore_wait(barrier, CORES + 1 - place + me_g)

    @pl.when(in_middle)
    def _():
        begin(mid_copies)

    @pl.when(at_end)
    def _():
        for core in range(CORES):
            signal(side_ready, dev(1, core), me_g)
        begin(side_copies)

    for g in range(n_grp - 1):

        @pl.when(me_g > g)
        def _():
            signal(peer_here, me_d, g)

    @pl.when(in_middle)
    def _():
        pl.semaphore_wait(side_ready, CORES)
        begin(side_copies)
        signal(mid_ready, dev(2, me_c), me_g)
        pl.semaphore_wait(mid_ready, 1)
        for core in range(CORES):
            signal(line_ready, dev(0, core), me_g)

    def chosen(blocks_of, block_at, alive):
        picked = blocks_of(block_at).astype(jnp.float32)
        return (picked * alive.astype(jnp.float32)).astype(jnp.bfloat16)

    def of_own(target):
        return chosen(lambda i: lhs[0, i], block_ref[0, target], live_ref[0, target])

    def of_side(target):
        return chosen(lambda i: raw_side[i], plan_side[0, 0, target], plan_side[1, 0, target])

    def of_mid(target, part):
        return chosen(
            lambda i: raw_mids[part][i], plan_mid[0, 0, target], plan_mid[1, 0, target]
        )

    def send_block(i, source, target):
        return remote(
            outgoing.at[i],
            far.at[source],
            out_send.at[i, 0],
            far_recv.at[source, 0],
            (target, me_g),
        )

    def send_half(i, source, target, h):
        return remote(
            outgoing.at[i, halves[h]],
            far.at[source, halves[h]],
            out_send.at[i, h],
            far_recv.at[source, h],
            (target, me_g),
        )

    for load in loads[:4]:
        load.wait()
    end_jobs = [(dev(t, core)) for t in (3, 2) for core in range(CORES)]

    @pl.when(at_end)
    def _():
        for i, target in enumerate(end_jobs):
            outgoing[2 + i] = of_own(target)

    @pl.when(me_g < n_grp - 1)
    def _():
        pl.semaphore_wait(peer_here, n_grp - 1 - me_g)

    near_copies = begin(
        [
            remote(
                feats_hbm,
                near.at[pl.ds(me_g * row_blocks, row_blocks)],
                near_send.at[o],
                near_recv.at[o],
                (me_d, grp_peer[o]),
            )
            for o in range(1, n_grp)
        ]
    )

    @pl.when(at_end)
    def _():
        pl.semaphore_wait(line_ready, CORES)
        for i, target in enumerate(end_jobs):
            send_block(2 + i, me_d, target).start()

    for o in range(1, n_grp):
        signal(grp_ready, me_d, grp_peer[o])
    outgoing[0] = of_own(core_peer)
    send_block(0, me_d, core_peer).start()
    far[me_d] = of_own(me_d)

    for load in loads[4:]:
        load.wait()
    pre[...] = f32_dot(flat(lhs[0]), w_self_ref[...])

    mid_d = dev(2, me_c)
    mid_jobs = [dev(0, 0), dev(0, 1), core_peer]

    @pl.when(in_middle)
    def _():
        for copy in mid_copies[:2]:
            copy.wait_recv()
        for h, part in enumerate(halves):
            mid_copies[2 + h].wait_recv()
            for i, target in enumerate(mid_jobs):
                outgoing[2 + i, part] = of_mid(target, h)
                send_half(2 + i, mid_d, target, h).start()
            far[mid_d, part] = of_mid(me_d, h)

    for copy in side_copies:
        copy.wait_recv()
    outgoing[1] = of_side(core_peer)
    send_block(1, side_d, core_peer).start()
    far[side_d] = of_side(me_d)

    for copy in near_copies:
        copy.wait_recv()
    acc = []
    for b in range(row_blocks):
        total = jnp.zeros((block, features), jnp.float32)
        for k in range(local_slots):
            total = total + f32_dot(local_ref[b, k], near[cols_ref[b, k]])
        acc.append(total)

    def arrived(source):
        send_block(0, source, core_peer).wait_recv()

    def arrived_halves(source):
        for h in range(2):
            send_half(0, source, core_peer, h).wait_recv()

    arrived(core_peer)
    arrived(side * CORES + 1 - me_c)

    @pl.when(in_middle)
    def _():
        arrived_halves(dev(2, 1 - me_c))
        for core in range(CORES):
            arrived(dev(3, core))

    @pl.when(at_end)
    def _():
        for core in range(CORES):
            arrived_halves(dev(2, core))
            arrived(dev(3, core))

    for b in range(row_blocks):
        tiles = jnp.concatenate([cut_ref[b, k] for k in range(cut_slots)], axis=1)
        blocks = [far[lax.rem(me_d + src_ref[b, k], n_dom)] for k in range(cut_slots)]
        total = acc[b] + f32_dot(tiles, jnp.concatenate(blocks, axis=0))
        lhs[1, b] = total.astype(jnp.bfloat16)
    preact = pre[...] + f32_dot(flat(lhs[1]), w_neigh_ref[...])
    sig = jax.nn.sigmoid(preact)
    grad_pre_ref[...] = (
        cot_ref[...].astype(jnp.float32) * sig * (1.0 + preact * (1.0 - sig))
    ).astype(jnp.bfloat16)
    out_ref[pl.ds(0, rows)] = (preact * sig).astype(jnp.bfloat16)

    wave = n_grp * piece
    plane = parts * wave

    def half_of(t):
        return pl.ds(pl.multiple_of((z_of(t) - 1) * plane, plane), plane)

    def product(which, part):
        return lax.dot_general(
            lhs[which, :, :, part].reshape(rows, plane),
            grad_pre_ref[...],
            (((0,), (0,)), ((), ())),
            preferred_element_type=jnp.float32,
        )

    core_copies = {}
    for t in (2, 1):
        part = half_of(t)
        core_out[part] = product(1 - me_c, part).astype(jnp.bfloat16)
        core_copies[t] = remote(
            core_out.at[part],
            core_in.at[part],
            core_send.at[t - 1],
            core_recv.at[z_of(t) - 1],
            (core_peer, me_g),
        )
        core_copies[t].start()
    for t in (2, 1):
        mine[half_of(t)] = product(me_c, half_of(t))
    pl.semaphore_wait(grp_ready, n_grp - 1)

    def owner_rows(t, g, h):
        return pl.multiple_of((z_of(t) - 1) * plane + h * wave + g * piece, piece)

    def give(t, o, h):
        back = (n_grp - o) % n_grp
        slot = n_grp * place + back if t == 2 else 2 * n_grp + (n_grp - 1) * place + back
        g = grp_peer[o]
        return remote(
            mine_low.at[pl.ds(owner_rows(t, g, h), piece)],
            pieces.at[h, slot],
            rs_send,
            rs_recv.at[h],
            (dev(t, me_c), g),
        )

    def share_at(z, g, h):
        start = rows + me_c * features + owner_rows(1, me_g, h)
        own = out_ref.at[pl.ds(pl.multiple_of(start, piece), piece)]
        return remote(own, own, ag_send, ag_recv.at[h, me_z - 1], (z * CORES + me_c, g))

    def share(t, o, h):
        return share_at(z_of(t), grp_peer[o], h)

    def wave_of(q, core, h):
        start = rows + core * features + q * plane + h * wave
        return out_ref.at[pl.ds(pl.multiple_of(start, wave), wave)]

    def forward(q, core, h):
        part = wave_of(q, core, h)
        return remote(part, part, fw_send.at[h, q], fw_recv.at[h, q], (core_peer, me_g))

    def all_of(ref, send, recv):
        return remote(ref, ref, send, recv, (core_peer, me_g))

    for t in (2, 1):
        part = half_of(t)
        core_copies[t].wait_recv()
        total = mine[part] + core_in[part].astype(jnp.float32)
        mine[part] = total
        mine_low[part] = total.astype(jnp.bfloat16)
        for o in OTHERS_FIRST if t == 2 else OTHERS_FIRST[:-1]:
            give(t, o, 0).start()

    @pl.when(at_end)
    def _():
        give(1, 0, 0).start()

    for h in range(1, parts):
        for t in (2, 1):
            for o in OTHERS_FIRST if t == 2 else OTHERS_FIRST[:-1]:
                give(t, o, h).start()

        @pl.when(at_end)
        def _():
            give(1, 0, h).start()

    for copy in [*near_copies, *side_copies, *core_copies.values()]:
        copy.wait_send()
    for i in range(2):
        send_block(i, me_d, core_peer).wait_send()

    @pl.when(in_middle)
    def _():
        for copy in mid_copies:
            copy.wait_send()
        for i, target in enumerate(mid_jobs):
            for h in range(2):
                send_half(2 + i, mid_d, target, h).wait_send()

    @pl.when(at_end)
    def _():
        for i, target in enumerate(end_jobs):
            send_block(2 + i, me_d, target).wait_send()

    others = [(t, o) for t in (3, 2, 0) for o in OTHERS_FIRST]
    others += [(1, o) for o in OTHERS_FIRST[:-1]]

    @pl.when(in_middle)
    def _():
        for h in range(parts):
            all_of(pieces.at[h], rs_send, rs_recv.at[h]).wait_recv()
            own_rows = owner_rows(1, me_g, h)
            total = mine[pl.ds(own_rows, piece)]
            for i in range(len(others)):
                total = total + pieces[h, i].astype(jnp.float32)
            start = pl.multiple_of(rows + me_c * features + own_rows, piece)
            out_ref[pl.ds(start, piece)] = total.astype(jnp.bfloat16)
            for g in range(n_grp):
                share_at(0, g, h).start()
            for o in OTHERS_FIRST:
                share_at(n_z - 1, grp_peer[o], h).start()
            for o in OTHERS_FIRST:
                share(2, o, h).start()
            for o in OTHERS_FIRST[:-1]:
                share(1, o, h).start()
        for h in range(parts):
            most = out_ref.at[pl.ds(rows + me_c * features, wave - piece)]
            all_of(most, ag_send, ag_recv.at[h, me_z - 1]).wait_recv()
            forward(me_z - 1, me_c, h).start()
            q = z_of(2) - 1
            all_of(wave_of(q, me_c, h), ag_send, ag_recv.at[h, q]).wait_recv()
            forward(q, me_c, h).start()
        all_of(mine_low.at[pl.ds(0, features - parts * piece)], rs_send, rs_recv.at[0]).wait_send()
        all_of(
            out_ref.at[pl.ds(0, len(others) * parts * piece)], ag_send, rs_recv.at[0]
        ).wait_send()

    @pl.when(at_end)
    def _():
        for h in range(parts):
            for t in (1, 2):
                q = z_of(t) - 1
                all_of(wave_of(q, me_c, h), ag_send, ag_recv.at[h, q]).wait_recv()
                forward(q, me_c, h).start()
        all_of(mine_low, rs_send, rs_recv.at[0]).wait_send()

    for h in range(parts):
        for q in range(2):
            forward(q, 1 - me_c, h).wait_recv()
    for h in range(parts):
        for q in range(2):
            forward(q, me_c, h).wait_send()


def body_wide(
    feats,
    w_self,
    w_neigh,
    local_tiles,
    local_cols,
    cut_tiles,
    cut_src,
    send_block,
    send_live,
    cotangent,
):
    row_blocks, _, block, _ = local_tiles.shape
    features = feats.shape[1]
    n_dom, n_grp = lax.axis_size("dom"), lax.axis_size("grp")
    blocks = (row_blocks, block, features)
    halves = len(ORDERS)
    count = {"grp": n_grp, "dom": n_dom}
    most = max(n_grp, n_dom)
    sizes = []
    for one, two in ORDERS:
        rows = 2 * features // count[one]
        sizes.append((count[one], rows, count[two], piece_rows(rows, count[two])))
    width = features // halves
    dma = pltpu.SemaphoreType.DMA
    hbm = pl.BlockSpec(memory_space=pltpu.HBM)
    vmem = pl.BlockSpec(memory_space=pltpu.VMEM)
    out, grads = pl.pallas_call(
        functools.partial(kernel_wide, n_dom, n_grp),
        out_shape=(
            jax.ShapeDtypeStruct(blocks, jnp.bfloat16),
            jax.ShapeDtypeStruct((2 * features, features), jnp.bfloat16),
        ),
        in_specs=[hbm] * 10,
        out_specs=(vmem, vmem),
        scratch_shapes=[
            pltpu.SMEM(local_cols.shape, jnp.int32),
            pltpu.SMEM(cut_src.shape, jnp.int32),
            pltpu.SMEM(send_block.shape, jnp.int32),
            pltpu.SMEM(send_live.shape, jnp.int32),
            pltpu.VMEM(w_self.shape, jnp.bfloat16),
            pltpu.VMEM(w_neigh.shape, jnp.bfloat16),
            pltpu.VMEM(local_tiles.shape, jnp.bfloat16),
            pltpu.VMEM(cut_tiles.shape, jnp.bfloat16),
            pltpu.VMEM(blocks, jnp.bfloat16),
            pltpu.VMEM(blocks, jnp.bfloat16),
            pltpu.VMEM((n_grp * row_blocks, block, features), jnp.bfloat16),
            pltpu.VMEM((n_dom, block, features), jnp.bfloat16),
            pltpu.VMEM((n_dom, block, features), jnp.bfloat16),
            pltpu.VMEM(blocks, jnp.float32),
            pltpu.VMEM(blocks, jnp.float32),
            pltpu.VMEM((halves, 2 * features, width), jnp.float32),
            pltpu.VMEM((halves, 2 * features, width), jnp.bfloat16),
        ]
        + [pltpu.VMEM((n, r, width), jnp.bfloat16) for n, r, _, _ in sizes]
        + [pltpu.VMEM((r, width), jnp.float32) for _, r, _, _ in sizes]
        + [pltpu.VMEM((r, width), jnp.bfloat16) for _, r, _, _ in sizes]
        + [pltpu.VMEM((n, p, width), jnp.bfloat16) for _, _, n, p in sizes]
        + [
            dma((11,)),
        ]
        + [dma((n_grp,))] * 2
        + [dma((n_dom,))] * 2
        + [dma((halves, most))] * 8,
        compiler_params=pltpu.CompilerParams(
            collective_id=0, has_side_effects=True, vmem_limit_bytes=32 * 2**20
        ),
    )(
        *(
            pltpu.with_memory_space_constraint(x, pltpu.HBM)
            for x in (
                local_cols,
                cut_src,
                send_block,
                send_live,
                feats.reshape(blocks),
                w_self,
                w_neigh,
                local_tiles,
                cut_tiles,
                cotangent.reshape(blocks),
            )
        )
    )
    summed = grads.astype(jnp.float32)
    return (out.reshape(feats.shape), summed[:features], summed[features:])


def body_near(
    feats,
    w_self,
    w_neigh,
    local_tiles,
    local_cols,
    cut_tiles,
    cut_src,
    send_block,
    send_live,
    cotangent,
):
    row_blocks, _, block, _ = local_tiles.shape
    rows, features = feats.shape
    blocks = (row_blocks, block, features)
    n_dom, n_grp = lax.axis_size("dom"), lax.axis_size("grp")
    chips = n_dom // CORES * n_grp
    piece = 2 * features // (PARTS * chips)
    dma = pltpu.SemaphoreType.DMA
    hbm = pl.BlockSpec(memory_space=pltpu.HBM)
    vmem = pl.BlockSpec(memory_space=pltpu.VMEM)
    low = functools.partial(pltpu.VMEM, dtype=jnp.bfloat16)
    wide = functools.partial(pltpu.VMEM, dtype=jnp.float32)
    res = pl.pallas_call(
        functools.partial(kernel_near, n_dom, n_grp),
        out_shape=jax.ShapeDtypeStruct((rows + 2 * features, features), jnp.bfloat16),
        in_specs=[hbm] * 10,
        out_specs=vmem,
        scratch_shapes=[
            pltpu.SMEM(local_cols.shape, jnp.int32),
            pltpu.SMEM(cut_src.shape, jnp.int32),
            pltpu.SMEM(send_block.shape, jnp.int32),
            pltpu.SMEM(send_live.shape, jnp.int32),
            low(w_self.shape),
            low(w_neigh.shape),
            low(local_tiles.shape),
            low(cut_tiles.shape),
            low(feats.shape),
            low((2, *blocks)),
            wide((rows, features)),
            low((rows, features)),
            low((n_grp * row_blocks, block, features)),
            low((6, block, features)),
            low((n_dom, block, features)),
            low(blocks),
            low((row_blocks, block // 2, features)),
            low((row_blocks, block // 2, features)),
            pltpu.SMEM((2, *send_block.shape), jnp.int32),
            pltpu.SMEM((2, *send_block.shape), jnp.int32),
            low((features, features)),
            low((features, features)),
            wide((features, features)),
            low((features, features)),
            low((PARTS, chips - 1, piece, features)),
            dma((11,)),
            dma((n_grp,)),
            dma((n_grp,)),
            dma((6, 2)),
            dma((n_dom, 2)),
            dma((2, 4)),
            dma((4,)),
            dma((4,)),
            dma((2,)),
            dma((2,)),
        ]
        + [dma, dma((PARTS,)), dma]
        + [dma((PARTS, 2))] * 3
        + [pltpu.SemaphoreType.REGULAR] * 5,
        compiler_params=pltpu.CompilerParams(
            collective_id=0, has_side_effects=True, vmem_limit_bytes=32 * 2**20
        ),
    )(
        *(
            pltpu.with_memory_space_constraint(x, pltpu.HBM)
            for x in (
                local_cols,
                cut_src,
                send_block,
                send_live,
                feats.reshape(blocks),
                w_self,
                w_neigh,
                local_tiles,
                cut_tiles,
                cotangent,
            )
        )
    )
    return (
        res[:rows],
        res[rows : rows + features].astype(jnp.float32),
        res[rows + features :].astype(jnp.float32),
    )


def solution(mesh):
    n_dom, n_grp = mesh.shape["dom"], mesh.shape["grp"]
    chips = n_dom // CORES * n_grp
    return jax.shard_map(
        lambda *args: (
            body_near
            if (n_dom, n_grp) == (LINE * CORES, len(OTHERS_FIRST))
            and 2 * args[1].shape[0] % (PACK * PARTS * chips) == 0
            else body_wide
        )(*args),
        mesh=mesh,
        in_specs=(
            P(("dom", "grp"), None),
            P(),
            P(),
            P(("dom", "grp"), None, None, None),
            P(("dom", "grp"), None),
            P(("dom", "grp"), None, None, None),
            P(("dom", "grp"), None),
            P(("dom", "grp"), None),
            P(("dom", "grp"), None),
            P(("dom", "grp"), None),
        ),
        out_specs=(P(("dom", "grp"), None), P(), P()),
        check_vma=False,
    )
```

```python
import functools

import jax
import jax.numpy as jnp
from jax import lax
from jax.experimental import pallas as pl
from jax.experimental.pallas import tpu as pltpu
from jax.sharding import PartitionSpec as P

MESH = pl.DeviceIdType.MESH
PACK = 16
FEW = 4
CORES = 2
LINE = 4
PARTS = 2
OTHERS_FIRST = (3, 1, 2, 0)
ORDERS = (("grp", "dom"), ("dom", "grp"))


def piece_rows(rows, n):
    return rows // n if n > FEW and rows % (PACK * n) == 0 else rows


def f32_dot(a, b):
    return jnp.dot(a, b, preferred_element_type=jnp.float32)


def kernel_wide(
    n_dom,
    n_grp,
    cols_hbm,
    src_hbm,
    block_hbm,
    live_hbm,
    feats_hbm,
    w_self_hbm,
    w_neigh_hbm,
    local_hbm,
    cut_hbm,
    cot_hbm,
    out_ref,
    grad_ref,
    cols_ref,
    src_ref,
    block_ref,
    live_ref,
    w_self_ref,
    w_neigh_ref,
    local_ref,
    cut_ref,
    cot_ref,
    feats_ref,
    near,
    outgoing,
    far,
    acc,
    pre,
    part,
    part_low,
    sums1_a,
    sums1_b,
    mid_a,
    mid_b,
    low_a,
    low_b,
    sums2_a,
    sums2_b,
    load_sem,
    near_send,
    near_recv,
    far_send,
    far_recv,
    s1_send,
    s1_recv,
    s2_send,
    s2_recv,
    s3_send,
    s3_recv,
    s4_send,
    s4_recv,
):
    sums1, mid, mid_low = (sums1_a, sums1_b), (mid_a, mid_b), (low_a, low_b)
    sums2 = (sums2_a, sums2_b)
    row_blocks, local_slots, block, _ = local_ref.shape
    cut_slots = cut_ref.shape[1]
    features = w_self_ref.shape[0]
    width = part.shape[2]
    me_d, me_g = lax.axis_index("dom"), lax.axis_index("grp")
    dom_peer = [lax.rem(me_d + o, n_dom) for o in range(n_dom)]
    grp_peer = [lax.rem(me_g + o, n_grp) for o in range(n_grp)]

    def remote(src, dst, send, recv, o, axis):
        peer = dom_peer[o] if axis == "dom" else grp_peer[o]
        return pltpu.make_async_remote_copy(
            src_ref=src,
            dst_ref=dst,
            send_sem=send,
            recv_sem=recv,
            device_id={axis: peer},
            device_id_type=MESH,
        )

    def begin(copies):
        for copy in copies:
            copy.start()
        return copies

    barrier = pltpu.get_barrier_semaphore()
    for o in range(1, n_dom):
        pl.semaphore_signal(barrier, inc=1, device_id={"dom": dom_peer[o]}, device_id_type=MESH)
    for o in range(1, n_grp):
        pl.semaphore_signal(barrier, inc=1, device_id={"grp": grp_peer[o]}, device_id_type=MESH)
    loads = begin(
        [
            pltpu.make_async_copy(src, dst, load_sem.at[i])
            for i, (src, dst) in enumerate(
                (
                    (block_hbm, block_ref),
                    (live_hbm, live_ref),
                    (feats_hbm, feats_ref),
                    (feats_hbm, near.at[pl.ds(0, row_blocks)]),
                    (cols_hbm, cols_ref),
                    (src_hbm, src_ref),
                    (w_self_hbm, w_self_ref),
                    (local_hbm, local_ref),
                    (cut_hbm, cut_ref),
                    (w_neigh_hbm, w_neigh_ref),
                    (cot_hbm, cot_ref),
                )
            )
        ]
    )
    for load in loads[:3]:
        load.wait()

    for o in range(n_dom):
        alive = live_ref[0, dom_peer[o]].astype(jnp.float32)
        chosen = feats_ref[block_ref[0, dom_peer[o]]].astype(jnp.float32)
        target = far if o == 0 else outgoing
        target[o] = (chosen * alive).astype(jnp.bfloat16)
    pl.semaphore_wait(barrier, n_dom + n_grp - 2)

    far_copies = begin(
        [
            remote(outgoing.at[o], far.at[o], far_send.at[o], far_recv.at[o], o, "dom")
            for o in sorted(range(1, n_dom), key=lambda o: abs(2 * o - n_dom))
        ]
    )
    near_copies = begin(
        [
            remote(
                feats_ref,
                near.at[pl.ds(o * row_blocks, row_blocks)],
                near_send.at[o],
                near_recv.at[o],
                o,
                "grp",
            )
            for o in range(1, n_grp)
        ]
    )

    for load in loads[3:]:
        load.wait()
    for b in range(row_blocks):
        pre[b] = f32_dot(feats_ref[b], w_self_ref[...])
    for copy in near_copies:
        copy.wait_recv()
    for b in range(row_blocks):
        total = jnp.zeros((block, features), jnp.float32)
        for k in range(local_slots):
            col = cols_ref[b, k]
            owner = lax.div(col, row_blocks)
            slot = lax.rem(me_g - owner + n_grp, n_grp)
            where = slot * row_blocks + lax.rem(col, row_blocks)
            total = total + f32_dot(local_ref[b, k], near[where])
        acc[b] = total

    for copy in far_copies:
        copy.wait_recv()
    grads_own = jnp.zeros((features, features), jnp.float32)
    grads_agg = jnp.zeros((features, features), jnp.float32)
    for b in range(row_blocks):
        total = acc[b]
        for k in range(cut_slots):
            slot = lax.rem(n_dom - src_ref[b, k], n_dom)
            total = total + f32_dot(cut_ref[b, k], far[slot])
        agg = total.astype(jnp.bfloat16)
        own = feats_ref[b]
        preact = pre[b] + f32_dot(agg, w_neigh_ref[...])
        sig = jax.nn.sigmoid(preact)
        out_ref[b] = (preact * sig).astype(jnp.bfloat16)
        grad_pre = (
            cot_ref[b].astype(jnp.float32) * sig * (1.0 + preact * (1.0 - sig))
        ).astype(jnp.bfloat16)
        dims = (((0,), (0,)), ((), ()))
        grads_own = grads_own + lax.dot_general(
            own, grad_pre, dims, preferred_element_type=jnp.float32
        )
        grads_agg = grads_agg + lax.dot_general(
            agg, grad_pre, dims, preferred_element_type=jnp.float32
        )

    peers = {"grp": grp_peer, "dom": dom_peer}
    here = {"grp": me_g, "dom": me_d}
    count = {"grp": n_grp, "dom": n_dom}

    def rows_at(start, size):
        return pl.ds(pl.multiple_of(start, size), size)

    def to_peers(axis, src, dst, send, recv):
        return begin(
            [
                remote(src(o), dst(o), send.at[o], recv.at[o], o, axis)
                for o in range(1, count[axis])
            ]
        )

    flows = []
    for h, (one, two) in enumerate(ORDERS):
        rows = 2 * features // count[one]
        piece = piece_rows(rows, count[two])
        split = piece < rows
        flows.append(
            dict(
                one=one,
                two=two,
                rows=rows,
                piece=piece,
                split=split,
                columns=pl.ds(h * width, width),
                mine=rows_at(here[one] * rows, rows),
                inner=rows_at(here[two] * piece, piece) if split else pl.ds(0, rows),
                spot=rows_at(here[one] * rows + (here[two] * piece if split else 0), piece),
                sums1=sums1[h],
                mid=mid[h],
                mid_low=mid_low[h],
                sums2=sums2[h],
            )
        )

    first = []
    for h, f in enumerate(flows):
        cut = slice(h * width, (h + 1) * width)
        part[h, 0:features] = grads_own[:, cut]
        part[h, features : 2 * features] = grads_agg[:, cut]
        part_low[h, 0:features] = grads_own[:, cut].astype(jnp.bfloat16)
        part_low[h, features : 2 * features] = grads_agg[:, cut].astype(jnp.bfloat16)
        first.append(
            to_peers(
                f["one"],
                lambda o: part_low.at[h, rows_at(peers[f["one"]][o] * f["rows"], f["rows"])],
                lambda o: f["sums1"].at[o],
                s1_send.at[h],
                s1_recv.at[h],
            )
        )
    second = []
    for h, f in enumerate(flows):
        total = part[h, f["mine"]]
        for o, copy in enumerate(first[h], 1):
            copy.wait_recv()
            total = total + f["sums1"][o].astype(jnp.float32)
        f["mid"][...] = total
        f["mid_low"][...] = total.astype(jnp.bfloat16)
        second.append(
            to_peers(
                f["two"],
                lambda o: f["mid_low"].at[rows_at(peers[f["two"]][o] * f["piece"], f["piece"])]
                if f["split"]
                else f["mid_low"],
                lambda o: f["sums2"].at[o if f["split"] else here[f["two"]]],
                s2_send.at[h],
                s2_recv.at[h],
            )
        )
    third, fourth = [], []

    def gather(h, f):
        rows_of = grad_ref.at[f["mine"], f["columns"]]
        return to_peers(
            f["one"], lambda o: rows_of, lambda o: rows_of, s4_send.at[h], s4_recv.at[h]
        )

    for h, f in enumerate(flows):
        if f["split"]:
            total = f["mid"][f["inner"]]
            for o, copy in enumerate(second[h], 1):
                copy.wait_recv()
                total = total + f["sums2"][o].astype(jnp.float32)
        else:
            f["sums2"][here[f["two"]]] = f["mid_low"][...]
            for copy in second[h]:
                copy.wait_recv()
            total = f["sums2"][0].astype(jnp.float32)
            for o in range(1, count[f["two"]]):
                total = total + f["sums2"][o].astype(jnp.float32)
        grad_ref[f["spot"], f["columns"]] = total.astype(jnp.bfloat16)
        if f["split"]:
            block_of = grad_ref.at[f["spot"], f["columns"]]
            third.append(
                to_peers(
                    f["two"],
                    lambda o: block_of,
                    lambda o: block_of,
                    s3_send.at[h],
                    s3_recv.at[h],
                )
            )
        else:
            third.append([])
            fourth += gather(h, f)
    for h, f in enumerate(flows):
        if f["split"]:
            for copy in third[h]:
                copy.wait_recv()
            fourth += gather(h, f)
    for copy in fourth:
        copy.wait_recv()

    sent = [far_copies, near_copies, *first, *second, *third, fourth]
    for copy in [copy for group in sent for copy in group]:
        copy.wait_send()


def kernel_near(
    n_dom,
    n_grp,
    cols_hbm,
    src_hbm,
    block_hbm,
    live_hbm,
    feats_hbm,
    w_self_hbm,
    w_neigh_hbm,
    local_hbm,
    cut_hbm,
    cot_hbm,
    out_ref,
    cols_ref,
    src_ref,
    block_ref,
    live_ref,
    w_self_ref,
    w_neigh_ref,
    local_ref,
    cut_ref,
    cot_ref,
    lhs,
    pre,
    grad_pre_ref,
    near,
    outgoing,
    far,
    raw_side,
    raw_mid_a,
    raw_mid_b,
    plan_side,
    plan_mid,
    core_out,
    core_in,
    mine,
    mine_low,
    pieces,
    load_sem,
    near_send,
    near_recv,
    out_send,
    far_recv,
    raw_send,
    side_recv,
    mid_recv,
    core_send,
    core_recv,
    rs_send,
    rs_recv,
    ag_send,
    ag_recv,
    fw_send,
    fw_recv,
    core_here,
    peer_here,
    side_ready,
    mid_ready,
    pair_ready,
    line_ready,
    grp_ready,
):
    row_blocks, local_slots, block, _ = local_ref.shape
    cut_slots = cut_ref.shape[1]
    features = w_self_ref.shape[0]
    rows = row_blocks * block
    n_z = n_dom // CORES
    parts, _, piece, _ = pieces.shape
    me_d, me_g = lax.axis_index("dom"), lax.axis_index("grp")
    me_z, me_c = lax.div(me_d, CORES), lax.rem(me_d, CORES)
    grp_peer = [lax.rem(me_g + o, n_grp) for o in range(n_grp)]
    place = jnp.where(me_z < n_z // 2, me_z, n_z - 1 - me_z)
    at_end, in_middle = place == 0, place == 1

    def z_of(t):
        return jnp.where(me_z < n_z // 2, t, n_z - 1 - t)

    def dev(t, core):
        return z_of(t) * CORES + core

    side = z_of(1 - place)
    core_peer = me_d + 1 - 2 * me_c
    raw_mids = (raw_mid_a, raw_mid_b)
    halves = [pl.ds(h * (block // 2), block // 2) for h in range(2)]

    def flat(x):
        return x.reshape(rows, features)

    def remote(src, dst, send, recv, device):
        return pltpu.make_async_remote_copy(
            src_ref=src,
            dst_ref=dst,
            send_sem=send,
            recv_sem=recv,
            device_id=device,
            device_id_type=MESH,
        )

    def begin(copies):
        for copy in copies:
            copy.start()
        return copies

    def signal(sem, dom, grp):
        pl.semaphore_signal(sem, inc=1, device_id=(dom, grp), device_id_type=MESH)

    barrier = pltpu.get_barrier_semaphore()
    @pl.when(me_c == 1)
    def _():
        signal(barrier, core_peer, me_g)

    @pl.when(in_middle)
    def _():
        signal(barrier, dev(2, me_c), me_g)
        for core in range(CORES):
            signal(barrier, dev(0, core), me_g)

    for g in range(1, n_grp):

        @pl.when(me_g < g)
        def _():
            signal(barrier, me_d, g)

    loads = begin(
        [
            pltpu.make_async_copy(src, dst, load_sem.at[i])
            for i, (src, dst) in enumerate(
                (
                    (block_hbm, block_ref),
                    (live_hbm, live_ref),
                    (feats_hbm, lhs.at[0]),
                    (feats_hbm, near.at[pl.ds(me_g * row_blocks, row_blocks)]),
                    (cols_hbm, cols_ref),
                    (src_hbm, src_ref),
                    (w_self_hbm, w_self_ref),
                    (local_hbm, local_ref),
                    (cut_hbm, cut_ref),
                    (w_neigh_hbm, w_neigh_ref),
                    (cot_hbm, cot_ref),
                )
            )
        ]
    )

    def plan_copies(target, plan, send, recv):
        device = (target, me_g)
        return [
            remote(block_hbm, plan.at[0], send.at[0], recv.at[0], device),
            remote(live_hbm, plan.at[1], send.at[1], recv.at[1], device),
        ]

    side_d = side * CORES + me_c
    side_copies = plan_copies(side_d, plan_side, raw_send.at[0], side_recv)
    side_copies.append(
        remote(feats_hbm, raw_side, raw_send.at[0, 2], side_recv.at[2], (side_d, me_g))
    )
    mid_copies = plan_copies(dev(2, me_c), plan_mid, raw_send.at[1], mid_recv)
    mid_copies += [
        remote(
            feats_hbm.at[:, part],
            raw_mids[h],
            raw_send.at[1, 2 + h],
            mid_recv.at[2 + h],
            (dev(2, me_c), me_g),
        )
        for h, part in enumerate(halves)
    ]
    pl.semaphore_wait(barrier, CORES + 1 - place + me_g - me_c)

    @pl.when(in_middle)
    def _():
        begin(mid_copies)

    @pl.when(at_end)
    def _():
        for core in range(CORES):
            signal(side_ready, dev(1, core), me_g)
        begin(side_copies)

    @pl.when(me_c == 0)
    def _():
        signal(core_here, core_peer, me_g)

    for g in range(n_grp - 1):

        @pl.when(me_g > g)
        def _():
            signal(peer_here, me_d, g)

    @pl.when(in_middle)
    def _():
        pl.semaphore_wait(side_ready, CORES)
        for core in range(CORES):
            signal(pair_ready, dev(0, core), me_g)
        begin(side_copies)
        signal(mid_ready, dev(2, me_c), me_g)
        pl.semaphore_wait(mid_ready, 1)
        for core in range(CORES):
            signal(line_ready, dev(0, core), me_g)

    def chosen(blocks_of, block_at, alive):
        picked = blocks_of(block_at).astype(jnp.float32)
        return (picked * alive.astype(jnp.float32)).astype(jnp.bfloat16)

    def of_own(target):
        return chosen(lambda i: lhs[0, i], block_ref[0, target], live_ref[0, target])

    def of_side(target):
        return chosen(lambda i: raw_side[i], plan_side[0, 0, target], plan_side[1, 0, target])

    def of_mid(target, part):
        return chosen(
            lambda i: raw_mids[part][i], plan_mid[0, 0, target], plan_mid[1, 0, target]
        )

    def send_block(i, source, target):
        return remote(
            outgoing.at[i],
            far.at[source],
            out_send.at[i, 0],
            far_recv.at[source, 0],
            (target, me_g),
        )

    def send_half(i, source, target, h):
        return remote(
            outgoing.at[i, halves[h]],
            far.at[source, halves[h]],
            out_send.at[i, h],
            far_recv.at[source, h],
            (target, me_g),
        )

    for load in loads[:4]:
        load.wait()
    end_jobs = [(dev(t, core)) for t in (2, 3) for core in range(CORES)]

    @pl.when(at_end)
    def _():
        for i, target in enumerate(end_jobs):
            outgoing[2 + i] = of_own(target)

    @pl.when(me_g < n_grp - 1)
    def _():
        pl.semaphore_wait(peer_here, n_grp - 1 - me_g)

    near_copies = begin(
        [
            remote(
                feats_hbm,
                near.at[pl.ds(me_g * row_blocks, row_blocks)],
                near_send.at[o],
                near_recv.at[o],
                (me_d, grp_peer[o]),
            )
            for o in range(1, n_grp)
        ]
    )

    @pl.when(at_end)
    def _():
        pl.semaphore_wait(pair_ready, CORES)
        for i in range(CORES):
            send_block(2 + i, me_d, end_jobs[i]).start()
        pl.semaphore_wait(line_ready, CORES)
        for i in range(CORES, 2 * CORES):
            send_block(2 + i, me_d, end_jobs[i]).start()

    for o in range(1, n_grp):
        signal(grp_ready, me_d, grp_peer[o])
    outgoing[0] = of_own(core_peer)

    @pl.when(me_c == 1)
    def _():
        pl.semaphore_wait(core_here, 1)

    send_block(0, me_d, core_peer).start()
    far[me_d] = of_own(me_d)

    for load in loads[4:]:
        load.wait()
    pre[...] = f32_dot(flat(lhs[0]), w_self_ref[...])

    mid_d = dev(2, me_c)
    mid_jobs = [dev(0, 0), dev(0, 1), core_peer]

    @pl.when(in_middle)
    def _():
        for copy in mid_copies[:2]:
            copy.wait_recv()
        for h, part in enumerate(halves):
            mid_copies[2 + h].wait_recv()
            for i, target in enumerate(mid_jobs):
                outgoing[2 + i, part] = of_mid(target, h)
                send_half(2 + i, mid_d, target, h).start()
            far[mid_d, part] = of_mid(me_d, h)

    for copy in side_copies:
        copy.wait_recv()
    outgoing[1] = of_side(core_peer)
    send_block(1, side_d, core_peer).start()
    far[side_d] = of_side(me_d)

    for copy in near_copies:
        copy.wait_recv()
    acc = []
    for b in range(row_blocks):
        total = jnp.zeros((block, features), jnp.float32)
        for k in range(local_slots):
            total = total + f32_dot(local_ref[b, k], near[cols_ref[b, k]])
        acc.append(total)

    def arrived(source):
        send_block(0, source, core_peer).wait_recv()

    def arrived_halves(source):
        for h in range(2):
            send_half(0, source, core_peer, h).wait_recv()

    arrived(core_peer)
    arrived(side * CORES + 1 - me_c)

    @pl.when(in_middle)
    def _():
        arrived_halves(dev(2, 1 - me_c))
        for core in range(CORES):
            arrived(dev(3, core))

    @pl.when(at_end)
    def _():
        for core in range(CORES):
            arrived_halves(dev(2, core))
            arrived(dev(3, core))

    for b in range(row_blocks):
        tiles = jnp.concatenate([cut_ref[b, k] for k in range(cut_slots)], axis=1)
        blocks = [far[lax.rem(me_d + src_ref[b, k], n_dom)] for k in range(cut_slots)]
        total = acc[b] + f32_dot(tiles, jnp.concatenate(blocks, axis=0))
        lhs[1, b] = total.astype(jnp.bfloat16)
    preact = pre[...] + f32_dot(flat(lhs[1]), w_neigh_ref[...])
    sig = jax.nn.sigmoid(preact)
    grad_pre_ref[...] = (
        cot_ref[...].astype(jnp.float32) * sig * (1.0 + preact * (1.0 - sig))
    ).astype(jnp.bfloat16)
    out_ref[pl.ds(0, rows)] = (preact * sig).astype(jnp.bfloat16)

    wave = n_grp * piece
    plane = parts * wave

    def half_of(t):
        return pl.ds(pl.multiple_of((z_of(t) - 1) * plane, plane), plane)

    def product(which, part):
        return lax.dot_general(
            lhs[which, :, :, part].reshape(rows, plane),
            grad_pre_ref[...],
            (((0,), (0,)), ((), ())),
            preferred_element_type=jnp.float32,
        )

    core_copies = {}
    for t in (2, 1):
        part = half_of(t)
        core_out[part] = product(1 - me_c, part).astype(jnp.bfloat16)
        core_copies[t] = remote(
            core_out.at[part],
            core_in.at[part],
            core_send.at[t - 1],
            core_recv.at[z_of(t) - 1],
            (core_peer, me_g),
        )
        core_copies[t].start()
    for t in (2, 1):
        mine[half_of(t)] = product(me_c, half_of(t))
    pl.semaphore_wait(grp_ready, n_grp - 1)

    def owner_rows(t, g, h):
        return pl.multiple_of((z_of(t) - 1) * plane + h * wave + g * piece, piece)

    def give(t, o, h):
        back = (n_grp - o) % n_grp
        slot = n_grp * place + back if t == 2 else 2 * n_grp + (n_grp - 1) * place + back
        g = grp_peer[o]
        return remote(
            mine_low.at[pl.ds(owner_rows(t, g, h), piece)],
            pieces.at[h, slot],
            rs_send,
            rs_recv.at[h],
            (dev(t, me_c), g),
        )

    def share_at(z, g, h):
        start = rows + me_c * features + owner_rows(1, me_g, h)
        own = out_ref.at[pl.ds(pl.multiple_of(start, piece), piece)]
        return remote(own, own, ag_send, ag_recv.at[h, me_z - 1], (z * CORES + me_c, g))

    def share(t, o, h):
        return share_at(z_of(t), grp_peer[o], h)

    def wave_of(q, core, h):
        start = rows + core * features + q * plane + h * wave
        return out_ref.at[pl.ds(pl.multiple_of(start, wave), wave)]

    def forward(q, core, h):
        part = wave_of(q, core, h)
        return remote(part, part, fw_send.at[h, q], fw_recv.at[h, q], (core_peer, me_g))

    def all_of(ref, send, recv):
        return remote(ref, ref, send, recv, (core_peer, me_g))

    for t in (2, 1):
        part = half_of(t)
        core_copies[t].wait_recv()
        total = mine[part] + core_in[part].astype(jnp.float32)
        mine[part] = total
        mine_low[part] = total.astype(jnp.bfloat16)
        for o in OTHERS_FIRST if t == 2 else OTHERS_FIRST[:-1]:
            give(t, o, 0).start()

    @pl.when(at_end)
    def _():
        give(1, 0, 0).start()

    for h in range(1, parts):
        for t in (2, 1):
            for o in OTHERS_FIRST if t == 2 else OTHERS_FIRST[:-1]:
                give(t, o, h).start()

        @pl.when(at_end)
        def _():
            give(1, 0, h).start()

    for copy in [*near_copies, *side_copies, *core_copies.values()]:
        copy.wait_send()
    for i in range(2):
        send_block(i, me_d, core_peer).wait_send()

    @pl.when(in_middle)
    def _():
        for copy in mid_copies:
            copy.wait_send()
        for i, target in enumerate(mid_jobs):
            for h in range(2):
                send_half(2 + i, mid_d, target, h).wait_send()

    @pl.when(at_end)
    def _():
        for i, target in enumerate(end_jobs):
            send_block(2 + i, me_d, target).wait_send()

    others = [(t, o) for t in (3, 2, 0) for o in OTHERS_FIRST]
    others += [(1, o) for o in OTHERS_FIRST[:-1]]

    @pl.when(in_middle)
    def _():
        for h in range(parts):
            all_of(pieces.at[h], rs_send, rs_recv.at[h]).wait_recv()
            own_rows = owner_rows(1, me_g, h)
            total = mine[pl.ds(own_rows, piece)]
            for i in range(len(others)):
                total = total + pieces[h, i].astype(jnp.float32)
            start = pl.multiple_of(rows + me_c * features + own_rows, piece)
            out_ref[pl.ds(start, piece)] = total.astype(jnp.bfloat16)
            for g in range(n_grp):
                share_at(0, g, h).start()
            for o in OTHERS_FIRST:
                share_at(n_z - 1, grp_peer[o], h).start()
            for o in OTHERS_FIRST:
                share(2, o, h).start()
            for o in OTHERS_FIRST[:-1]:
                share(1, o, h).start()
        for h in range(parts):
            most = out_ref.at[pl.ds(rows + me_c * features, wave - piece)]
            all_of(most, ag_send, ag_recv.at[h, me_z - 1]).wait_recv()
            forward(me_z - 1, me_c, h).start()
            q = z_of(2) - 1
            all_of(wave_of(q, me_c, h), ag_send, ag_recv.at[h, q]).wait_recv()
            forward(q, me_c, h).start()
        all_of(mine_low.at[pl.ds(0, features - parts * piece)], rs_send, rs_recv.at[0]).wait_send()
        all_of(
            out_ref.at[pl.ds(0, len(others) * parts * piece)], ag_send, rs_recv.at[0]
        ).wait_send()

    @pl.when(at_end)
    def _():
        for h in range(parts):
            for t in (1, 2):
                q = z_of(t) - 1
                all_of(wave_of(q, me_c, h), ag_send, ag_recv.at[h, q]).wait_recv()
                forward(q, me_c, h).start()
        all_of(mine_low, rs_send, rs_recv.at[0]).wait_send()

    for h in range(parts):
        for q in range(2):
            forward(q, 1 - me_c, h).wait_recv()
    for h in range(parts):
        for q in range(2):
            forward(q, me_c, h).wait_send()


def body_wide(
    feats,
    w_self,
    w_neigh,
    local_tiles,
    local_cols,
    cut_tiles,
    cut_src,
    send_block,
    send_live,
    cotangent,
):
    row_blocks, _, block, _ = local_tiles.shape
    features = feats.shape[1]
    n_dom, n_grp = lax.axis_size("dom"), lax.axis_size("grp")
    blocks = (row_blocks, block, features)
    halves = len(ORDERS)
    count = {"grp": n_grp, "dom": n_dom}
    most = max(n_grp, n_dom)
    sizes = []
    for one, two in ORDERS:
        rows = 2 * features // count[one]
        sizes.append((count[one], rows, count[two], piece_rows(rows, count[two])))
    width = features // halves
    dma = pltpu.SemaphoreType.DMA
    hbm = pl.BlockSpec(memory_space=pltpu.HBM)
    vmem = pl.BlockSpec(memory_space=pltpu.VMEM)
    out, grads = pl.pallas_call(
        functools.partial(kernel_wide, n_dom, n_grp),
        out_shape=(
            jax.ShapeDtypeStruct(blocks, jnp.bfloat16),
            jax.ShapeDtypeStruct((2 * features, features), jnp.bfloat16),
        ),
        in_specs=[hbm] * 10,
        out_specs=(vmem, vmem),
        scratch_shapes=[
            pltpu.SMEM(local_cols.shape, jnp.int32),
            pltpu.SMEM(cut_src.shape, jnp.int32),
            pltpu.SMEM(send_block.shape, jnp.int32),
            pltpu.SMEM(send_live.shape, jnp.int32),
            pltpu.VMEM(w_self.shape, jnp.bfloat16),
            pltpu.VMEM(w_neigh.shape, jnp.bfloat16),
            pltpu.VMEM(local_tiles.shape, jnp.bfloat16),
            pltpu.VMEM(cut_tiles.shape, jnp.bfloat16),
            pltpu.VMEM(blocks, jnp.bfloat16),
            pltpu.VMEM(blocks, jnp.bfloat16),
            pltpu.VMEM((n_grp * row_blocks, block, features), jnp.bfloat16),
            pltpu.VMEM((n_dom, block, features), jnp.bfloat16),
            pltpu.VMEM((n_dom, block, features), jnp.bfloat16),
            pltpu.VMEM(blocks, jnp.float32),
            pltpu.VMEM(blocks, jnp.float32),
            pltpu.VMEM((halves, 2 * features, width), jnp.float32),
            pltpu.VMEM((halves, 2 * features, width), jnp.bfloat16),
        ]
        + [pltpu.VMEM((n, r, width), jnp.bfloat16) for n, r, _, _ in sizes]
        + [pltpu.VMEM((r, width), jnp.float32) for _, r, _, _ in sizes]
        + [pltpu.VMEM((r, width), jnp.bfloat16) for _, r, _, _ in sizes]
        + [pltpu.VMEM((n, p, width), jnp.bfloat16) for _, _, n, p in sizes]
        + [
            dma((11,)),
        ]
        + [dma((n_grp,))] * 2
        + [dma((n_dom,))] * 2
        + [dma((halves, most))] * 8,
        compiler_params=pltpu.CompilerParams(
            collective_id=0, has_side_effects=True, vmem_limit_bytes=32 * 2**20
        ),
    )(
        *(
            pltpu.with_memory_space_constraint(x, pltpu.HBM)
            for x in (
                local_cols,
                cut_src,
                send_block,
                send_live,
                feats.reshape(blocks),
                w_self,
                w_neigh,
                local_tiles,
                cut_tiles,
                cotangent.reshape(blocks),
            )
        )
    )
    summed = grads.astype(jnp.float32)
    return (out.reshape(feats.shape), summed[:features], summed[features:])


def body_near(
    feats,
    w_self,
    w_neigh,
    local_tiles,
    local_cols,
    cut_tiles,
    cut_src,
    send_block,
    send_live,
    cotangent,
):
    row_blocks, _, block, _ = local_tiles.shape
    rows, features = feats.shape
    blocks = (row_blocks, block, features)
    n_dom, n_grp = lax.axis_size("dom"), lax.axis_size("grp")
    chips = n_dom // CORES * n_grp
    piece = 2 * features // (PARTS * chips)
    dma = pltpu.SemaphoreType.DMA
    hbm = pl.BlockSpec(memory_space=pltpu.HBM)
    vmem = pl.BlockSpec(memory_space=pltpu.VMEM)
    low = functools.partial(pltpu.VMEM, dtype=jnp.bfloat16)
    wide = functools.partial(pltpu.VMEM, dtype=jnp.float32)
    res = pl.pallas_call(
        functools.partial(kernel_near, n_dom, n_grp),
        out_shape=jax.ShapeDtypeStruct((rows + 2 * features, features), jnp.bfloat16),
        in_specs=[hbm] * 10,
        out_specs=vmem,
        scratch_shapes=[
            pltpu.SMEM(local_cols.shape, jnp.int32),
            pltpu.SMEM(cut_src.shape, jnp.int32),
            pltpu.SMEM(send_block.shape, jnp.int32),
            pltpu.SMEM(send_live.shape, jnp.int32),
            low(w_self.shape),
            low(w_neigh.shape),
            low(local_tiles.shape),
            low(cut_tiles.shape),
            low(feats.shape),
            low((2, *blocks)),
            wide((rows, features)),
            low((rows, features)),
            low((n_grp * row_blocks, block, features)),
            low((6, block, features)),
            low((n_dom, block, features)),
            low(blocks),
            low((row_blocks, block // 2, features)),
            low((row_blocks, block // 2, features)),
            pltpu.SMEM((2, *send_block.shape), jnp.int32),
            pltpu.SMEM((2, *send_block.shape), jnp.int32),
            low((features, features)),
            low((features, features)),
            wide((features, features)),
            low((features, features)),
            low((PARTS, chips - 1, piece, features)),
            dma((11,)),
            dma((n_grp,)),
            dma((n_grp,)),
            dma((6, 2)),
            dma((n_dom, 2)),
            dma((2, 4)),
            dma((4,)),
            dma((4,)),
            dma((2,)),
            dma((2,)),
        ]
        + [dma, dma((PARTS,)), dma]
        + [dma((PARTS, 2))] * 3
        + [pltpu.SemaphoreType.REGULAR] * 7,
        compiler_params=pltpu.CompilerParams(
            collective_id=0, has_side_effects=True, vmem_limit_bytes=32 * 2**20
        ),
    )(
        *(
            pltpu.with_memory_space_constraint(x, pltpu.HBM)
            for x in (
                local_cols,
                cut_src,
                send_block,
                send_live,
                feats.reshape(blocks),
                w_self,
                w_neigh,
                local_tiles,
                cut_tiles,
                cotangent,
            )
        )
    )
    return (
        res[:rows],
        res[rows : rows + features].astype(jnp.float32),
        res[rows + features :].astype(jnp.float32),
    )


def solution(mesh):
    n_dom, n_grp = mesh.shape["dom"], mesh.shape["grp"]
    chips = n_dom // CORES * n_grp
    return jax.shard_map(
        lambda *args: (
            body_near
            if (n_dom, n_grp) == (LINE * CORES, len(OTHERS_FIRST))
            and 2 * args[1].shape[0] % (PACK * PARTS * chips) == 0
            else body_wide
        )(*args),
        mesh=mesh,
        in_specs=(
            P(("dom", "grp"), None),
            P(),
            P(),
            P(("dom", "grp"), None, None, None),
            P(("dom", "grp"), None),
            P(("dom", "grp"), None, None, None),
            P(("dom", "grp"), None),
            P(("dom", "grp"), None),
            P(("dom", "grp"), None),
            P(("dom", "grp"), None),
        ),
        out_specs=(P(("dom", "grp"), None), P(), P()),
        check_vma=False,
    )
```
